32 devices in a mesh: seq: 16 (over z, y, x), batch: 2 (over core).
Axes of the slice: x: 2, y: 2, z: 4, core: 2. Of those that a mesh axis runs over, the one named last changes fastest.
Arguments:
- inputs: bfloat16 [16, 2048, 1024], P('batch', 'seq'), may hold values from -6 to 6
- segments: int32 [16, 2048], P('batch', 'seq'), may hold values from 0 to 2, as said below
- groups: int32 [16, 2048], P('batch', 'seq'), may hold values from 0 to 7
- group_loss_weight: float32 [8], replicated, may hold values from 0.5 to 2
- attention_norm_gain: bfloat16 [1024], replicated, may hold values from 0.5 to 1.5
- attention_norm_bias: bfloat16 [1024], replicated, may hold values from -1.75 to 1.75
- query_key_value_weight: bfloat16 [1024, 3072], replicated, may hold values from -0.1875 to 0.1875
- query_value_bias: bfloat16 [2, 1024], replicated, may hold values from -1.75 to 1.75
- attention_out_weight: bfloat16 [1024, 1024], replicated, may hold values from -0.75 to 0.75
- attention_out_bias: bfloat16 [1024], replicated, may hold values from -1.75 to 1.75
- feedforward_norm_gain: bfloat16 [1024], replicated, may hold values from 0.099609375 to 1.8984375
- feedforward_norm_bias: bfloat16 [1024], replicated, may hold values from -1.75 to 1.75
- expand_weight: bfloat16 [1024, 4096], replicated, may hold values from -0.1875 to 0.1875
- expand_bias: bfloat16 [4096], replicated, may hold values from -1.75 to 1.75
- contract_weight: bfloat16 [4096, 1024], replicated, may hold values from -0.09375 to 0.09375
- contract_bias: bfloat16 [1024], replicated, may hold values from -1.75 to 1.75
- adapter_down_maps: float32 [2, 1024, 4], replicated, may hold values from -0.1875 to 0.1875
- adapter_up_maps: float32 [2, 4, 1024], replicated, may hold values from -0.375 to 0.375
- down_velocity: float32 [2, 1024, 4], replicated, may hold values from -6144 to 6144
- up_velocity: float32 [2, 4, 1024], replicated, may hold values from -3072 to 3072
- running_down_mean: float32 [2, 1024, 4], replicated, may hold values from -0.1875 to 0.1875
- running_up_mean: float32 [2, 4, 1024], replicated, may hold values from -0.375 to 0.375
- cotangent: bfloat16 [16, 2048, 1024], P('batch', 'seq'), may hold values from -6 to 6
Outputs:
- layer_output: bfloat16 [16, 2048, 1024], P('batch', 'seq')
- input_grad: bfloat16 [16, 2048, 1024], P('batch', 'seq')
- lora_a_grad: float32 [2, 1024, 4], replicated
- lora_b_grad: float32 [2, 4, 1024], replicated
- adapter_down_updated: float32 [2, 1024, 4], replicated
- adapter_up_updated: float32 [2, 4, 1024], replicated
- down_velocity_next: float32 [2, 1024, 4], replicated
- up_velocity_next: float32 [2, 4, 1024], replicated
- updated_down_mean: float32 [2, 1024, 4], replicated
- updated_up_mean: float32 [2, 4, 1024], replicated
- lora_a_copy: bfloat16 [2, 1024, 4], replicated
- lora_b_copy: bfloat16 [2, 4, 1024], replicated
The draws below stay inside these ranges and needn't reach their ends.
Inputs may be any that keep to these rules, and one draw needn't show every extreme that they name: `segments`: in each row the segment numbers start at 0, never fall and rise by one from one example to the next; every example has 1 to 1024 tokens, the second example of each row has exactly 1024 tokens, and every row holds the same number of examples.
All inputs are finite; a program needn't handle non-finite values.
Results may differ from the reference program's by a relative error of at most 0.019.
Values may be sent and summed in bfloat16 or wider, within the bound.
No kernel may reach another device: no remote copies, remote signals or barrier semaphores. Data moves between devices by JAX's collectives and lax.ppermute only.
A program may use at most 576 MiB of HBM per device.

```python
import math
import jax
import jax.numpy as jnp
from jax import lax

MODEL_DIMENSION = 1024
FF = 4096
HEADS = 16
ADAPTER_RANK = 4
GROUPS = 8
EXAMPLE_MAX = 1024
TOK_DEV = 128
SEQ_LEN = 2048
ROWS = 16


def draw_segments(key, part):
    first_key, rest_key = jax.random.split(key)
    spacing = EXAMPLE_MAX // 2
    later = (SEQ_LEN - 2 * EXAMPLE_MAX + spacing - 2) // spacing + 1
    leading = jax.random.randint(first_key, (ROWS, 1), 1, min(TOK_DEV, EXAMPLE_MAX // 4)).astype(jnp.int32)
    jitter = jax.random.randint(rest_key, (ROWS, later), 0, spacing // 2).astype(jnp.int32)
    column = jnp.arange(later, dtype=jnp.int32)
    jitter = jnp.where(column[None, :] == 0, 0, jitter).astype(jnp.int32)
    marks = leading + EXAMPLE_MAX + column[None, :] * spacing + jitter
    bounds = jnp.concatenate([leading, marks.astype(jnp.int32)], axis=1)
    places = jnp.arange(SEQ_LEN, dtype=jnp.int32)
    passed = (places[None, :, None] >= bounds[:, None, :]).astype(jnp.int32)
    return jnp.sum(passed, axis=2).astype(jnp.int32)


def plant(array, own_key, least, largest):
    extent = array.shape
    place = [jax.random.randint(jax.random.fold_in(own_key, axis), (), 0, extent[axis]) for axis in range(len(extent))]
    array = array.at[tuple(place)].set(least)
    longest = extent.index(max(extent))
    place[longest] = (place[longest] + 1) % extent[longest]
    return array.at[tuple(place)].set(largest)


def block_levels(stream_key, dims, cuts, least, largest):
    def one(dim, blocks):
        heights = jax.random.uniform(jax.random.fold_in(jax.random.fold_in(stream_key, 6), dim), (blocks,), jnp.float32, least / len(cuts), largest / len(cuts))
        return jnp.repeat(jnp.exp(heights), dims[dim] // blocks).reshape((-1,) + (1,) * (len(dims) - dim - 1))

    level = one(*cuts[0])
    for cut in cuts[1:]:
        level = level * one(*cut)
    return level


def gaussian(stream_key, extent, spread, limit, pieces=(), held_as=jnp.bfloat16):
    array = spread * jax.random.normal(stream_key, extent, jnp.float32)
    if pieces:
        array = array * block_levels(stream_key, extent, pieces, -0.22, 0.18)
    return jnp.clip(array, -limit, limit).astype(held_as)


def setup_inputs(seed: int = 0) -> dict:
    keys = jax.random.split(jax.random.key(seed), 24)
    inputs = gaussian(keys[0], (ROWS, SEQ_LEN, MODEL_DIMENSION), 1.0, 6.0, ((0, 2), (1, 16)))
    segments = draw_segments(jax.random.fold_in(keys[23], 71), 0)
    groups = plant(jax.random.randint(keys[2], (ROWS, SEQ_LEN), 0, GROUPS), jax.random.fold_in(keys[2], 1), 0, GROUPS - 1).astype(jnp.int32)
    group_loss_weight = jnp.clip(jnp.exp(jax.random.uniform(keys[3], (GROUPS,), jnp.float32, math.log(0.5), math.log(2.0))), 0.5, 2.0)
    attention_norm_gain = jnp.clip(1.0 + 0.1 * jax.random.normal(keys[4], (MODEL_DIMENSION,), jnp.float32), 0.5, 1.5).astype(jnp.bfloat16)
    attention_norm_bias = gaussian(keys[5], (MODEL_DIMENSION,), 0.3, 1.75)
    query_key_value_weight = gaussian(keys[6], (MODEL_DIMENSION, 3 * MODEL_DIMENSION), MODEL_DIMENSION ** -0.5, 0.1875)
    query_value_bias = gaussian(keys[7], (2, MODEL_DIMENSION), 0.3, 1.75)
    attention_out_weight = gaussian(keys[8], (MODEL_DIMENSION, MODEL_DIMENSION), (MODEL_DIMENSION // 16) ** -0.5, 0.75)
    attention_out_bias = gaussian(keys[9], (MODEL_DIMENSION,), 0.3, 1.75)
    feedforward_norm_gain = jnp.clip(1.0 + 0.18 * jax.random.normal(keys[10], (MODEL_DIMENSION,), jnp.float32), 0.099609375, 1.8984375).astype(jnp.bfloat16)
    feedforward_norm_bias = gaussian(keys[11], (MODEL_DIMENSION,), 0.3, 1.75)
    expand_weight = gaussian(keys[12], (MODEL_DIMENSION, FF), MODEL_DIMENSION ** -0.5, 0.1875)
    expand_bias = gaussian(keys[13], (FF,), 0.3, 1.75)
    contract_weight = gaussian(keys[14], (FF, MODEL_DIMENSION), FF ** -0.5, 0.09375)
    contract_bias = gaussian(keys[15], (MODEL_DIMENSION,), 0.3, 1.75)
    adapter_down_maps = gaussian(keys[16], (2, MODEL_DIMENSION, ADAPTER_RANK), MODEL_DIMENSION ** -0.5, 0.1875, (), jnp.float32)
    adapter_up_maps = gaussian(keys[17], (2, ADAPTER_RANK, MODEL_DIMENSION), 0.0625, 0.375, (), jnp.float32)
    down_velocity = gaussian(keys[18], (2, MODEL_DIMENSION, ADAPTER_RANK), (6.0 * (ROWS * SEQ_LEN) ** 0.5), 6144.0, (), jnp.float32)
    up_velocity = gaussian(keys[19], (2, ADAPTER_RANK, MODEL_DIMENSION), (3.0 * (ROWS * SEQ_LEN) ** 0.5), 3072.0, (), jnp.float32)
    running_down_mean = gaussian(keys[20], (2, MODEL_DIMENSION, ADAPTER_RANK), 0.03125, 0.1875, (), jnp.float32)
    running_up_mean = gaussian(keys[21], (2, ADAPTER_RANK, MODEL_DIMENSION), 0.0625, 0.375, (), jnp.float32)
    cotangent = gaussian(keys[22], (ROWS, SEQ_LEN, MODEL_DIMENSION), 1.0, 6.0, ((0, 2), (1, 16)))
    return {"inputs": inputs, "segments": segments, "groups": groups, "group_loss_weight": group_loss_weight, "attention_norm_gain": attention_norm_gain, "attention_norm_bias": attention_norm_bias, "query_key_value_weight": query_key_value_weight, "query_value_bias": query_value_bias, "attention_out_weight": attention_out_weight, "attention_out_bias": attention_out_bias, "feedforward_norm_gain": feedforward_norm_gain, "feedforward_norm_bias": feedforward_norm_bias, "expand_weight": expand_weight, "expand_bias": expand_bias, "contract_weight": contract_weight, "contract_bias": contract_bias, "adapter_down_maps": adapter_down_maps, "adapter_up_maps": adapter_up_maps, "down_velocity": down_velocity, "up_velocity": up_velocity, "running_down_mean": running_down_mean, "running_up_mean": running_up_mean, "cotangent": cotangent}


norm_eps = 1e-05
adapter_scale = 8.0
learning_step_size = 3e-05
velocity_factor = 0.5
mean_decay_factor = 0.5
masked_score = -1e+30
score_scale = 0.125

@jax.custom_vjp
def reduced_rows(v):
    return lax.optimization_barrier(v.astype(jnp.bfloat16)).astype(jnp.float32)

@jax.custom_vjp
def reduced_backward(v):
    return v

def low_keep(v):
    return (reduced_rows(v), None)

def low_pass(kept, grad):
    return (grad,)

def back_keep(v):
    return (v, None)

def back_low(kept, grad):
    return (reduced_rows(grad),)
reduced_rows.defvjp(low_keep, low_pass)
reduced_backward.defvjp(back_keep, back_low)

def norm_layer(values, gain_row, shift_row):
    average = lax.optimization_barrier(jnp.mean(values, axis=-1, keepdims=True))
    centred = values - average
    variance = lax.optimization_barrier(jnp.mean(centred * centred, axis=-1, keepdims=True))
    return centred * lax.rsqrt(variance + norm_eps) * gain_row + shift_row

def attend_block(query_block, query_place, query_seg, key_heads, value_heads, key_seg):
    scores = jnp.einsum('qhe,khe->hqk', query_block, key_heads, precision=lax.Precision.HIGHEST) * score_scale
    scores = reduced_backward(scores)
    key_place = jnp.arange(key_heads.shape[0], dtype=jnp.int32)
    allowed = (key_seg[None, :] == query_seg[:, None]) & (key_place[None, :] <= query_place[:, None])
    scores = jnp.where(allowed[None, :, :], scores, masked_score)
    highest = lax.optimization_barrier(jnp.max(scores, axis=-1, keepdims=True))
    raised = jnp.exp(scores - highest)
    weights = reduced_rows(raised / lax.optimization_barrier(jnp.sum(raised, axis=-1, keepdims=True)))
    return jnp.einsum('hqk,khe->qhe', weights, value_heads, precision=lax.Precision.HIGHEST)

def forward_per_row(input_row, row_segment, frozen_params, adapter_down_weight, adapter_up_weight):
    attention_norm_gain, attention_norm_bias, query_key_value_weight, query_value_bias, attention_out_weight, attention_out_bias, feedforward_norm_gain, feedforward_norm_bias, expand_weight, expand_bias, contract_weight, contract_bias = frozen_params
    seq_length = input_row.shape[0]
    hidden_width = input_row.shape[1]
    head_width = hidden_width // HEADS
    normalized_rows = reduced_rows(norm_layer(input_row, attention_norm_gain, attention_norm_bias))
    projected_rows = jnp.dot(normalized_rows, query_key_value_weight, precision=lax.Precision.HIGHEST)
    adapter_down_apply = reduced_backward(reduced_rows(jnp.einsum('gv,ivp->igp', normalized_rows, reduced_rows(adapter_down_weight), precision=lax.Precision.HIGHEST)))
    adapter_up_apply = jnp.einsum('adx,axw->adw', adapter_down_apply, reduced_rows(adapter_up_weight), precision=lax.Precision.HIGHEST)
    query_matrix = reduced_backward(reduced_rows(projected_rows[:, :hidden_width] + query_value_bias[0] + adapter_scale * adapter_up_apply[0]))
    key_rows = reduced_backward(reduced_rows(projected_rows[:, hidden_width:2 * hidden_width]))
    value_matrix = reduced_backward(reduced_rows(projected_rows[:, 2 * hidden_width:] + query_value_bias[1] + adapter_scale * adapter_up_apply[1]))
    block_rows = math.gcd(seq_length, 512)
    block_count = seq_length // block_rows
    key_heads = key_rows.reshape(seq_length, HEADS, head_width)
    value_heads = value_matrix.reshape(seq_length, HEADS, head_width)
    query_blocks = query_matrix.reshape(block_count, block_rows, HEADS, head_width)
    places = jnp.arange(seq_length, dtype=jnp.int32).reshape(block_count, block_rows)
    seg_blocks = row_segment.reshape(block_count, block_rows)
    checked = jax.checkpoint(attend_block)

    def one_block(member):
        return checked(member[0], member[1], member[2], key_heads, value_heads, row_segment)
    attended = lax.map(one_block, (query_blocks, places, seg_blocks)).reshape(seq_length, hidden_width)
    attended = reduced_backward(reduced_rows(attended))
    attn_out = reduced_backward(jnp.dot(attended, attention_out_weight, precision=lax.Precision.HIGHEST) + attention_out_bias)
    middle = input_row + attn_out
    normed_two = reduced_rows(norm_layer(middle, feedforward_norm_gain, feedforward_norm_bias))
    pre_act = reduced_backward(jnp.dot(normed_two, expand_weight, precision=lax.Precision.HIGHEST) + expand_bias)
    activated = reduced_rows(jax.nn.gelu(pre_act, approximate=True))
    return middle + reduced_backward(jnp.dot(activated, contract_weight, precision=lax.Precision.HIGHEST) + contract_bias)

def reference(inputs, segments, groups, group_loss_weight, attention_norm_gain, attention_norm_bias, query_key_value_weight, query_value_bias, attention_out_weight, attention_out_bias, feedforward_norm_gain, feedforward_norm_bias, expand_weight, expand_bias, contract_weight, contract_bias, adapter_down_maps, adapter_up_maps, down_velocity, up_velocity, running_down_mean, running_up_mean, cotangent):
    frozen_params = tuple((array_in.astype(jnp.float32) for array_in in (attention_norm_gain, attention_norm_bias, query_key_value_weight, query_value_bias, attention_out_weight, attention_out_bias, feedforward_norm_gain, feedforward_norm_bias, expand_weight, expand_bias, contract_weight, contract_bias)))

    def forward_pass(values_in, down_weight, up_weight):

        def scan_row(carry_zero, row_member):
            return (carry_zero, forward_per_row(row_member[0], row_member[1], frozen_params, down_weight, up_weight))
        _, stacked = lax.scan(scan_row, jnp.zeros((), jnp.float32), (values_in, segments))
        return stacked
    layer_result, backward_function = jax.vjp(forward_pass, inputs.astype(jnp.float32), adapter_down_maps, adapter_up_maps)
    token_weight = group_loss_weight[groups]
    grad_out = cotangent.astype(jnp.float32) * token_weight[..., None]
    gradient_incoming, down_map_gradient, up_map_gradient = backward_function(grad_out)
    down_velocity_next = velocity_factor * down_velocity + down_map_gradient
    up_velocity_next = velocity_factor * up_velocity + up_map_gradient
    adapter_down_updated = adapter_down_maps - learning_step_size * (down_map_gradient + velocity_factor * down_velocity_next)
    adapter_up_updated = adapter_up_maps - learning_step_size * (up_map_gradient + velocity_factor * up_velocity_next)
    updated_down_mean = mean_decay_factor * running_down_mean + (1.0 - mean_decay_factor) * adapter_down_updated
    updated_up_mean = mean_decay_factor * running_up_mean + (1.0 - mean_decay_factor) * adapter_up_updated
    return (layer_result.astype(jnp.bfloat16), gradient_incoming.astype(jnp.bfloat16), down_map_gradient, up_map_gradient, adapter_down_updated, adapter_up_updated, down_velocity_next, up_velocity_next, updated_down_mean, updated_up_mean, adapter_down_updated.astype(jnp.bfloat16), adapter_up_updated.astype(jnp.bfloat16))
```

```python
import functools

import jax
import jax.numpy as jnp
from jax import lax
from jax.experimental import pallas as pl
from jax.experimental.pallas import tpu as pltpu
from jax.sharding import PartitionSpec as P

HEADS = 16
EXAMPLE_MAX = 1024
SEGMENT_SLOTS = 8
LANES = 128
QUERY_BLOCK = 256

norm_eps = 1e-05
adapter_scale = 8.0
learning_step_size = 3e-05
velocity_factor = 0.5
mean_decay_factor = 0.5
masked_score = -1e30
score_scale = 0.125


def norm_layer(values, gain_row, shift_row):
    average = jnp.mean(values, axis=-1, keepdims=True)
    centred = values - average
    variance = jnp.mean(centred * centred, axis=-1, keepdims=True)
    return centred * lax.rsqrt(variance + norm_eps) * gain_row + shift_row


def matmul_rows(left_side, right_side):
    return lax.dot_general(
        left_side, right_side, (((1,), (0,)), ((), ())), preferred_element_type=jnp.float32
    )


def matmul_back(left_side, right_side):
    return lax.dot_general(
        left_side, right_side, (((1,), (1,)), ((), ())), preferred_element_type=jnp.float32
    )


def matmul_over(left_side, right_side):
    return lax.dot_general(
        left_side, right_side, (((0,), (0,)), ((), ())), preferred_element_type=jnp.float32
    )


def gelu_tanh(values):
    return jax.nn.gelu(values, approximate=True)


def rows_home(x):
    cores = lax.axis_size("batch")
    rows, tokens, width = x.shape
    stripe = tokens // cores
    y = lax.all_to_all(x.reshape(rows, cores, stripe, width), "batch", 1, 0)
    y = y.reshape(cores * rows, stripe, width)
    y = lax.all_to_all(y, "seq", 0, 0, tiled=True)
    return y.reshape(cores * rows * stripe, width)


def rows_back(y, rows, tokens):
    cores = lax.axis_size("batch")
    stripe = tokens // cores
    width = y.shape[-1]
    y = lax.all_to_all(y.reshape(cores * rows, stripe, width), "seq", 0, 0, tiled=True)
    y = lax.all_to_all(y.reshape(cores, rows, stripe, width), "batch", 0, 1)
    return y.reshape(rows, tokens, width)


def row_codes(codes):
    cores = lax.axis_size("batch")
    rows, tokens = codes.shape
    y = jnp.broadcast_to(codes[None], (cores, rows, tokens))
    y = lax.all_to_all(y, "batch", 0, 0, tiled=True).reshape(cores * rows, tokens)
    return lax.all_to_all(y, "seq", 0, 0, tiled=True)


def from_core(x, by):
    cores = lax.axis_size("batch")
    return lax.ppermute(x, "batch", [(i, (i + by) % cores) for i in range(cores)])


def sum_everywhere(x):
    for axis in ("batch", "seq"):
        size = lax.axis_size(axis)
        step = 1
        while step < size:
            x = x + lax.ppermute(x, axis, [(i, i ^ step) for i in range(size)])
            step *= 2
    return x


def lane_masks(dtype):
    lane = lax.broadcasted_iota(jnp.int32, (1, LANES), 1)
    first = (lane < LANES // 2).astype(jnp.float32).astype(dtype)
    second = (lane >= LANES // 2).astype(jnp.float32).astype(dtype)
    return first, second


def block_of(ref, index):
    return ref[pl.ds(index * QUERY_BLOCK, QUERY_BLOCK), :]


def attend_kernel(cores, reach, *refs):
    query_ref, mark_ref = refs[0], refs[1]
    key_refs = refs[2 : 2 + cores]
    value_refs = refs[2 + cores : 2 + 2 * cores]
    key_mark_refs = refs[2 + 2 * cores : 2 + 3 * cores]
    causal_ref = refs[2 + 3 * cores]
    out_ref, log_ref = refs[3 + 3 * cores :]
    masks = lane_masks(jnp.bfloat16)
    lane = lax.broadcasted_iota(jnp.int32, (1, LANES), 1)
    in_first = lane < LANES // 2
    blocks = query_ref.shape[0] // QUERY_BLOCK
    scale = jnp.asarray(score_scale, jnp.bfloat16)
    for n in range(blocks):
        query = block_of(query_ref, n) * scale
        mark = block_of(mark_ref, n)
        results = []
        for own, other in (masks, masks[::-1]):
            query_head = query * own + mark * other
            tiles = []
            for j in range(max(0, n - reach), n + 1):
                for k in range(cores):
                    key_head = block_of(key_refs[k], j) * own + block_of(key_mark_refs[k], j) * other
                    score = matmul_back(query_head, key_head)
                    if j == n:
                        score = score + causal_ref[k]
                    tiles.append((score, k, j))
            top = tiles[0][0]
            for score, _, _ in tiles[1:]:
                top = jnp.maximum(top, score)
            top = jnp.max(top, axis=-1, keepdims=True)
            total = jnp.zeros((QUERY_BLOCK, LANES), jnp.float32)
            for score, k, j in tiles:
                weight = jnp.exp(score - top).astype(jnp.bfloat16)
                value_head = block_of(value_refs[k], j) * own + other
                total = total + matmul_rows(weight, value_head)
            results.append((total, top))
        (first, first_top), (second, second_top) = results
        swapped = jnp.where(in_first, second, first)
        both = jnp.where(in_first, first, second)
        rows = pl.ds(n * QUERY_BLOCK, QUERY_BLOCK)
        out_ref[rows, :] = (both / pltpu.roll(swapped, LANES // 2, 1)).astype(out_ref.dtype)
        log_ref[rows, :] = jnp.log(swapped) + jnp.where(in_first, second_top, first_top)


def spread(wide):
    high = wide.astype(jnp.bfloat16)
    rest = wide - high.astype(jnp.float32)
    middle = rest.astype(jnp.bfloat16)
    low = (rest - middle.astype(jnp.float32)).astype(jnp.bfloat16)
    return high, middle, low


def pull_kernel(cores, reach, *refs):
    query_ref, mark_ref, grad_ref, out_ref, log_ref = refs[:5]
    key_refs = refs[5 : 5 + cores]
    value_refs = refs[5 + cores : 5 + 2 * cores]
    key_mark_refs = refs[5 + 2 * cores : 5 + 3 * cores]
    causal_ref = refs[5 + 3 * cores]
    outs = refs[6 + 3 * cores :]
    grad_query_ref = outs[0]
    grad_key_refs = outs[1 : 1 + cores]
    grad_value_refs = outs[1 + cores : 1 + 2 * cores]
    query_heads, grad_heads, turned = outs[1 + 2 * cores :]
    own_first, own_second = lane_masks(jnp.bfloat16)
    lane = lax.broadcasted_iota(jnp.int32, (1, LANES), 1)
    slot = lax.rem(lane, LANES // 2)
    picks = [
        (slot == SEGMENT_SLOTS + i).astype(jnp.float32).astype(jnp.bfloat16) for i in range(3)
    ]
    value_mark = -(picks[0] + picks[1] + picks[2])
    row = lax.broadcasted_iota(jnp.int32, (LANES, LANES), 0)
    column = lax.broadcasted_iota(jnp.int32, (LANES, LANES), 1)
    across = ((row < LANES // 2) != (column < LANES // 2)).astype(jnp.float32).astype(jnp.bfloat16)
    blocks = query_ref.shape[0] // QUERY_BLOCK
    scale = jnp.asarray(score_scale, jnp.bfloat16)
    heads = ((own_first, own_second), (own_second, own_first))
    for n in range(blocks):
        rows = pl.ds(n * QUERY_BLOCK, QUERY_BLOCK)
        query = query_ref[rows, :] * scale
        grad = grad_ref[rows, :]
        product = grad.astype(jnp.float32) * out_ref[rows, :].astype(jnp.float32)
        high, middle, _ = spread(product)
        dots = matmul_rows(high, across) + matmul_rows(middle, across)
        high, middle, low = spread(dots)
        grad_mark = high * picks[0] + middle * picks[1] + low * picks[2]
        high, middle, low = spread(log_ref[rows, :])
        mark = mark_ref[rows, :] + high * picks[0] + middle * picks[1] + low * picks[2]
        for h, (own, other) in enumerate(heads):
            query_heads[h, rows, :] = query * own + mark * other
            grad_heads[h, rows, :] = grad * own + grad_mark * other
    turned[...] = jnp.zeros_like(turned)
    half = LANES // 2
    for j in range(blocks):
        for k in range(cores):
            key = block_of(key_refs[k], j)
            value = block_of(value_refs[k], j)
            key_mark = block_of(key_mark_refs[k], j)
            grad_key = [None, None]
            grad_value = [None, None]
            for n in range(j, min(blocks, j + reach + 1)):
                rows = pl.ds(n * QUERY_BLOCK, QUERY_BLOCK)
                for h, (own, other) in enumerate(heads):
                    query_head = query_heads[h, rows, :]
                    grad_head = grad_heads[h, rows, :]
                    score = matmul_back(key * own + key_mark * other, query_head)
                    if j == n:
                        score = score + causal_ref[k]
                    weight = jnp.exp(score)
                    change = matmul_back(value * own + value_mark * other, grad_head)
                    change = (weight * change).astype(jnp.bfloat16)
                    weight = weight.astype(jnp.bfloat16)
                    part = matmul_rows(weight, grad_head)
                    grad_value[h] = part if grad_value[h] is None else grad_value[h] + part
                    part = matmul_rows(change, query_head)
                    grad_key[h] = part if grad_key[h] is None else grad_key[h] + part
                    turn = matmul_over(key * own, change)
                    turned[pl.ds(h * half, half), rows] += turn[h * half : (h + 1) * half, :]
            rows = pl.ds(j * QUERY_BLOCK, QUERY_BLOCK)
            in_first = lane < half
            grad_key_refs[k][rows, :] = jnp.where(in_first, *grad_key).astype(jnp.bfloat16)
            grad_value_refs[k][rows, :] = jnp.where(in_first, *grad_value).astype(jnp.bfloat16)
    grad_query_ref[...] = (turned[...].T * score_scale).astype(jnp.bfloat16)


def attention_calls(tokens, width, cores, reach):
    pair = pl.BlockSpec((tokens, LANES), lambda p: (0, p))
    fixed = pl.BlockSpec((tokens, LANES), lambda p: (0, 0))
    causal = pl.BlockSpec((cores, QUERY_BLOCK, QUERY_BLOCK), lambda p: (0, 0, 0))
    grid = (width // LANES,)
    blocks = tokens // QUERY_BLOCK
    pairs = sum(min(n, reach) + 1 for n in range(blocks)) * cores * QUERY_BLOCK**2 * HEADS
    head_width = width // HEADS
    low = jax.ShapeDtypeStruct((tokens, width), jnp.bfloat16)
    wide = jax.ShapeDtypeStruct((tokens, width), jnp.float32)
    params = pltpu.CompilerParams(
        dimension_semantics=("arbitrary",), vmem_limit_bytes=48 * 1024 * 1024
    )
    forward = pl.pallas_call(
        functools.partial(attend_kernel, cores, reach),
        grid=grid,
        in_specs=[pair, fixed] + [pair] * (2 * cores) + [fixed] * cores + [causal],
        out_specs=[pair, pair],
        out_shape=[low, wide],
        compiler_params=params,
        cost_estimate=pl.CostEstimate(
            flops=4 * pairs * head_width,
            bytes_accessed=2 * tokens * width * (4 + 2 * cores),
            transcendentals=pairs,
        ),
        name="attend",
    )
    backward = pl.pallas_call(
        functools.partial(pull_kernel, cores, reach),
        grid=grid,
        in_specs=[pair, fixed, pair, pair, pair]
        + [pair] * (2 * cores)
        + [fixed] * cores
        + [causal],
        out_specs=[pair] * (1 + 2 * cores),
        out_shape=[low] * (1 + 2 * cores),
        scratch_shapes=[
            pltpu.VMEM((2, tokens, LANES), jnp.bfloat16),
            pltpu.VMEM((2, tokens, LANES), jnp.bfloat16),
            pltpu.VMEM((LANES, tokens), jnp.float32),
        ],
        compiler_params=params,
        cost_estimate=pl.CostEstimate(
            flops=10 * pairs * head_width,
            bytes_accessed=2 * tokens * width * (6 + 4 * cores),
            transcendentals=pairs,
        ),
        name="pull",
    )
    return forward, backward


def body(
    inputs,
    segments,
    groups,
    group_loss_weight,
    attention_norm_gain,
    attention_norm_bias,
    query_key_value_weight,
    query_value_bias,
    attention_out_weight,
    attention_out_bias,
    feedforward_norm_gain,
    feedforward_norm_bias,
    expand_weight,
    expand_bias,
    contract_weight,
    contract_bias,
    adapter_down_maps,
    adapter_up_maps,
    down_velocity,
    up_velocity,
    running_down_mean,
    running_up_mean,
    cotangent,
):
    rows_here, tokens_here, width = inputs.shape
    cores = lax.axis_size("batch")
    ring = lax.axis_size("seq")
    assert rows_here * cores == ring
    stripe = tokens_here // cores
    tokens = ring * stripe
    span = QUERY_BLOCK * cores
    reach = -(-(EXAMPLE_MAX - 1) // span)
    rank = adapter_down_maps.shape[-1]
    core = lax.axis_index("batch")
    attend, pull = attention_calls(tokens, width, cores, reach)

    codes = row_codes(segments * SEGMENT_SLOTS + groups).reshape(ring, cores, stripe)
    values_in = rows_home(inputs).astype(jnp.float32)
    cotangent_home = rows_home(cotangent)

    def codes_of(which):
        return lax.dynamic_index_in_dim(codes, which, 1, keepdims=False).reshape(tokens)

    own_codes = codes_of(core)
    own_groups = lax.rem(own_codes, SEGMENT_SLOTS)
    slot = jnp.arange(LANES, dtype=jnp.int32) % (LANES // 2)

    def one_hot(code_row):
        return (code_row // SEGMENT_SLOTS)[:, None] == slot[None, :]

    query_mark = jnp.where(one_hot(own_codes), masked_score, 0.0).astype(jnp.bfloat16)
    place = jnp.arange(QUERY_BLOCK, dtype=jnp.int32)
    place = tokens_here * (place // stripe) + place % stripe
    key_marks, after = [], []
    for by in range(cores):
        which = lax.rem(core - by + cores, cores)
        key_mark = jnp.where(
            slot[None, :] < SEGMENT_SLOTS,
            1.0 - one_hot(codes_of(which)).astype(jnp.float32),
            jnp.where(slot[None, :] < SEGMENT_SLOTS + 3, -1.0, 0.0),
        )
        key_marks.append(key_mark.astype(jnp.bfloat16))
        key_place = place + stripe * which
        after.append(key_place[None, :] > (place + stripe * core)[:, None])
    causal = jnp.where(jnp.stack(after), masked_score, 0.0).astype(jnp.float32)
    causal_turned = jnp.transpose(causal, (0, 2, 1))

    def first_norm(values):
        return norm_layer(
            values, attention_norm_gain.astype(jnp.float32), attention_norm_bias.astype(jnp.float32)
        )

    def second_norm(values):
        return norm_layer(
            values,
            feedforward_norm_gain.astype(jnp.float32),
            feedforward_norm_bias.astype(jnp.float32),
        )

    normed_low = first_norm(values_in).astype(jnp.bfloat16)
    down_reduced = adapter_down_maps.astype(jnp.bfloat16)
    up_reduced = adapter_up_maps.astype(jnp.bfloat16)
    bias_as_float = query_value_bias.astype(jnp.float32)

    def projected(which):
        return matmul_rows(normed_low, query_key_value_weight[:, which * width : (which + 1) * width])

    lora_down = [matmul_rows(normed_low, down_reduced[j]).astype(jnp.bfloat16) for j in range(2)]
    lora_up = [adapter_scale * matmul_rows(lora_down[j], up_reduced[j]) for j in range(2)]
    keys = projected(1).astype(jnp.bfloat16)
    values = (projected(2) + bias_as_float[1] + lora_up[1]).astype(jnp.bfloat16)
    queries = (projected(0) + bias_as_float[0] + lora_up[0]).astype(jnp.bfloat16)
    all_keys = [keys] + [from_core(keys, by) for by in range(1, cores)]
    all_values = [values] + [from_core(values, by) for by in range(1, cores)]
    attended, log_total = attend(queries, query_mark, *all_keys, *all_values, *key_marks, causal)
    middle = (
        values_in
        + matmul_rows(attended, attention_out_weight)
        + attention_out_bias.astype(jnp.float32)
    )
    normed_two = second_norm(middle).astype(jnp.bfloat16)
    pre_act = matmul_rows(normed_two, expand_weight) + expand_bias.astype(jnp.float32)
    act_low = gelu_tanh(pre_act).astype(jnp.bfloat16)
    layer_result = middle + matmul_rows(act_low, contract_weight) + contract_bias.astype(jnp.float32)
    layer_out = rows_back(layer_result.astype(jnp.bfloat16), rows_here, tokens_here)

    chooser = own_groups[:, None] == jnp.arange(group_loss_weight.shape[0], dtype=jnp.int32)
    token_weight = jnp.sum(jnp.where(chooser, group_loss_weight[None, :], 0.0), axis=-1)
    grad_out = cotangent_home.astype(jnp.float32) * token_weight[:, None]
    grad_act = matmul_back(grad_out.astype(jnp.bfloat16), contract_weight)
    _, gelu_pull = jax.vjp(gelu_tanh, pre_act)
    grad_pre = gelu_pull(grad_act)[0].astype(jnp.bfloat16)
    _, second_pull = jax.vjp(second_norm, middle)
    grad_middle = grad_out + second_pull(matmul_back(grad_pre, expand_weight))[0]
    grad_attended = matmul_back(grad_middle.astype(jnp.bfloat16), attention_out_weight).astype(
        jnp.bfloat16
    )
    pulled = pull(
        queries,
        query_mark,
        grad_attended,
        attended,
        log_total,
        *all_keys,
        *all_values,
        *key_marks,
        causal_turned,
    )
    grad_queries = pulled[0]

    def owned(parts):
        total = parts[0].astype(jnp.float32)
        for by in range(1, cores):
            total = total + from_core(parts[by], -by).astype(jnp.float32)
        return total.astype(jnp.bfloat16)

    grad_keys = owned(pulled[1 : 1 + cores])
    grad_values = owned(pulled[1 + cores :])
    incoming = (grad_queries, grad_values)
    up_parts = [adapter_scale * matmul_over(lora_down[j], incoming[j]) for j in range(2)]
    grad_down = [
        (adapter_scale * matmul_back(incoming[j], up_reduced[j])).astype(jnp.bfloat16)
        for j in range(2)
    ]
    down_parts = [matmul_over(grad_down[j], normed_low) for j in range(2)]
    adapter_sums = sum_everywhere(jnp.concatenate(up_parts + down_parts, axis=0))
    adapter_sums = adapter_sums.reshape(2, 2, rank, width)
    up_map_gradient = adapter_sums[0]
    down_map_gradient = jnp.transpose(adapter_sums[1], (0, 2, 1))
    grad_normed = matmul_back(
        jnp.concatenate([grad_queries, grad_keys, grad_values], axis=-1), query_key_value_weight
    )
    for j in range(2):
        grad_normed = grad_normed + matmul_back(grad_down[j], down_reduced[j])
    _, first_pull = jax.vjp(first_norm, values_in)
    input_grad = (grad_middle + first_pull(grad_normed)[0]).astype(jnp.bfloat16)
    input_grad = rows_back(input_grad, rows_here, tokens_here)

    down_velocity_next = velocity_factor * down_velocity + down_map_gradient
    up_velocity_next = velocity_factor * up_velocity + up_map_gradient
    adapter_down_updated = adapter_down_maps - learning_step_size * (
        down_map_gradient + velocity_factor * down_velocity_next
    )
    adapter_up_updated = adapter_up_maps - learning_step_size * (
        up_map_gradient + velocity_factor * up_velocity_next
    )
    updated_down_mean = (
        mean_decay_factor * running_down_mean + (1.0 - mean_decay_factor) * adapter_down_updated
    )
    updated_up_mean = (
        mean_decay_factor * running_up_mean + (1.0 - mean_decay_factor) * adapter_up_updated
    )
    return (
        layer_out,
        input_grad,
        down_map_gradient,
        up_map_gradient,
        adapter_down_updated,
        adapter_up_updated,
        down_velocity_next,
        up_velocity_next,
        updated_down_mean,
        updated_up_mean,
        adapter_down_updated.astype(jnp.bfloat16),
        adapter_up_updated.astype(jnp.bfloat16),
    )


def solution(mesh):
    tokens = P("batch", "seq", None)
    codes = P("batch", "seq")
    return jax.shard_map(
        body,
        mesh=mesh,
        in_specs=(tokens, codes, codes) + (P(),) * 19 + (tokens,),
        out_specs=(tokens, tokens) + (P(),) * 10,
        check_vma=False,
    )
```

```python
import functools

import jax
import jax.numpy as jnp
from jax import lax
from jax.experimental import pallas as pl
from jax.experimental.pallas import tpu as pltpu
from jax.sharding import PartitionSpec as P

HEADS = 16
EXAMPLE_MAX = 1024
SEGMENT_SLOTS = 8
LANES = 128
QUERY_BLOCK = 256
TOKEN_BLOCK = 256
HIDDEN_BLOCK = 1024
AHEAD = 3

norm_eps = 1e-05
adapter_scale = 8.0
learning_step_size = 3e-05
velocity_factor = 0.5
mean_decay_factor = 0.5
masked_score = -1e30
score_scale = 0.125


def matmul_rows(left_side, right_side):
    return lax.dot_general(
        left_side, right_side, (((1,), (0,)), ((), ())), preferred_element_type=jnp.float32
    )


def matmul_back(left_side, right_side):
    return lax.dot_general(
        left_side, right_side, (((1,), (1,)), ((), ())), preferred_element_type=jnp.float32
    )


def matmul_over(left_side, right_side):
    return lax.dot_general(
        left_side, right_side, (((0,), (0,)), ((), ())), preferred_element_type=jnp.float32
    )


def gather_kernel(cores, with_codes, core_ref, *refs):
    stripes, codes, out_ref = refs[:cores], refs[cores:-1], refs[-1]
    came_from = lax.rem(core_ref[0] - pl.program_id(0) + cores, cores)
    stripe, width = stripes[0].shape[1:]
    for by in range(cores):

        @pl.when(came_from == by)
        def _(by=by):
            for group in range(width // LANES):
                rows = pl.ds(group * stripe, stripe)
                out_ref[:, rows, :] = stripes[by][:, :, group * LANES : (group + 1) * LANES]
            if with_codes:
                out_ref[:, width // LANES * stripe :, :] = codes[by][...]


def gather_stripes(x, codes=None):
    cores = lax.axis_size("batch")
    core = lax.axis_index("batch")
    rows, tokens, width = x.shape
    stripe = tokens // cores
    parts, extra = [x], [] if codes is None else [codes]
    for by in range(1, cores):
        goes = lax.rem(core + by, cores)
        parts.append(from_core(lax.dynamic_slice_in_dim(x, goes * stripe, stripe, 1), by))
        extra += [] if codes is None else [from_core(codes, by)]
    deep = width // LANES * stripe + sum(c.shape[1] for c in extra[:1])
    whole = pl.BlockSpec((rows, stripe, width), lambda c, core: (0, 0, 0))
    return pl.pallas_call(
        functools.partial(gather_kernel, cores, bool(extra)),
        grid_spec=pltpu.PrefetchScalarGridSpec(
            num_scalar_prefetch=1,
            grid=(cores,),
            in_specs=[pl.BlockSpec((rows, stripe, width), lambda c, core: (0, core[0], 0))]
            + [whole] * (cores - 1)
            + [pl.BlockSpec(c.shape, lambda c, core: (0, 0, 0)) for c in extra],
            out_specs=pl.BlockSpec((rows, deep, LANES), lambda c, core: (c, 0, 0)),
        ),
        out_shape=jax.ShapeDtypeStruct((rows * cores, deep, LANES), x.dtype),
        compiler_params=pltpu.CompilerParams(vmem_limit_bytes=32 * 1024 * 1024),
        name="gather_stripes",
    )(core[None], *parts, *extra)


def spread_kernel(cores, core_ref, *refs):
    came_from = lax.rem(core_ref[0] - pl.program_id(0) + cores, cores)
    for by in range(cores):

        @pl.when(came_from == by)
        def _(by=by):
            refs[-1][...] = refs[by][...]


def spread_stripes(y):
    cores = lax.axis_size("batch")
    core = lax.axis_index("batch")
    rows, stripe, width = y.shape[0] // cores, *y.shape[1:]
    parts = [y]
    for by in range(1, cores):
        goes = lax.rem(core + by, cores)
        parts.append(from_core(lax.dynamic_slice_in_dim(y, goes * rows, rows, 0), by))
    block = (rows, stripe, width)
    return pl.pallas_call(
        functools.partial(spread_kernel, cores),
        grid_spec=pltpu.PrefetchScalarGridSpec(
            num_scalar_prefetch=1,
            grid=(cores,),
            in_specs=[pl.BlockSpec(block, lambda c, core: (core[0], 0, 0))]
            + [pl.BlockSpec(block, lambda c, core: (0, 0, 0))] * (cores - 1),
            out_specs=pl.BlockSpec(block, lambda c, core: (0, c, 0)),
        ),
        out_shape=jax.ShapeDtypeStruct((rows, stripe * cores, width), y.dtype),
        compiler_params=pltpu.CompilerParams(vmem_limit_bytes=32 * 1024 * 1024),
        name="spread_stripes",
    )(core[None], *parts)


def rows_home(y):
    return lax.all_to_all(y, "seq", 0, 0, tiled=True)


def rows_back(y):
    ring = lax.axis_size("seq")
    y = y.reshape(ring, y.shape[0] // ring, y.shape[1])
    return lax.all_to_all(y, "seq", 0, 0, tiled=True)


def tokens_of(ref, stripe, width):
    groups = []
    for group in range(width // LANES):
        rows = slice(group * stripe, (group + 1) * stripe)
        groups.append(jnp.concatenate([ref[c, rows, :] for c in range(ref.shape[0])], axis=0))
    return jnp.concatenate(groups, axis=1)


def from_core(x, by):
    cores = lax.axis_size("batch")
    return lax.ppermute(x, "batch", [(i, (i + by) % cores) for i in range(cores)])


def sum_everywhere(x):
    for axis in ("batch", "seq"):
        size = lax.axis_size(axis)
        step = 1
        while step < size:
            x = x + lax.ppermute(x, axis, [(i, i ^ step) for i in range(size)])
            step *= 2
    return x


def lane_masks(dtype):
    lane = lax.broadcasted_iota(jnp.int32, (1, LANES), 1)
    first = (lane < LANES // 2).astype(jnp.float32).astype(dtype)
    second = (lane >= LANES // 2).astype(jnp.float32).astype(dtype)
    return first, second


def block_of(ref, index):
    return ref[pl.ds(index * QUERY_BLOCK, QUERY_BLOCK), :]


def attend_kernel(cores, reach, *refs):
    far_ref, query_ref, mark_ref = refs[:3]
    key_refs = refs[3 : 3 + cores]
    value_refs = refs[3 + cores : 3 + 2 * cores]
    key_mark_refs = refs[3 + 2 * cores : 3 + 3 * cores]
    causal_ref = refs[3 + 3 * cores]
    out_ref, log_ref, key_heads, turned_values = refs[4 + 3 * cores :]
    heads = lane_masks(jnp.bfloat16)
    half = LANES // 2
    blocks = query_ref.shape[0] // QUERY_BLOCK
    tile = cores * QUERY_BLOCK
    scale = jnp.asarray(score_scale, jnp.bfloat16)
    for h in range(2):
        turned_values[h, half:, :] = jnp.ones_like(turned_values[h, half:, :])
    for j in range(blocks):
        for k in range(cores):
            key = block_of(key_refs[k], j)
            key_mark = block_of(key_mark_refs[k], j)
            turned = block_of(value_refs[k], j).T
            at = pl.ds(j * tile + k * QUERY_BLOCK, QUERY_BLOCK)
            for h, own in enumerate(heads):
                key_heads[h, at, :] = key * own + key_mark * heads[1 - h]
                turned_values[h, :half, at] = turned[h * half : (h + 1) * half]

    def scores_of(n, h, start):
        query_head = block_of(query_ref, n) * scale * heads[h] + block_of(mark_ref, n) * heads[1 - h]
        scores = []
        for j in range(start, n + 1):
            score = matmul_back(key_heads[h, pl.ds(j * tile, tile), :], query_head)
            scores.append(score + causal_ref[...] if j == n else score)
        return scores

    def finish(n, h, start, scores):
        rows = pl.ds(n * QUERY_BLOCK, QUERY_BLOCK)
        top = scores[0]
        for score in scores[1:]:
            top = jnp.maximum(top, score)
        top = jnp.max(top, axis=0, keepdims=True)
        weights = [jnp.exp(score - top).astype(jnp.bfloat16) for score in scores]
        keys = pl.ds(start * tile, (n + 1 - start) * tile)
        out = matmul_rows(turned_values[h, :, keys], jnp.concatenate(weights))
        total = out[half : half + 1]
        log_ref[h : h + 1, rows] = top + jnp.log(total)
        return out[:half] / total

    def every(skipped):
        waiting, outs = [], []
        units = []
        for n in range(blocks):
            start = max(0, n - reach) + (skipped and n == blocks - 1)
            units += [(n, h, start) for h in range(2)]
        for unit in units + [None] * AHEAD:
            if unit is not None:
                waiting.append((unit, scores_of(*unit)))
            if len(waiting) > AHEAD or unit is None:
                done, scores = waiting.pop(0)
                outs.append(finish(*done, scores))
                if len(outs) == 2:
                    rows = pl.ds(done[0] * QUERY_BLOCK, QUERY_BLOCK)
                    out_ref[rows, :] = jnp.concatenate(outs).T.astype(out_ref.dtype)
                    outs = []

    either_way(every, far_ref, blocks > reach)


def either_way(every, far_ref, can_skip):
    if not can_skip:
        every(False)
        return
    pl.when(far_ref[0] == 1)(functools.partial(every, False))
    pl.when(far_ref[0] != 1)(functools.partial(every, True))


def spread(wide):
    high = wide.astype(jnp.bfloat16)
    return high, (wide - high.astype(jnp.float32)).astype(jnp.bfloat16)


def pull_kernel(cores, reach, *refs):
    far_ref, query_ref, mark_ref, grad_ref, out_ref, log_ref = refs[:6]
    key_refs = refs[6 : 6 + cores]
    value_refs = refs[6 + cores : 6 + 2 * cores]
    key_mark_refs = refs[6 + 2 * cores : 6 + 3 * cores]
    causal_ref = refs[6 + 3 * cores]
    outs = refs[7 + 3 * cores :]
    grad_query_ref = outs[0]
    grad_key_refs = outs[1 : 1 + cores]
    grad_value_refs = outs[1 + cores : 1 + 2 * cores]
    (
        query_heads, key_heads, value_heads, turned_queries, turned_keys, turned_grads,
        turned_sums, dots,
    ) = outs[1 + 2 * cores :]
    heads = lane_masks(jnp.bfloat16)
    half = LANES // 2
    blocks = query_ref.shape[0] // QUERY_BLOCK
    tile = cores * QUERY_BLOCK
    scale = jnp.asarray(score_scale, jnp.bfloat16)
    lane = lax.broadcasted_iota(jnp.int32, (8, LANES), 1)
    row = lax.broadcasted_iota(jnp.int32, (8, LANES), 0)
    chooser = (lane // half == row).astype(jnp.float32).astype(jnp.bfloat16)
    for n in range(blocks):
        rows = pl.ds(n * QUERY_BLOCK, QUERY_BLOCK)
        query = query_ref[rows, :] * scale
        grad = grad_ref[rows, :]
        high, rest = spread(grad.astype(jnp.float32) * out_ref[rows, :].astype(jnp.float32))
        dots[:, rows] = matmul_back(chooser, high) + matmul_back(chooser, rest)
        turned_queries[:, rows] = query.T
        turned_grads[:, rows] = grad.T
        for h, own in enumerate(heads):
            query_heads[h, rows, :] = query * own + mark_ref[rows, :] * heads[1 - h]
        for k in range(cores):
            key = block_of(key_refs[k], n)
            key_mark = block_of(key_mark_refs[k], n)
            value = block_of(value_refs[k], n)
            at = pl.ds(n * tile + k * QUERY_BLOCK, QUERY_BLOCK)
            turned_keys[:, at] = key.T
            for h, own in enumerate(heads):
                key_heads[h, at, :] = key * own + key_mark * heads[1 - h]
                value_heads[h, at, :] = value * own
    turned_sums[...] = jnp.zeros_like(turned_sums)

    def products(j, n, h):
        keys = pl.ds(j * tile, tile)
        rows = pl.ds(n * QUERY_BLOCK, QUERY_BLOCK)
        score = matmul_back(key_heads[h, keys, :], query_heads[h, rows, :])
        change = matmul_back(value_heads[h, keys, :], grad_ref[rows, :])
        return score, change

    def weigh(j, n, h, score, change):
        rows = pl.ds(n * QUERY_BLOCK, QUERY_BLOCK)
        if n == j:
            score = score + causal_ref[...]
        weight = jnp.exp(score - log_ref[h : h + 1, rows])
        change = (weight * (change - dots[h : h + 1, rows])).astype(jnp.bfloat16)
        return weight.astype(jnp.bfloat16), change

    def finish(j, h, members):
        part = pl.ds(h * half, half)
        keys = pl.ds(j * tile, tile)
        rows = pl.ds(members[0][0] * QUERY_BLOCK, len(members) * QUERY_BLOCK)
        weights = jnp.concatenate([m[1] for m in members], axis=1)
        changes = jnp.concatenate([m[2] for m in members], axis=1)
        turned_sums[part, rows] += matmul_rows(turned_keys[part, keys], changes)
        return (
            matmul_back(turned_queries[part, rows], changes),
            matmul_back(turned_grads[part, rows], weights),
        )

    def every(skipped):
        units = []
        for j in range(blocks):
            last = min(blocks - 1, j + reach)
            if skipped and j + reach == blocks - 1:
                last -= 1
            units += [(j, n, h, n == last) for h in range(2) for n in range(j, last + 1)]
        waiting, members, sums = [], [], []
        for unit in units + [None] * AHEAD:
            if unit is not None:
                waiting.append((unit, products(*unit[:3])))
            if len(waiting) > AHEAD or unit is None:
                (j, n, h, closing), pair = waiting.pop(0)
                members.append((n, *weigh(j, n, h, *pair)))
                if closing:
                    sums.append(finish(j, h, members))
                    members = []
                if len(sums) == 2:
                    for out_refs, which in ((grad_key_refs, 0), (grad_value_refs, 1)):
                        both = jnp.concatenate([s[which] for s in sums]).T.astype(jnp.bfloat16)
                        for k in range(cores):
                            out_refs[k][pl.ds(j * QUERY_BLOCK, QUERY_BLOCK), :] = both[
                                k * QUERY_BLOCK : (k + 1) * QUERY_BLOCK
                            ]
                    sums = []

    either_way(every, far_ref, blocks > reach)
    grad_query_ref[...] = (turned_sums[...] * score_scale).T.astype(jnp.bfloat16)


def standardized(values):
    average = jnp.mean(values, axis=-1, keepdims=True)
    centred = values - average
    spread_inverse = lax.rsqrt(jnp.mean(centred * centred, axis=-1, keepdims=True) + norm_eps)
    return centred * spread_inverse, spread_inverse


def norm_pull(grad, shaped, spread_inverse):
    mean_grad = jnp.mean(grad, axis=-1, keepdims=True)
    mean_product = jnp.mean(grad * shaped, axis=-1, keepdims=True)
    return spread_inverse * (grad - mean_grad - shaped * mean_product)


def enter_kernel(
    stripe, x_ref, gain_ref, shift_ref, weight_ref, bias_ref, down_ref, up_ref,
    query_ref, key_ref, value_ref, lora_ref,
):
    width = key_ref.shape[1]
    shaped, _ = standardized(tokens_of(x_ref, stripe, width).astype(jnp.float32))
    normed = (shaped * gain_ref[...] + shift_ref[...]).astype(jnp.bfloat16)
    lora = matmul_rows(normed, down_ref[...]).astype(jnp.bfloat16)
    lora_ref[...] = lora
    key_ref[...] = matmul_rows(normed, weight_ref[:, width : 2 * width]).astype(jnp.bfloat16)
    for out_ref, j, at in ((value_ref, 1, 2), (query_ref, 0, 0)):
        out = matmul_rows(normed, weight_ref[:, at * width : (at + 1) * width])
        out = out + matmul_rows(lora, up_ref[:, j * width : (j + 1) * width])
        out_ref[...] = (out + bias_ref[j : j + 1, :]).astype(jnp.bfloat16)


root_two_over_pi = 0.7978845608028654
cubic = 0.044715


def middle_kernel(
    stripe, x_ref, attended_ref, cotangent_ref, token_weight_ref,
    out_weight_ref, out_bias_ref, gain_ref, shift_ref,
    expand_ref, expand_bias_ref, contract_ref, contract_bias_ref,
    result_ref, grad_middle_ref, grad_attended_ref,
):
    width = attended_ref.shape[1]
    middle = (
        tokens_of(x_ref, stripe, width).astype(jnp.float32)
        + matmul_rows(attended_ref[...], out_weight_ref[...])
        + out_bias_ref[...]
    )
    shaped, spread_inverse = standardized(middle)
    normed = (shaped * gain_ref[...] + shift_ref[...]).astype(jnp.bfloat16)
    grad_out = tokens_of(cotangent_ref, stripe, width).astype(jnp.float32) * token_weight_ref[...]
    grad_low = grad_out.astype(jnp.bfloat16)
    result = middle + contract_bias_ref[...]
    grad_normed = jnp.zeros_like(middle)
    hidden = expand_ref.shape[1]
    for at in range(0, hidden, HIDDEN_BLOCK):
        part = slice(at, at + HIDDEN_BLOCK)
        pre = matmul_rows(normed, expand_ref[:, part]) + expand_bias_ref[:, part]
        grad_act = matmul_back(grad_low, contract_ref[part, :])
        square = pre * pre
        bent = jnp.tanh(root_two_over_pi * pre * (1.0 + cubic * square))
        upper = 0.5 + 0.5 * bent
        act = (pre * upper).astype(jnp.bfloat16)
        slope = upper + (0.5 * root_two_over_pi) * pre * (1.0 - bent * bent) * (
            1.0 + (3.0 * cubic) * square
        )
        grad_pre = (grad_act * slope).astype(jnp.bfloat16)
        result = result + matmul_rows(act, contract_ref[part, :])
        grad_normed = grad_normed + matmul_back(grad_pre, expand_ref[:, part])
    result_ref[...] = result.astype(jnp.bfloat16)
    grad_middle = grad_out + norm_pull(grad_normed * gain_ref[...], shaped, spread_inverse)
    grad_middle_low = grad_middle.astype(jnp.bfloat16)
    grad_middle_ref[...] = grad_middle_low
    grad_attended_ref[...] = matmul_back(grad_middle_low, out_weight_ref[...]).astype(jnp.bfloat16)


def total(parts):
    out = parts[0][...].astype(jnp.float32)
    for part in parts[1:]:
        out = out + part[...].astype(jnp.float32)
    return out.astype(jnp.bfloat16)


def adapt_kernel(
    stripe, cores, x_ref, gain_ref, shift_ref, up_ref, lora_ref, grad_query_ref, *refs
):
    value_refs = refs[:cores]
    grad_lora_ref, down_sum_ref, up_sum_ref = refs[cores:]
    slots = down_sum_ref.shape[0]

    @pl.when(pl.program_id(0) == 0)
    def _():
        down_sum_ref[...] = jnp.zeros_like(down_sum_ref)
        up_sum_ref[...] = jnp.zeros_like(up_sum_ref)

    width = grad_query_ref.shape[1]
    grad_query = grad_query_ref[...]
    grad_value = total(value_refs)
    shaped, _ = standardized(tokens_of(x_ref, stripe, width).astype(jnp.float32))
    normed = (shaped * gain_ref[...] + shift_ref[...]).astype(jnp.bfloat16)
    grad_lora = matmul_back(grad_query, up_ref[:, :width]) + matmul_back(
        grad_value, up_ref[:, width:]
    )
    grad_lora = grad_lora.astype(jnp.bfloat16)
    grad_lora_ref[...] = grad_lora
    lora = lora_ref[...]
    down_sum_ref[...] += matmul_over(grad_lora, normed)[:slots]
    up_sum_ref[:, :width] += matmul_over(lora, grad_query)[:slots]
    up_sum_ref[:, width:] += matmul_over(lora, grad_value)[:slots]


def leave_kernel(
    stripe, cores, x_ref, gain_ref, weight_ref, down_ref, grad_lora_ref, grad_middle_ref,
    grad_query_ref, *refs,
):
    key_refs, value_refs, grad_ref = refs[:cores], refs[cores : 2 * cores], refs[-1]
    width = grad_query_ref.shape[1]
    shaped, spread_inverse = standardized(tokens_of(x_ref, stripe, width).astype(jnp.float32))
    grad_normed = (
        matmul_back(grad_query_ref[...], weight_ref[:, :width])
        + matmul_back(total(key_refs), weight_ref[:, width : 2 * width])
        + matmul_back(total(value_refs), weight_ref[:, 2 * width :])
        + matmul_back(grad_lora_ref[...], down_ref[...])
    )
    grad = norm_pull(grad_normed * gain_ref[...], shaped, spread_inverse)
    grad_ref[...] = (grad_middle_ref[...].astype(jnp.float32) + grad).astype(jnp.bfloat16)


def over_tokens(kernel, name, tokens, tiled, fixed, outs, sums, flops):
    block = min(TOKEN_BLOCK, tokens)

    def tile(x):
        share = x.shape[0] * block // tokens
        return pl.BlockSpec((share, *x.shape[1:]), lambda i: (i,) + (0,) * (x.ndim - 1))

    def whole(x, **how):
        return pl.BlockSpec(x.shape, lambda i: (0,) * x.ndim, **how)

    kept = dict(pipeline_mode=pl.Buffered(1))
    moved = sum(x.size * x.dtype.itemsize for x in [*tiled, *fixed, *outs, *sums])
    order = kernel[1]
    operands = order(tiled, fixed)
    known = {id(x): tile(x) for x in tiled} | {id(x): whole(x, **kept) for x in fixed}
    return pl.pallas_call(
        kernel[0],
        grid=(tokens // block,),
        in_specs=[known[id(x)] for x in operands],
        out_specs=[tile(x) for x in outs] + [whole(x) for x in sums],
        out_shape=[*outs, *sums],
        compiler_params=pltpu.CompilerParams(
            dimension_semantics=("arbitrary",), vmem_limit_bytes=56 * 1024 * 1024
        ),
        cost_estimate=pl.CostEstimate(flops=flops, bytes_accessed=moved, transcendentals=0),
        name=name,
    )(*operands)


def attention_calls(tokens, width, cores, reach):
    pair = pl.BlockSpec((tokens, LANES), lambda p, far: (0, p))
    fixed = pl.BlockSpec((tokens, LANES), lambda p, far: (0, 0))
    causal = pl.BlockSpec((cores * QUERY_BLOCK, QUERY_BLOCK), lambda p, far: (0, 0))
    logs = pl.BlockSpec((8, tokens), lambda p, far: (p, 0))
    grid = (width // LANES,)
    blocks = tokens // QUERY_BLOCK
    pairs = sum(min(n, reach) + 1 for n in range(blocks)) * cores * QUERY_BLOCK**2 * HEADS
    head_width = width // HEADS
    low = jax.ShapeDtypeStruct((tokens, width), jnp.bfloat16)
    log_rows = jax.ShapeDtypeStruct((8 * grid[0], tokens), jnp.float32)
    params = pltpu.CompilerParams(
        dimension_semantics=("arbitrary",), vmem_limit_bytes=40 * 1024 * 1024
    )
    low_scratch = functools.partial(pltpu.VMEM, dtype=jnp.bfloat16)
    forward = pl.pallas_call(
        functools.partial(attend_kernel, cores, reach),
        grid_spec=pltpu.PrefetchScalarGridSpec(
            num_scalar_prefetch=1,
            grid=grid,
            in_specs=[pair, fixed] + [pair] * (2 * cores) + [fixed] * cores + [causal],
            out_specs=[pair, logs],
            scratch_shapes=[
                low_scratch((2, cores * tokens, LANES)),
                low_scratch((2, LANES // 2 + 16, cores * tokens)),
            ],
        ),
        out_shape=[low, log_rows],
        compiler_params=params,
        cost_estimate=pl.CostEstimate(
            flops=4 * pairs * head_width,
            bytes_accessed=2 * tokens * width * (2 + 2 * cores),
            transcendentals=pairs,
        ),
        name="attend",
    )
    backward = pl.pallas_call(
        functools.partial(pull_kernel, cores, reach),
        grid_spec=pltpu.PrefetchScalarGridSpec(
            num_scalar_prefetch=1,
            grid=grid,
            in_specs=[pair, fixed, pair, pair, logs]
            + [pair] * (2 * cores)
            + [fixed] * cores
            + [causal],
            out_specs=[pair] * (1 + 2 * cores),
            scratch_shapes=[
                low_scratch((2, tokens, LANES)),
                low_scratch((2, cores * tokens, LANES)),
                low_scratch((2, cores * tokens, LANES)),
                low_scratch((LANES, tokens)),
                low_scratch((LANES, cores * tokens)),
                low_scratch((LANES, tokens)),
                pltpu.VMEM((LANES, tokens), jnp.float32),
                pltpu.VMEM((8, tokens), jnp.float32),
            ],
        ),
        out_shape=[low] * (1 + 2 * cores),
        compiler_params=params,
        cost_estimate=pl.CostEstimate(
            flops=10 * pairs * head_width,
            bytes_accessed=2 * tokens * width * (4 + 4 * cores),
            transcendentals=pairs,
        ),
        name="pull",
    )
    return forward, backward


def body(
    inputs,
    segments,
    groups,
    group_loss_weight,
    attention_norm_gain,
    attention_norm_bias,
    query_key_value_weight,
    query_value_bias,
    attention_out_weight,
    attention_out_bias,
    feedforward_norm_gain,
    feedforward_norm_bias,
    expand_weight,
    expand_bias,
    contract_weight,
    contract_bias,
    adapter_down_maps,
    adapter_up_maps,
    down_velocity,
    up_velocity,
    running_down_mean,
    running_up_mean,
    cotangent,
):
    rows_here, tokens_here, width = inputs.shape
    cores = lax.axis_size("batch")
    ring = lax.axis_size("seq")
    assert rows_here * cores == ring
    stripe = tokens_here // cores
    tokens = ring * stripe
    span = QUERY_BLOCK * cores
    reach = -(-(EXAMPLE_MAX - 1) // span)
    rank = adapter_down_maps.shape[-1]
    core = lax.axis_index("batch")
    attend, pull = attention_calls(tokens, width, cores, reach)

    assert tokens_here == LANES
    codes = (segments * SEGMENT_SLOTS + groups).astype(jnp.bfloat16)
    codes = jnp.broadcast_to(codes[:, None, :], (rows_here, 8, tokens_here))
    x = rows_home(gather_stripes(inputs, codes))
    stripes, x = lax.optimization_barrier((gather_stripes(cotangent), x))
    cotangent_home = rows_home(stripes)
    row_codes = x[:, width // LANES * stripe, :].astype(jnp.int32)
    row_segments = (row_codes // SEGMENT_SLOTS).reshape(ring * tokens_here)
    codes = row_codes.reshape(ring, cores, stripe)
    last = max(0, tokens // QUERY_BLOCK - 1 - reach)
    far = row_segments[span * (last + 1) - 1] >= row_segments[span * (tokens // QUERY_BLOCK - 1)]
    far = far.astype(jnp.int32)[None]

    def codes_of(which):
        return lax.dynamic_index_in_dim(codes, which, 1, keepdims=False).reshape(tokens)

    own_codes = codes_of(core)
    own_groups = lax.rem(own_codes, SEGMENT_SLOTS)
    slot = jnp.arange(LANES, dtype=jnp.int32) % (LANES // 2)

    def one_hot(code_row):
        return (code_row // SEGMENT_SLOTS)[:, None] == slot[None, :]

    query_mark = jnp.where(one_hot(own_codes), masked_score, 0.0).astype(jnp.bfloat16)
    place = jnp.arange(QUERY_BLOCK, dtype=jnp.int32)
    place = tokens_here * (place // stripe) + place % stripe
    key_marks, after = [], []
    for by in range(cores):
        which = lax.rem(core - by + cores, cores)
        key_mark = jnp.where(
            slot[None, :] < SEGMENT_SLOTS,
            1.0 - one_hot(codes_of(which)).astype(jnp.float32),
            jnp.where(slot[None, :] < SEGMENT_SLOTS + 3, -1.0, 0.0),
        )
        key_marks.append(key_mark.astype(jnp.bfloat16))
        key_place = place + stripe * which
        after.append(key_place[:, None] > (place + stripe * core)[None, :])
    causal = jnp.where(jnp.concatenate(after), masked_score, 0.0).astype(jnp.float32)

    def row_of(vector):
        return vector.astype(jnp.float32).reshape(1, -1)

    first_gain, first_shift = row_of(attention_norm_gain), row_of(attention_norm_bias)
    second_gain, second_shift = row_of(feedforward_norm_gain), row_of(feedforward_norm_bias)
    pad = LANES - 2 * rank
    down_packed = jnp.concatenate([adapter_down_maps[0], adapter_down_maps[1]], axis=1)
    down_packed = jnp.pad(down_packed, ((0, 0), (0, pad))).astype(jnp.bfloat16)
    up_packed = jnp.concatenate(
        [
            jnp.pad(adapter_up_maps[0], ((0, rank + pad), (0, 0))),
            jnp.pad(adapter_up_maps[1], ((rank, pad), (0, 0))),
        ],
        axis=1,
    )
    up_packed = (adapter_scale * up_packed).astype(jnp.bfloat16)
    chooser = own_groups[:, None] == jnp.arange(group_loss_weight.shape[0], dtype=jnp.int32)
    token_weight = jnp.sum(
        jnp.where(chooser, group_loss_weight[None, :], 0.0), axis=-1, keepdims=True
    )
    low = jax.ShapeDtypeStruct((tokens, width), jnp.bfloat16)
    queries, keys, values, lora = over_tokens(
        (functools.partial(enter_kernel, stripe), lambda t, f: [*t, *f]),
        "enter",
        tokens,
        [x],
        [
            first_gain,
            first_shift,
            query_key_value_weight,
            query_value_bias.astype(jnp.float32),
            down_packed,
            up_packed,
        ],
        [low, low, low, jax.ShapeDtypeStruct((tokens, LANES), jnp.bfloat16)],
        [],
        6 * tokens * width * width,
    )
    all_keys = [keys] + [from_core(keys, by) for by in range(1, cores)]
    all_values = [values] + [from_core(values, by) for by in range(1, cores)]
    attended, log_total = attend(far, queries, query_mark, *all_keys, *all_values, *key_marks, causal)

    hidden = expand_weight.shape[1]
    layer_result, grad_middle, grad_attended = over_tokens(
        (functools.partial(middle_kernel, stripe), lambda t, f: [*t, *f]),
        "middle",
        tokens,
        [x, attended, cotangent_home, token_weight],
        [
            attention_out_weight,
            row_of(attention_out_bias),
            second_gain,
            second_shift,
            expand_weight,
            row_of(expand_bias),
            contract_weight,
            row_of(contract_bias),
        ],
        [low, low, low],
        [],
        4 * tokens * width * (width + 2 * hidden),
    )
    layer_out = rows_back(layer_result)

    pulled = pull(
        far,
        queries,
        query_mark,
        grad_attended,
        attended,
        log_total,
        *all_keys,
        *all_values,
        *key_marks,
        causal,
    )

    layer_out, pulled = lax.optimization_barrier((layer_out, pulled))
    layer_out = spread_stripes(layer_out)

    def owned(parts):
        return [parts[0]] + [from_core(parts[by], -by) for by in range(1, cores)]

    sums = [
        jax.ShapeDtypeStruct((2 * rank, width), jnp.float32),
        jax.ShapeDtypeStruct((2 * rank, 2 * width), jnp.float32),
    ]
    owned_values = owned(pulled[1 + cores :])
    owned_keys = owned(pulled[1 : 1 + cores])
    grad_lora, down_sum, up_sum = over_tokens(
        (functools.partial(adapt_kernel, stripe, cores), lambda t, f: [t[0], *f, *t[1:]]),
        "adapt",
        tokens,
        [x, lora, pulled[0], *owned_values],
        [first_gain, first_shift, up_packed],
        [jax.ShapeDtypeStruct((tokens, LANES), jnp.bfloat16)],
        sums,
        1024 * tokens * width,
    )
    (input_grad,) = over_tokens(
        (functools.partial(leave_kernel, stripe, cores), lambda t, f: [t[0], *f, *t[1:]]),
        "leave",
        tokens,
        [x, grad_lora, grad_middle, pulled[0], *owned_keys, *owned_values],
        [first_gain, query_key_value_weight, down_packed],
        [low],
        [],
        6 * tokens * width * width,
    )
    input_grad = spread_stripes(rows_back(input_grad))
    up_parts = [
        adapter_scale * up_sum[j * rank : (j + 1) * rank, j * width : (j + 1) * width]
        for j in range(2)
    ]
    adapter_sums = sum_everywhere(jnp.concatenate([*up_parts, down_sum], axis=0))
    adapter_sums = adapter_sums.reshape(2, 2, rank, width)
    up_map_gradient = adapter_sums[0]
    down_map_gradient = jnp.transpose(adapter_sums[1], (0, 2, 1))

    down_velocity_next = velocity_factor * down_velocity + down_map_gradient
    up_velocity_next = velocity_factor * up_velocity + up_map_gradient
    adapter_down_updated = adapter_down_maps - learning_step_size * (
        down_map_gradient + velocity_factor * down_velocity_next
    )
    adapter_up_updated = adapter_up_maps - learning_step_size * (
        up_map_gradient + velocity_factor * up_velocity_next
    )
    updated_down_mean = (
        mean_decay_factor * running_down_mean + (1.0 - mean_decay_factor) * adapter_down_updated
    )
    updated_up_mean = (
        mean_decay_factor * running_up_mean + (1.0 - mean_decay_factor) * adapter_up_updated
    )
    return (
        layer_out,
        input_grad,
        down_map_gradient,
        up_map_gradient,
        adapter_down_updated,
        adapter_up_updated,
        down_velocity_next,
        up_velocity_next,
        updated_down_mean,
        updated_up_mean,
        adapter_down_updated.astype(jnp.bfloat16),
        adapter_up_updated.astype(jnp.bfloat16),
    )


def solution(mesh):
    tokens = P("batch", "seq", None)
    codes = P("batch", "seq")
    return jax.shard_map(
        body,
        mesh=mesh,
        in_specs=(tokens, codes, codes) + (P(),) * 19 + (tokens,),
        out_specs=(tokens, tokens) + (P(),) * 10,
        check_vma=False,
    )
```

```python
import functools

import jax
import jax.numpy as jnp
from jax import lax
from jax.experimental import pallas as pl
from jax.experimental.pallas import tpu as pltpu
from jax.sharding import PartitionSpec as P

HEADS = 16
EXAMPLE_MAX = 1024
SEGMENT_SLOTS = 8
LANES = 128
QUERY_BLOCK = 256
TOKEN_BLOCK = 256
HIDDEN_BLOCK = 1024
AHEAD = 3
VMEM_BYTES = 60 * 1024 * 1024

norm_eps = 1e-05
adapter_scale = 8.0
learning_step_size = 3e-05
velocity_factor = 0.5
mean_decay_factor = 0.5
masked_score = -1e30
score_scale = 0.125


def matmul_rows(left_side, right_side):
    return lax.dot_general(
        left_side, right_side, (((1,), (0,)), ((), ())), preferred_element_type=jnp.float32
    )


def matmul_back(left_side, right_side):
    return lax.dot_general(
        left_side, right_side, (((1,), (1,)), ((), ())), preferred_element_type=jnp.float32
    )


def matmul_over(left_side, right_side):
    return lax.dot_general(
        left_side, right_side, (((0,), (0,)), ((), ())), preferred_element_type=jnp.float32
    )


def gather_kernel(cores, with_codes, core_ref, *refs):
    stripes, codes, out_ref = refs[:cores], refs[cores:-1], refs[-1]
    came_from = lax.rem(core_ref[0] - pl.program_id(0) + cores, cores)
    stripe, width = stripes[0].shape[1:]
    for by in range(cores):

        @pl.when(came_from == by)
        def _(by=by):
            for group in range(width // LANES):
                rows = pl.ds(group * stripe, stripe)
                out_ref[:, rows, :] = stripes[by][:, :, group * LANES : (group + 1) * LANES]
            if with_codes:
                out_ref[:, width // LANES * stripe :, :] = codes[by][...]


def gather_stripes(x, codes=None):
    cores = lax.axis_size("batch")
    core = lax.axis_index("batch")
    rows, tokens, width = x.shape
    stripe = tokens // cores
    parts, extra = [x], [] if codes is None else [codes]
    for by in range(1, cores):
        goes = lax.rem(core + by, cores)
        parts.append(from_core(lax.dynamic_slice_in_dim(x, goes * stripe, stripe, 1), by))
        extra += [] if codes is None else [from_core(codes, by)]
    deep = width // LANES * stripe + sum(c.shape[1] for c in extra[:1])
    whole = pl.BlockSpec((rows, stripe, width), lambda c, core: (0, 0, 0))
    return pl.pallas_call(
        functools.partial(gather_kernel, cores, bool(extra)),
        grid_spec=pltpu.PrefetchScalarGridSpec(
            num_scalar_prefetch=1,
            grid=(cores,),
            in_specs=[pl.BlockSpec((rows, stripe, width), lambda c, core: (0, core[0], 0))]
            + [whole] * (cores - 1)
            + [pl.BlockSpec(c.shape, lambda c, core: (0, 0, 0)) for c in extra],
            out_specs=pl.BlockSpec((rows, deep, LANES), lambda c, core: (c, 0, 0)),
        ),
        out_shape=jax.ShapeDtypeStruct((rows * cores, deep, LANES), x.dtype),
        compiler_params=pltpu.CompilerParams(vmem_limit_bytes=32 * 1024 * 1024),
        name="gather_stripes",
    )(core[None], *parts, *extra)


def spread_kernel(cores, core_ref, *refs):
    came_from = lax.rem(core_ref[0] - pl.program_id(0) + cores, cores)
    for by in range(cores):

        @pl.when(came_from == by)
        def _(by=by):
            refs[-1][...] = refs[by][...]


def spread_stripes(y):
    cores = lax.axis_size("batch")
    core = lax.axis_index("batch")
    rows, stripe, width = y.shape[0] // cores, *y.shape[1:]
    parts = [y]
    for by in range(1, cores):
        goes = lax.rem(core + by, cores)
        parts.append(from_core(lax.dynamic_slice_in_dim(y, goes * rows, rows, 0), by))
    block = (rows, stripe, width)
    return pl.pallas_call(
        functools.partial(spread_kernel, cores),
        grid_spec=pltpu.PrefetchScalarGridSpec(
            num_scalar_prefetch=1,
            grid=(cores,),
            in_specs=[pl.BlockSpec(block, lambda c, core: (core[0], 0, 0))]
            + [pl.BlockSpec(block, lambda c, core: (0, 0, 0))] * (cores - 1),
            out_specs=pl.BlockSpec(block, lambda c, core: (0, c, 0)),
        ),
        out_shape=jax.ShapeDtypeStruct((rows, stripe * cores, width), y.dtype),
        compiler_params=pltpu.CompilerParams(vmem_limit_bytes=32 * 1024 * 1024),
        name="spread_stripes",
    )(core[None], *parts)


def rows_home(y):
    return lax.all_to_all(y, "seq", 0, 0, tiled=True)


def rows_back(y):
    ring = lax.axis_size("seq")
    y = y.reshape(ring, y.shape[0] // ring, y.shape[1])
    return lax.all_to_all(y, "seq", 0, 0, tiled=True)


def tokens_of(ref, stripe, width):
    groups = []
    for group in range(width // LANES):
        rows = slice(group * stripe, (group + 1) * stripe)
        groups.append(jnp.concatenate([ref[c, rows, :] for c in range(ref.shape[0])], axis=0))
    return jnp.concatenate(groups, axis=1)


def from_core(x, by):
    cores = lax.axis_size("batch")
    return lax.ppermute(x, "batch", [(i, (i + by) % cores) for i in range(cores)])


def sum_over(x, axis, low, high):
    size = lax.axis_size(axis)
    terms = [x]
    for by in range(1, 1 << (high - low)):
        terms.append(lax.ppermute(x, axis, [(i, i ^ (by << low)) for i in range(size)]))
    while len(terms) > 1:
        terms = [terms[i] + terms[i + 1] for i in range(0, len(terms), 2)]
    return terms[0]


def lane_masks(dtype):
    lane = lax.broadcasted_iota(jnp.int32, (1, LANES), 1)
    first = (lane < LANES // 2).astype(jnp.float32).astype(dtype)
    second = (lane >= LANES // 2).astype(jnp.float32).astype(dtype)
    return first, second


def slot_row():
    lane = lax.broadcasted_iota(jnp.int32, (1, LANES), 1)
    return (lax.rem(lane, LANES // 2) < SEGMENT_SLOTS).astype(jnp.float32).astype(jnp.bfloat16)


def block_of(ref, index):
    return ref[pl.ds(index * QUERY_BLOCK, QUERY_BLOCK), :]


def attend_kernel(cores, reach, *refs):
    far_ref, query_ref = refs[:2]
    key_refs = refs[2 : 2 + cores]
    value_refs = refs[2 + cores : 2 + 2 * cores]
    mark_ref, causal_ref, out_ref, log_ref, key_heads, turned_values = refs[2 + 2 * cores :]
    slots = slot_row()
    heads = lane_masks(jnp.bfloat16)
    half = LANES // 2
    blocks = query_ref.shape[0] // QUERY_BLOCK
    tile = cores * QUERY_BLOCK
    scale = jnp.asarray(score_scale, jnp.bfloat16)
    excluded = jnp.asarray(masked_score, jnp.bfloat16)
    for h in range(2):
        turned_values[h, half:, :] = jnp.ones_like(turned_values[h, half:, :])
    for j in range(blocks):
        for k in range(cores):
            key = block_of(key_refs[k], j)
            key_mark = slots - block_of(mark_ref, k * blocks + j)
            turned = block_of(value_refs[k], j).T
            at = pl.ds(j * tile + k * QUERY_BLOCK, QUERY_BLOCK)
            for h, own in enumerate(heads):
                key_heads[h, at, :] = key * own + key_mark * heads[1 - h]
                turned_values[h, :half, at] = turned[h * half : (h + 1) * half]

    def scores_of(n, h, start):
        query_head = block_of(query_ref, n) * scale * heads[h] + block_of(mark_ref, n) * excluded * heads[1 - h]
        scores = []
        for j in range(start, n + 1):
            score = matmul_back(key_heads[h, pl.ds(j * tile, tile), :], query_head)
            scores.append(score + causal_ref[...] if j == n else score)
        return scores

    def finish(n, h, start, scores):
        rows = pl.ds(n * QUERY_BLOCK, QUERY_BLOCK)
        top = scores[0]
        for score in scores[1:]:
            top = jnp.maximum(top, score)
        top = jnp.max(top, axis=0, keepdims=True)
        weights = [jnp.exp(score - top).astype(jnp.bfloat16) for score in scores]
        keys = pl.ds(start * tile, (n + 1 - start) * tile)
        out = matmul_rows(turned_values[h, :, keys], jnp.concatenate(weights))
        total = out[half : half + 1]
        log_ref[h : h + 1, rows] = top + jnp.log(total)
        return out[:half] / total

    def every(skipped):
        waiting, outs = [], []
        units = []
        for n in range(blocks):
            start = max(0, n - reach) + (skipped and n == blocks - 1)
            units += [(n, h, start) for h in range(2)]
        for unit in units + [None] * AHEAD:
            if unit is not None:
                waiting.append((unit, scores_of(*unit)))
            if len(waiting) > AHEAD or unit is None:
                done, scores = waiting.pop(0)
                outs.append(finish(*done, scores))
                if len(outs) == 2:
                    rows = pl.ds(done[0] * QUERY_BLOCK, QUERY_BLOCK)
                    out_ref[rows, :] = jnp.concatenate(outs).T.astype(out_ref.dtype)
                    outs = []

    either_way(every, far_ref, blocks > reach)


def either_way(every, far_ref, can_skip):
    if not can_skip:
        every(False)
        return
    pl.when(far_ref[0] == 1)(functools.partial(every, False))
    pl.when(far_ref[0] != 1)(functools.partial(every, True))


def spread(wide):
    high = wide.astype(jnp.bfloat16)
    return high, (wide - high.astype(jnp.float32)).astype(jnp.bfloat16)


def pull_kernel(cores, reach, *refs):
    far_ref, query_ref, grad_ref, out_ref, log_ref = refs[:5]
    key_refs = refs[5 : 5 + cores]
    value_refs = refs[5 + cores : 5 + 2 * cores]
    mark_ref, causal_ref = refs[5 + 2 * cores : 7 + 2 * cores]
    outs = refs[7 + 2 * cores :]
    slots = slot_row()
    excluded = jnp.asarray(masked_score, jnp.bfloat16)
    grad_query_ref = outs[0]
    grad_key_refs = outs[1 : 1 + cores]
    grad_value_refs = outs[1 + cores : 1 + 2 * cores]
    (
        query_heads, key_heads, value_heads, turned_queries, turned_keys, turned_grads,
        turned_sums, dots,
    ) = outs[1 + 2 * cores :]
    heads = lane_masks(jnp.bfloat16)
    half = LANES // 2
    blocks = query_ref.shape[0] // QUERY_BLOCK
    tile = cores * QUERY_BLOCK
    scale = jnp.asarray(score_scale, jnp.bfloat16)
    lane = lax.broadcasted_iota(jnp.int32, (8, LANES), 1)
    row = lax.broadcasted_iota(jnp.int32, (8, LANES), 0)
    chooser = (lane // half == row).astype(jnp.float32).astype(jnp.bfloat16)
    for n in range(blocks):
        rows = pl.ds(n * QUERY_BLOCK, QUERY_BLOCK)
        query = query_ref[rows, :] * scale
        grad = grad_ref[rows, :]
        high, rest = spread(grad.astype(jnp.float32) * out_ref[rows, :].astype(jnp.float32))
        dots[:, rows] = matmul_back(chooser, high) + matmul_back(chooser, rest)
        turned_queries[:, rows] = query.T
        turned_grads[:, rows] = grad.T
        for h, own in enumerate(heads):
            query_heads[h, rows, :] = query * own + mark_ref[rows, :] * excluded * heads[1 - h]
        for k in range(cores):
            key = block_of(key_refs[k], n)
            key_mark = slots - block_of(mark_ref, k * blocks + n)
            value = block_of(value_refs[k], n)
            at = pl.ds(n * tile + k * QUERY_BLOCK, QUERY_BLOCK)
            turned_keys[:, at] = key.T
            for h, own in enumerate(heads):
                key_heads[h, at, :] = key * own + key_mark * heads[1 - h]
                value_heads[h, at, :] = value * own
    turned_sums[...] = jnp.zeros_like(turned_sums)

    def products(j, n, h):
        keys = pl.ds(j * tile, tile)
        rows = pl.ds(n * QUERY_BLOCK, QUERY_BLOCK)
        score = matmul_back(key_heads[h, keys, :], query_heads[h, rows, :])
        change = matmul_back(value_heads[h, keys, :], grad_ref[rows, :])
        return score, change

    def weigh(j, n, h, score, change):
        rows = pl.ds(n * QUERY_BLOCK, QUERY_BLOCK)
        if n == j:
            score = score + causal_ref[...]
        weight = jnp.exp(score - log_ref[h : h + 1, rows])
        change = (weight * (change - dots[h : h + 1, rows])).astype(jnp.bfloat16)
        return weight.astype(jnp.bfloat16), change

    def finish(j, h, members):
        part = pl.ds(h * half, half)
        keys = pl.ds(j * tile, tile)
        rows = pl.ds(members[0][0] * QUERY_BLOCK, len(members) * QUERY_BLOCK)
        weights = jnp.concatenate([m[1] for m in members], axis=1)
        changes = jnp.concatenate([m[2] for m in members], axis=1)
        turned_sums[part, rows] += matmul_rows(turned_keys[part, keys], changes)
        return (
            matmul_back(turned_queries[part, rows], changes),
            matmul_back(turned_grads[part, rows], weights),
        )

    def every(skipped):
        units = []
        for j in range(blocks):
            last = min(blocks - 1, j + reach)
            if skipped and j + reach == blocks - 1:
                last -= 1
            units += [(j, n, h, n == last) for h in range(2) for n in range(j, last + 1)]
        waiting, members, sums = [], [], []
        for unit in units + [None] * AHEAD:
            if unit is not None:
                waiting.append((unit, products(*unit[:3])))
            if len(waiting) > AHEAD or unit is None:
                (j, n, h, closing), pair = waiting.pop(0)
                members.append((n, *weigh(j, n, h, *pair)))
                if closing:
                    sums.append(finish(j, h, members))
                    members = []
                if len(sums) == 2:
                    for out_refs, which in ((grad_key_refs, 0), (grad_value_refs, 1)):
                        both = jnp.concatenate([s[which] for s in sums]).T.astype(jnp.bfloat16)
                        for k in range(cores):
                            out_refs[k][pl.ds(j * QUERY_BLOCK, QUERY_BLOCK), :] = both[
                                k * QUERY_BLOCK : (k + 1) * QUERY_BLOCK
                            ]
                    sums = []

    either_way(every, far_ref, blocks > reach)
    grad_query_ref[...] = (turned_sums[...] * score_scale).T.astype(jnp.bfloat16)


def standardized(values):
    average = jnp.mean(values, axis=-1, keepdims=True)
    centred = values - average
    spread_inverse = lax.rsqrt(jnp.mean(centred * centred, axis=-1, keepdims=True) + norm_eps)
    return centred * spread_inverse, spread_inverse


def norm_pull(grad, shaped, spread_inverse):
    mean_grad = jnp.mean(grad, axis=-1, keepdims=True)
    mean_product = jnp.mean(grad * shaped, axis=-1, keepdims=True)
    return spread_inverse * (grad - mean_grad - shaped * mean_product)


def enter_kernel(
    stripe, kinds, x_ref, gain_ref, shift_ref, bias_ref, down_ref, up_ref, *refs
):
    weight_refs, out_refs = refs[: len(kinds)], refs[len(kinds) :]
    width = out_refs[0].shape[1]
    shaped, _ = standardized(tokens_of(x_ref, stripe, width).astype(jnp.float32))
    normed = (shaped * gain_ref[...] + shift_ref[...]).astype(jnp.bfloat16)
    lora = matmul_rows(normed, down_ref[...]).astype(jnp.bfloat16)
    if len(out_refs) > len(kinds):
        out_refs[-1][...] = lora
    for kind, weight_ref, out_ref in zip(kinds, weight_refs, out_refs):
        out = matmul_rows(normed, weight_ref[...])
        if kind != 1:
            j = kind // 2
            out = out + matmul_rows(lora, up_ref[:, j * width : (j + 1) * width])
            out = out + bias_ref[j : j + 1, :]
        out_ref[...] = out.astype(jnp.bfloat16)


root_two_over_pi = 0.7978845608028654
cubic = 0.044715


def middle_kernel(
    stripe, x_ref, attended_ref, cotangent_ref,
    out_bias_ref, gain_ref, shift_ref, expand_bias_ref, contract_bias_ref,
    out_weight_from, expand_from, contract_from,
    result_ref, grad_middle_ref, grad_attended_ref,
    out_weight_ref, expand_ref, contract_ref, arrivals,
):
    width, hidden = expand_ref.shape
    parts = [slice(at, at + HIDDEN_BLOCK) for at in range(0, hidden, HIDDEN_BLOCK)]
    copies = [pltpu.make_async_copy(out_weight_from, out_weight_ref, arrivals.at[0])]
    for i, part in enumerate(parts):
        for which, source, to in (
            (1, expand_from.at[:, part], expand_ref.at[:, part]),
            (2, contract_from.at[part, :], contract_ref.at[part, :]),
        ):
            copies.append(pltpu.make_async_copy(source, to, arrivals.at[2 * i + which]))

    def block(first):
        if first:
            for copy in copies:
                copy.start()
            copies[0].wait()
        middle = (
            tokens_of(x_ref, stripe, width).astype(jnp.float32)
            + matmul_rows(attended_ref[...], out_weight_ref[...])
            + out_bias_ref[...]
        )
        shaped, spread_inverse = standardized(middle)
        normed = (shaped * gain_ref[...] + shift_ref[...]).astype(jnp.bfloat16)
        grad_low = tokens_of(cotangent_ref, stripe, width)
        grad_out = grad_low.astype(jnp.float32)
        result = middle + contract_bias_ref[...]
        grad_normed = jnp.zeros_like(middle)
        for i, part in enumerate(parts):
            if first:
                copies[2 * i + 1].wait()
                copies[2 * i + 2].wait()
            pre = matmul_rows(normed, expand_ref[:, part]) + expand_bias_ref[:, part]
            grad_act = matmul_back(grad_low, contract_ref[part, :])
            square = pre * pre
            bent = jnp.tanh(root_two_over_pi * pre * (1.0 + cubic * square))
            upper = 0.5 + 0.5 * bent
            act = (pre * upper).astype(jnp.bfloat16)
            slope = upper + (0.5 * root_two_over_pi) * pre * (1.0 - bent * bent) * (
                1.0 + (3.0 * cubic) * square
            )
            grad_pre = (grad_act * slope).astype(jnp.bfloat16)
            result = result + matmul_rows(act, contract_ref[part, :])
            grad_normed = grad_normed + matmul_back(grad_pre, expand_ref[:, part])
        result_ref[...] = result.astype(jnp.bfloat16)
        grad_middle = grad_out + norm_pull(grad_normed * gain_ref[...], shaped, spread_inverse)
        grad_middle_low = grad_middle.astype(jnp.bfloat16)
        grad_middle_ref[...] = grad_middle_low
        grad_attended = matmul_back(grad_middle_low, out_weight_ref[...])
        grad_attended_ref[...] = grad_attended.astype(jnp.bfloat16)

    pl.when(pl.program_id(0) == 0)(functools.partial(block, True))
    pl.when(pl.program_id(0) != 0)(functools.partial(block, False))


def total(parts):
    out = parts[0][...].astype(jnp.float32)
    for part in parts[1:]:
        out = out + part[...].astype(jnp.float32)
    return out.astype(jnp.bfloat16)


def adapt_kernel(
    stripe, cores, x_ref, gain_ref, shift_ref, up_ref, lora_ref, grad_query_ref, *refs
):
    value_refs = refs[:cores]
    grad_lora_ref, down_sum_ref, up_sum_ref = refs[cores:]
    slots = down_sum_ref.shape[0]

    @pl.when(pl.program_id(0) == 0)
    def _():
        down_sum_ref[...] = jnp.zeros_like(down_sum_ref)
        up_sum_ref[...] = jnp.zeros_like(up_sum_ref)

    width = grad_query_ref.shape[1]
    grad_query = grad_query_ref[...]
    grad_value = total(value_refs)
    shaped, _ = standardized(tokens_of(x_ref, stripe, width).astype(jnp.float32))
    normed = (shaped * gain_ref[...] + shift_ref[...]).astype(jnp.bfloat16)
    grad_lora = matmul_back(grad_query, up_ref[:, :width]) + matmul_back(
        grad_value, up_ref[:, width:]
    )
    grad_lora = grad_lora.astype(jnp.bfloat16)
    grad_lora_ref[...] = grad_lora
    lora = lora_ref[...]
    down_sum_ref[...] += matmul_over(grad_lora, normed)[:slots]
    up_sum_ref[:, :width] += matmul_over(lora, grad_query)[:slots]
    up_sum_ref[:, width:] += matmul_over(lora, grad_value)[:slots]


def leave_kernel(
    stripe, cores, x_ref, gain_ref, weight_ref, down_ref, grad_lora_ref, grad_middle_ref,
    grad_query_ref, *refs,
):
    key_refs, value_refs, grad_ref = refs[:cores], refs[cores : 2 * cores], refs[-1]
    width = grad_query_ref.shape[1]
    shaped, spread_inverse = standardized(tokens_of(x_ref, stripe, width).astype(jnp.float32))
    grad_normed = (
        matmul_back(grad_query_ref[...], weight_ref[:, :width])
        + matmul_back(total(key_refs), weight_ref[:, width : 2 * width])
        + matmul_back(total(value_refs), weight_ref[:, 2 * width :])
        + matmul_back(grad_lora_ref[...], down_ref[...])
    )
    grad = norm_pull(grad_normed * gain_ref[...], shaped, spread_inverse)
    grad_ref[...] = (grad_middle_ref[...].astype(jnp.float32) + grad).astype(jnp.bfloat16)


def tile(x):
    def spec(tokens):
        share = x.shape[0] * min(TOKEN_BLOCK, tokens) // tokens
        return pl.BlockSpec((share, *x.shape[1:]), lambda i: (i,) + (0,) * (len(x.shape) - 1))

    return x, spec


def whole(x):
    def spec(tokens):
        kept = pl.Buffered(1)
        return pl.BlockSpec(x.shape, lambda i: (0,) * len(x.shape), pipeline_mode=kept)

    return x, spec


def columns(x, which, width):
    def spec(tokens):
        kept = pl.Buffered(1)
        return pl.BlockSpec((x.shape[0], width), lambda i: (0, which), pipeline_mode=kept)

    return x, spec


def in_place(x):
    return x, lambda tokens: pl.BlockSpec(memory_space=pl.ANY)


def over_tokens(kernel, name, tokens, operands, outs, sums, flops, scratch=()):
    moved = sum(x.size * x.dtype.itemsize for x in [*(x for x, _ in operands), *outs, *sums])
    return pl.pallas_call(
        kernel,
        grid=(tokens // min(TOKEN_BLOCK, tokens),),
        in_specs=[spec(tokens) for _, spec in operands],
        out_specs=[tile(x)[1](tokens) for x in outs]
        + [pl.BlockSpec(x.shape, lambda i: (0, 0)) for x in sums],
        out_shape=[*outs, *sums],
        scratch_shapes=list(scratch),
        compiler_params=pltpu.CompilerParams(
            dimension_semantics=("arbitrary",), vmem_limit_bytes=VMEM_BYTES
        ),
        cost_estimate=pl.CostEstimate(flops=flops, bytes_accessed=moved, transcendentals=0),
        name=name,
    )(*(x for x, _ in operands))


def attention_calls(tokens, width, cores, reach):
    pair = pl.BlockSpec((tokens, LANES), lambda p, far: (0, p))
    marks = pl.BlockSpec((cores * tokens, LANES), lambda p, far: (0, 0))
    causal = pl.BlockSpec((cores * QUERY_BLOCK, QUERY_BLOCK), lambda p, far: (0, 0))
    logs = pl.BlockSpec((8, tokens), lambda p, far: (p, 0))
    grid = (width // LANES,)
    blocks = tokens // QUERY_BLOCK
    pairs = sum(min(n, reach) + 1 for n in range(blocks)) * cores * QUERY_BLOCK**2 * HEADS
    head_width = width // HEADS
    low = jax.ShapeDtypeStruct((tokens, width), jnp.bfloat16)
    log_rows = jax.ShapeDtypeStruct((8 * grid[0], tokens), jnp.float32)
    params = pltpu.CompilerParams(
        dimension_semantics=("arbitrary",), vmem_limit_bytes=VMEM_BYTES
    )
    low_scratch = functools.partial(pltpu.VMEM, dtype=jnp.bfloat16)
    forward = pl.pallas_call(
        functools.partial(attend_kernel, cores, reach),
        grid_spec=pltpu.PrefetchScalarGridSpec(
            num_scalar_prefetch=1,
            grid=grid,
            in_specs=[pair] * (1 + 2 * cores) + [marks, causal],
            out_specs=[pair, logs],
            scratch_shapes=[
                low_scratch((2, cores * tokens, LANES)),
                low_scratch((2, LANES // 2 + 16, cores * tokens)),
            ],
        ),
        out_shape=[low, log_rows],
        compiler_params=params,
        cost_estimate=pl.CostEstimate(
            flops=4 * pairs * head_width,
            bytes_accessed=2 * tokens * width * (2 + 2 * cores),
            transcendentals=pairs,
        ),
        name="attend",
    )
    backward = pl.pallas_call(
        functools.partial(pull_kernel, cores, reach),
        grid_spec=pltpu.PrefetchScalarGridSpec(
            num_scalar_prefetch=1,
            grid=grid,
            in_specs=[pair, pair, pair, logs] + [pair] * (2 * cores) + [marks, causal],
            out_specs=[pair] * (1 + 2 * cores),
            scratch_shapes=[
                low_scratch((2, tokens, LANES)),
                low_scratch((2, cores * tokens, LANES)),
                low_scratch((2, cores * tokens, LANES)),
                low_scratch((LANES, tokens)),
                low_scratch((LANES, cores * tokens)),
                low_scratch((LANES, tokens)),
                pltpu.VMEM((LANES, tokens), jnp.float32),
                pltpu.VMEM((8, tokens), jnp.float32),
            ],
        ),
        out_shape=[low] * (1 + 2 * cores),
        compiler_params=params,
        cost_estimate=pl.CostEstimate(
            flops=10 * pairs * head_width,
            bytes_accessed=2 * tokens * width * (4 + 4 * cores),
            transcendentals=pairs,
        ),
        name="pull",
    )
    return forward, backward


def body(
    inputs,
    segments,
    groups,
    group_loss_weight,
    attention_norm_gain,
    attention_norm_bias,
    query_key_value_weight,
    query_value_bias,
    attention_out_weight,
    attention_out_bias,
    feedforward_norm_gain,
    feedforward_norm_bias,
    expand_weight,
    expand_bias,
    contract_weight,
    contract_bias,
    adapter_down_maps,
    adapter_up_maps,
    down_velocity,
    up_velocity,
    running_down_mean,
    running_up_mean,
    cotangent,
):
    rows_here, tokens_here, width = inputs.shape
    cores = lax.axis_size("batch")
    ring = lax.axis_size("seq")
    assert rows_here * cores == ring
    stripe = tokens_here // cores
    tokens = ring * stripe
    span = QUERY_BLOCK * cores
    reach = -(-(EXAMPLE_MAX - 1) // span)
    rank = adapter_down_maps.shape[-1]
    core = lax.axis_index("batch")
    attend, pull = attention_calls(tokens, width, cores, reach)

    assert tokens_here == LANES
    marks = jnp.broadcast_to(segments[:, None, :], (rows_here, 8, tokens_here))
    x = rows_home(gather_stripes(inputs, marks.astype(jnp.bfloat16)))
    chooser = groups[..., None] == jnp.arange(group_loss_weight.shape[0], dtype=jnp.int32)
    token_weight = jnp.sum(jnp.where(chooser, group_loss_weight, 0.0), axis=-1, keepdims=True)
    weighted = (cotangent.astype(jnp.float32) * token_weight).astype(jnp.bfloat16)
    stripes = gather_stripes(weighted)
    place = jnp.arange(QUERY_BLOCK, dtype=jnp.int32)
    place = tokens_here * (place // stripe) + place % stripe
    after = []
    for by in range(cores):
        key_place = place + stripe * lax.rem(core - by + cores, cores)
        after.append(key_place[:, None] > (place + stripe * core)[None, :])
    causal = jnp.where(jnp.concatenate(after), masked_score, 0.0).astype(jnp.float32)

    def row_of(vector):
        return vector.astype(jnp.float32).reshape(1, -1)

    first_gain, first_shift = row_of(attention_norm_gain), row_of(attention_norm_bias)
    second_gain, second_shift = row_of(feedforward_norm_gain), row_of(feedforward_norm_bias)
    pad = LANES - 2 * rank
    down_packed = jnp.concatenate([adapter_down_maps[0], adapter_down_maps[1]], axis=1)
    down_packed = jnp.pad(down_packed, ((0, 0), (0, pad))).astype(jnp.bfloat16)
    up_packed = jnp.concatenate(
        [
            jnp.pad(adapter_up_maps[0], ((0, rank + pad), (0, 0))),
            jnp.pad(adapter_up_maps[1], ((rank, pad), (0, 0))),
        ],
        axis=1,
    )
    up_packed = (adapter_scale * up_packed).astype(jnp.bfloat16)
    value_bias = query_value_bias.astype(jnp.float32)
    out_bias, up_bias, down_bias = map(row_of, (attention_out_bias, expand_bias, contract_bias))
    (
        x, stripes, causal, first_gain, first_shift, second_gain, second_shift,
        value_bias, out_bias, up_bias, down_bias, down_packed, up_packed,
    ) = lax.optimization_barrier(
        (
            x, stripes, causal, first_gain, first_shift, second_gain, second_shift,
            value_bias, out_bias, up_bias, down_bias, down_packed, up_packed,
        )
    )
    cotangent_home = rows_home(stripes)
    row_segments = x[:, width // LANES * stripe, :].astype(jnp.int32)
    parts = row_segments.reshape(ring, cores, stripe)
    turns = [lax.rem(core - by + cores, cores) for by in range(cores)]
    parts = [lax.dynamic_index_in_dim(parts, turn, 1, keepdims=False) for turn in turns]
    slot = jnp.arange(LANES, dtype=jnp.int32) % (LANES // 2)
    marks = jnp.concatenate(parts).reshape(cores * tokens, 1) == slot[None, :]
    marks = marks.astype(jnp.bfloat16)
    row_segments = row_segments.reshape(ring * tokens_here)
    blocks = tokens // QUERY_BLOCK
    last = max(0, blocks - 1 - reach)
    far = row_segments[span * (last + 1) - 1] >= row_segments[span * (blocks - 1)]
    far = far.astype(jnp.int32)[None]

    low = jax.ShapeDtypeStruct((tokens, width), jnp.bfloat16)

    def enter(kinds, extra):
        return over_tokens(
            functools.partial(enter_kernel, stripe, kinds),
            "enter",
            tokens,
            [tile(x), whole(first_gain), whole(first_shift), whole(value_bias)]
            + [whole(down_packed), whole(up_packed)]
            + [columns(query_key_value_weight, kind, width) for kind in kinds],
            [low] * len(kinds) + extra,
            [],
            2 * len(kinds) * tokens * width * width,
        )

    keys, values = enter((1, 2), [])
    all_keys = [keys] + [from_core(keys, by) for by in range(1, cores)]
    all_values = [values] + [from_core(values, by) for by in range(1, cores)]
    queries, lora = enter((0,), [jax.ShapeDtypeStruct((tokens, LANES), jnp.bfloat16)])
    attended, log_total = attend(far, queries, *all_keys, *all_values, marks, causal)

    hidden = expand_weight.shape[1]
    layer_result, grad_middle, grad_attended = over_tokens(
        functools.partial(middle_kernel, stripe),
        "middle",
        tokens,
        [tile(x), tile(attended), tile(cotangent_home)]
        + [whole(v) for v in (out_bias, second_gain, second_shift, up_bias, down_bias)]
        + [in_place(w) for w in (attention_out_weight, expand_weight, contract_weight)],
        [low, low, low],
        [],
        4 * tokens * width * (width + 2 * hidden),
        [pltpu.VMEM(w.shape, w.dtype) for w in (attention_out_weight, expand_weight, contract_weight)]
        + [pltpu.SemaphoreType.DMA((1 + 2 * (hidden // HIDDEN_BLOCK),))],
    )
    layer_out = rows_back(layer_result)

    pulled = pull(
        far,
        queries,
        grad_attended,
        attended,
        log_total,
        *all_keys,
        *all_values,
        marks,
        causal,
    )

    layer_out, pulled = lax.optimization_barrier((layer_out, pulled))
    layer_out = spread_stripes(layer_out)

    def owned(parts):
        return [parts[0]] + [from_core(parts[by], -by) for by in range(1, cores)]

    sums = [
        jax.ShapeDtypeStruct((2 * rank, width), jnp.float32),
        jax.ShapeDtypeStruct((2 * rank, 2 * width), jnp.float32),
    ]
    owned_values = owned(pulled[1 + cores :])
    owned_keys = owned(pulled[1 : 1 + cores])
    grad_lora, down_sum, up_sum = over_tokens(
        functools.partial(adapt_kernel, stripe, cores),
        "adapt",
        tokens,
        [tile(x), whole(first_gain), whole(first_shift), whole(up_packed), tile(lora)]
        + [tile(part) for part in (pulled[0], *owned_values)],
        [jax.ShapeDtypeStruct((tokens, LANES), jnp.bfloat16)],
        sums,
        1024 * tokens * width,
    )
    up_parts = [
        adapter_scale * up_sum[j * rank : (j + 1) * rank, j * width : (j + 1) * width]
        for j in range(2)
    ]
    adapter_sums = jnp.concatenate([*up_parts, down_sum], axis=0)
    bits = ring.bit_length() - 1
    adapter_sums = sum_over(adapter_sums, "seq", max(0, bits - 2), bits)
    (input_grad,) = over_tokens(
        functools.partial(leave_kernel, stripe, cores),
        "leave",
        tokens,
        [tile(x), whole(first_gain), whole(query_key_value_weight), whole(down_packed)]
        + [tile(part) for part in (grad_lora, grad_middle, pulled[0], *owned_keys, *owned_values)],
        [low],
        [],
        6 * tokens * width * width,
    )
    input_grad, adapter_sums = lax.optimization_barrier((input_grad, adapter_sums))
    input_grad = spread_stripes(rows_back(input_grad))
    for low in range(max(0, bits - 4), -1, -2) if bits > 2 else ():
        adapter_sums = sum_over(adapter_sums, "seq", low, min(low + 2, bits - 2))
    adapter_sums = sum_over(adapter_sums, "batch", 0, cores.bit_length() - 1)
    adapter_sums = adapter_sums.reshape(2, 2, rank, width)
    up_map_gradient = adapter_sums[0]
    down_map_gradient = jnp.transpose(adapter_sums[1], (0, 2, 1))

    down_velocity_next = velocity_factor * down_velocity + down_map_gradient
    up_velocity_next = velocity_factor * up_velocity + up_map_gradient
    adapter_down_updated = adapter_down_maps - learning_step_size * (
        down_map_gradient + velocity_factor * down_velocity_next
    )
    adapter_up_updated = adapter_up_maps - learning_step_size * (
        up_map_gradient + velocity_factor * up_velocity_next
    )
    updated_down_mean = (
        mean_decay_factor * running_down_mean + (1.0 - mean_decay_factor) * adapter_down_updated
    )
    updated_up_mean = (
        mean_decay_factor * running_up_mean + (1.0 - mean_decay_factor) * adapter_up_updated
    )
    return (
        layer_out,
        input_grad,
        down_map_gradient,
        up_map_gradient,
        adapter_down_updated,
        adapter_up_updated,
        down_velocity_next,
        up_velocity_next,
        updated_down_mean,
        updated_up_mean,
        adapter_down_updated.astype(jnp.bfloat16),
        adapter_up_updated.astype(jnp.bfloat16),
    )


def solution(mesh):
    tokens = P("batch", "seq", None)
    codes = P("batch", "seq")
    return jax.shard_map(
        body,
        mesh=mesh,
        in_specs=(tokens, codes, codes) + (P(),) * 19 + (tokens,),
        out_specs=(tokens, tokens) + (P(),) * 10,
        check_vma=False,
    )
```

```python
import functools

import jax
import jax.numpy as jnp
from jax import lax
from jax.experimental import pallas as pl
from jax.experimental.pallas import tpu as pltpu
from jax.sharding import PartitionSpec as P

HEADS = 16
EXAMPLE_MAX = 1024
SEGMENT_SLOTS = 8
LANES = 128
QUERY_BLOCK = 256
TOKEN_BLOCK = 256
HIDDEN_BLOCK = 1024
AHEAD = 2
PER = 2
SCORES_AHEAD = 2
DELAY = 0
VMEM_BYTES = 63 * 1024 * 1024

norm_eps = 1e-05
adapter_scale = 8.0
learning_step_size = 3e-05
velocity_factor = 0.5
mean_decay_factor = 0.5
masked_score = -1e30
score_scale = 0.125


def matmul_rows(left_side, right_side):
    return lax.dot_general(
        left_side, right_side, (((1,), (0,)), ((), ())), preferred_element_type=jnp.float32
    )


def matmul_back(left_side, right_side):
    return lax.dot_general(
        left_side, right_side, (((1,), (1,)), ((), ())), preferred_element_type=jnp.float32
    )


def matmul_over(left_side, right_side):
    return lax.dot_general(
        left_side, right_side, (((0,), (0,)), ((), ())), preferred_element_type=jnp.float32
    )


def gather_kernel(cores, with_codes, core_ref, *refs):
    stripes, codes, out_ref = refs[:cores], refs[cores:-1], refs[-1]
    came_from = lax.rem(core_ref[0] - pl.program_id(0) + cores, cores)
    stripe, width = stripes[0].shape[1:]
    for by in range(cores):

        @pl.when(came_from == by)
        def _(by=by):
            for group in range(width // LANES):
                rows = pl.ds(group * stripe, stripe)
                out_ref[:, rows, :] = stripes[by][:, :, group * LANES : (group + 1) * LANES]
            if with_codes:
                out_ref[:, width // LANES * stripe :, :] = codes[by][...]


def gather_stripes(x, codes=None):
    cores = lax.axis_size("batch")
    core = lax.axis_index("batch")
    rows, tokens, width = x.shape
    stripe = tokens // cores
    parts, extra = [x], [] if codes is None else [codes]
    for by in range(1, cores):
        goes = lax.rem(core + by, cores)
        parts.append(from_core(lax.dynamic_slice_in_dim(x, goes * stripe, stripe, 1), by))
        extra += [] if codes is None else [from_core(codes, by)]
    deep = width // LANES * stripe + sum(c.shape[1] for c in extra[:1])
    whole = pl.BlockSpec((rows, stripe, width), lambda c, core: (0, 0, 0))
    return pl.pallas_call(
        functools.partial(gather_kernel, cores, bool(extra)),
        grid_spec=pltpu.PrefetchScalarGridSpec(
            num_scalar_prefetch=1,
            grid=(cores,),
            in_specs=[pl.BlockSpec((rows, stripe, width), lambda c, core: (0, core[0], 0))]
            + [whole] * (cores - 1)
            + [pl.BlockSpec(c.shape, lambda c, core: (0, 0, 0)) for c in extra],
            out_specs=pl.BlockSpec((rows, deep, LANES), lambda c, core: (c, 0, 0)),
        ),
        out_shape=jax.ShapeDtypeStruct((rows * cores, deep, LANES), x.dtype),
        compiler_params=pltpu.CompilerParams(vmem_limit_bytes=32 * 1024 * 1024),
        name="gather_stripes",
    )(core[None], *parts, *extra)


def spread_kernel(cores, core_ref, *refs):
    came_from = lax.rem(core_ref[0] - pl.program_id(0) + cores, cores)
    for by in range(cores):

        @pl.when(came_from == by)
        def _(by=by):
            refs[-1][...] = refs[by][...]


def spread_stripes(y):
    cores = lax.axis_size("batch")
    core = lax.axis_index("batch")
    rows, stripe, width = y.shape[0] // cores, *y.shape[1:]
    parts = [y]
    for by in range(1, cores):
        goes = lax.rem(core + by, cores)
        parts.append(from_core(lax.dynamic_slice_in_dim(y, goes * rows, rows, 0), by))
    block = (rows, stripe, width)
    return pl.pallas_call(
        functools.partial(spread_kernel, cores),
        grid_spec=pltpu.PrefetchScalarGridSpec(
            num_scalar_prefetch=1,
            grid=(cores,),
            in_specs=[pl.BlockSpec(block, lambda c, core: (core[0], 0, 0))]
            + [pl.BlockSpec(block, lambda c, core: (0, 0, 0))] * (cores - 1),
            out_specs=pl.BlockSpec(block, lambda c, core: (0, c, 0)),
        ),
        out_shape=jax.ShapeDtypeStruct((rows, stripe * cores, width), y.dtype),
        compiler_params=pltpu.CompilerParams(vmem_limit_bytes=32 * 1024 * 1024),
        name="spread_stripes",
    )(core[None], *parts)


def rows_home(y):
    return lax.all_to_all(y, "seq", 0, 0, tiled=True)


def rows_back(y):
    ring = lax.axis_size("seq")
    y = y.reshape(ring, y.shape[0] // ring, y.shape[1])
    return lax.all_to_all(y, "seq", 0, 0, tiled=True)


def tokens_of(ref, stripe, width):
    groups = []
    for group in range(width // LANES):
        rows = slice(group * stripe, (group + 1) * stripe)
        groups.append(jnp.concatenate([ref[c, rows, :] for c in range(ref.shape[0])], axis=0))
    return jnp.concatenate(groups, axis=1)


def from_core(x, by):
    cores = lax.axis_size("batch")
    return lax.ppermute(x, "batch", [(i, (i + by) % cores) for i in range(cores)])


def paired_sum(terms):
    while len(terms) > 1:
        terms = [terms[i] + terms[i + 1] for i in range(0, len(terms), 2)]
    return terms[0]


def sum_everywhere(x):
    ring, cores = lax.axis_size("seq"), lax.axis_size("batch")
    assert ring & (ring - 1) == 0 and cores & (cores - 1) == 0

    def exchanged(x, axis, size, by):
        return lax.ppermute(x, axis, [(i, i ^ by) for i in range(size)])

    step = 1
    while step < cores:
        x = x + exchanged(x, "batch", cores, step)
        step *= 2
    near = min(4, ring)
    share = x.shape[0] // near
    me = lax.rem(lax.axis_index("seq"), near)

    def shares_of(x, which):
        return lax.dynamic_slice_in_dim(x, which * share, share, 0)

    terms = [shares_of(x, me)]
    for by in range(1, near):
        terms.append(exchanged(shares_of(x, me ^ by), "seq", ring, by))
    mine = paired_sum(terms)
    step = near
    while step < ring:
        width = min(4, ring // step)
        mine = paired_sum(
            [mine] + [exchanged(mine, "seq", ring, by * step) for by in range(1, width)]
        )
        step *= width
    held = [mine] + [exchanged(mine, "seq", ring, by) for by in range(1, near)]
    held = jnp.concatenate(held)
    return jnp.concatenate([shares_of(held, me ^ at) for at in range(near)])


def lane_masks(dtype):
    lane = lax.broadcasted_iota(jnp.int32, (1, LANES), 1)
    first = (lane < LANES // 2).astype(jnp.float32).astype(dtype)
    second = (lane >= LANES // 2).astype(jnp.float32).astype(dtype)
    return first, second


def slot_row():
    lane = lax.broadcasted_iota(jnp.int32, (1, LANES), 1)
    return (lax.rem(lane, LANES // 2) < SEGMENT_SLOTS).astype(jnp.float32).astype(jnp.bfloat16)


def block_of(ref, index):
    return ref[pl.ds(index * QUERY_BLOCK, QUERY_BLOCK), :]


def attend_block(cores, reach, skipped, *refs):
    far_ref, query_ref = refs[:2]
    key_refs = refs[2 : 2 + cores]
    value_refs = refs[2 + cores : 2 + 2 * cores]
    mark_ref, causal_ref, out_ref, log_ref, key_heads, turned_values = refs[2 + 2 * cores :]
    slots = slot_row()
    heads = lane_masks(jnp.bfloat16)
    half = LANES // 2
    blocks = query_ref.shape[0] // QUERY_BLOCK
    tile = cores * QUERY_BLOCK
    scale = jnp.asarray(score_scale, jnp.bfloat16)
    excluded = jnp.asarray(masked_score, jnp.bfloat16)
    for h in range(2):
        turned_values[h, half:, :] = jnp.ones_like(turned_values[h, half:, :])
    for j in range(blocks):
        for k in range(cores):
            key = block_of(key_refs[k], j)
            key_mark = slots - block_of(mark_ref, k * blocks + j)
            turned = block_of(value_refs[k], j).T
            at = pl.ds(j * tile + k * QUERY_BLOCK, QUERY_BLOCK)
            for h, own in enumerate(heads):
                key_heads[h, at, :] = key * own + key_mark * heads[1 - h]
                turned_values[h, :half, at] = turned[h * half : (h + 1) * half]

    def scores_of(n, h, start):
        query_head = block_of(query_ref, n) * scale * heads[h] + block_of(mark_ref, n) * excluded * heads[1 - h]
        scores = []
        for j in range(start, n + 1):
            score = matmul_back(key_heads[h, pl.ds(j * tile, tile), :], query_head)
            scores.append(score + causal_ref[...] if j == n else score)
        return scores

    def soften(scores):
        top = scores[0]
        for score in scores[1:]:
            top = jnp.maximum(top, score)
        top = jnp.max(top, axis=0, keepdims=True)
        return top, [jnp.exp(score - top).astype(jnp.bfloat16) for score in scores]

    def finish(n, h, start, top, weights, outs):
        rows = pl.ds(n * QUERY_BLOCK, QUERY_BLOCK)
        keys = pl.ds(start * tile, (n + 1 - start) * tile)
        out = matmul_rows(turned_values[h, :, keys], jnp.concatenate(weights))
        total = out[half : half + 1]
        log_ref[h : h + 1, rows] = top + jnp.log(total)
        outs.append(out[:half] / total)
        if h:
            out_ref[rows, :] = jnp.concatenate(outs[-2:]).T.astype(out_ref.dtype)

    def every(skipped):
        waiting, left, outs = [], [], []
        units = []
        for n in range(blocks):
            start = max(0, n - reach) + (skipped and n == blocks - 1)
            units += [(n, h, start) for h in range(2)]
        for unit in units + [None] * SCORES_AHEAD:
            if unit is not None:
                waiting.append((unit, scores_of(*unit)))
            if len(waiting) > SCORES_AHEAD or unit is None:
                done, scores = waiting.pop(0)
                left.append((*done, *soften(scores)))
                if len(left) > DELAY:
                    finish(*left.pop(0), outs)
        for one in left:
            finish(*one, outs)

    every(skipped)


def either_way(block, cores, reach, *refs):
    far_ref, query_ref = refs[:2]
    if query_ref.shape[0] // QUERY_BLOCK <= reach:
        block(cores, reach, False, *refs)
        return
    pl.when(far_ref[0] == 1)(functools.partial(block, cores, reach, False, *refs))
    pl.when(far_ref[0] != 1)(functools.partial(block, cores, reach, True, *refs))


def spread(wide):
    high = wide.astype(jnp.bfloat16)
    return high, (wide - high.astype(jnp.float32)).astype(jnp.bfloat16)


def pull_block(cores, reach, skipped, *refs):
    far_ref, query_ref, grad_ref, out_ref, log_ref = refs[:5]
    key_refs = refs[5 : 5 + cores]
    value_refs = refs[5 + cores : 5 + 2 * cores]
    mark_ref, causal_ref = refs[5 + 2 * cores : 7 + 2 * cores]
    outs = refs[7 + 2 * cores :]
    slots = slot_row()
    excluded = jnp.asarray(masked_score, jnp.bfloat16)
    grad_query_ref = outs[0]
    grad_key_refs = outs[1 : 1 + cores]
    grad_value_refs = outs[1 + cores : 1 + 2 * cores]
    (
        query_marked, query_heads, key_heads, all_values, grad_heads, turned_keys, turned_sums,
        dots,
    ) = outs[1 + 2 * cores :]
    heads = lane_masks(jnp.bfloat16)
    half = LANES // 2
    blocks = query_ref.shape[0] // QUERY_BLOCK
    tile = cores * QUERY_BLOCK
    scale = jnp.asarray(score_scale, jnp.bfloat16)
    lane = lax.broadcasted_iota(jnp.int32, (8, LANES), 1)
    row = lax.broadcasted_iota(jnp.int32, (8, LANES), 0)
    chooser = (lane // half == row).astype(jnp.float32).astype(jnp.bfloat16)
    for n in range(blocks):
        rows = pl.ds(n * QUERY_BLOCK, QUERY_BLOCK)
        query = query_ref[rows, :] * scale
        grad = grad_ref[rows, :]
        high, rest = spread(grad.astype(jnp.float32) * out_ref[rows, :].astype(jnp.float32))
        dots[:, rows] = matmul_back(chooser, high) + matmul_back(chooser, rest)
        for h, own in enumerate(heads):
            mine = query * own
            query_heads[h, rows, :] = mine
            query_marked[h, rows, :] = mine + mark_ref[rows, :] * excluded * heads[1 - h]
            grad_heads[h, rows, :] = grad * own
        for k in range(cores):
            key = block_of(key_refs[k], n)
            key_mark = slots - block_of(mark_ref, k * blocks + n)
            at = pl.ds(n * tile + k * QUERY_BLOCK, QUERY_BLOCK)
            turned_keys[:, at] = key.T
            all_values[at, :] = block_of(value_refs[k], n)
            for h, own in enumerate(heads):
                key_heads[h, at, :] = key * own + key_mark * heads[1 - h]
    turned_sums[...] = jnp.zeros_like(turned_sums)

    def products(j, n, h):
        keys = pl.ds(j * tile, tile)
        rows = pl.ds(n * QUERY_BLOCK, QUERY_BLOCK)
        score = matmul_back(key_heads[h, keys, :], query_marked[h, rows, :])
        change = matmul_back(all_values[keys, :], grad_heads[h, rows, :])
        return score, change

    def weigh(j, n, h, score, change):
        rows = pl.ds(n * QUERY_BLOCK, QUERY_BLOCK)
        if n == j:
            score = score + causal_ref[...]
        weight = jnp.exp(score - log_ref[h : h + 1, rows])
        change = (weight * (change - dots[h : h + 1, rows])).astype(jnp.bfloat16)
        return weight.astype(jnp.bfloat16), change

    def finishing(j, members):
        count = len(members) // 2
        keys = pl.ds(j * tile, tile)
        rows = pl.ds(j * QUERY_BLOCK, count * QUERY_BLOCK)

        def query_side(h):
            part = pl.ds(h * half, half)
            mine = jnp.concatenate([m[1] for m in members[h * count : (h + 1) * count]], axis=1)
            turned_sums[part, rows] += matmul_rows(turned_keys[part, keys], mine)

        def key_side(out_refs, which, right):
            left = jnp.concatenate([m[which] for m in members], axis=1)
            right = jnp.concatenate([right[0, rows, :], right[1, rows, :]])
            both = matmul_rows(left, right).astype(jnp.bfloat16)
            for k in range(cores):
                mine = both[k * QUERY_BLOCK : (k + 1) * QUERY_BLOCK]
                out_refs[k][pl.ds(j * QUERY_BLOCK, QUERY_BLOCK), :] = mine

        return [
            functools.partial(key_side, grad_value_refs, 0, grad_heads),
            functools.partial(query_side, 0),
            functools.partial(key_side, grad_key_refs, 1, query_heads),
            functools.partial(query_side, 1),
        ]

    def every(skipped):
        units = []
        for j in range(blocks):
            last = min(blocks - 1, j + reach)
            if skipped and j + reach == blocks - 1:
                last -= 1
            units += [(j, n, h, n == last and h) for h in range(2) for n in range(j, last + 1)]
        waiting, members, left = [], [], []
        for unit in units + [None] * AHEAD:
            if unit is not None:
                waiting.append((unit, products(*unit[:3])))
            if len(waiting) > AHEAD or unit is None:
                (j, n, h, closing), pair = waiting.pop(0)
                members.append(weigh(j, n, h, *pair))
                for task in left[:PER]:
                    task()
                left = left[PER:]
                if closing:
                    left += finishing(j, members)
                    members = []
        for task in left:
            task()

    every(skipped)
    grad_query_ref[...] = (turned_sums[...] * score_scale).T.astype(jnp.bfloat16)


def standardized(values):
    average = jnp.mean(values, axis=-1, keepdims=True)
    centred = values - average
    spread_inverse = lax.rsqrt(jnp.mean(centred * centred, axis=-1, keepdims=True) + norm_eps)
    return centred * spread_inverse, spread_inverse


def norm_pull(grad, shaped, spread_inverse):
    mean_grad = jnp.mean(grad, axis=-1, keepdims=True)
    mean_product = jnp.mean(grad * shaped, axis=-1, keepdims=True)
    return spread_inverse * (grad - mean_grad - shaped * mean_product)


def enter_kernel(
    stripe, x_ref, gain_ref, shift_ref, bias_ref, down_ref, up_ref, key_weight_ref,
    value_weight_ref, key_ref, value_ref, normed_ref, lora_ref,
):
    shaped, _ = standardized(tokens_of(x_ref, stripe, key_ref.shape[1]).astype(jnp.float32))
    normed = (shaped * gain_ref[...] + shift_ref[...]).astype(jnp.bfloat16)
    normed_ref[...] = normed
    key_ref[...] = matmul_rows(normed, key_weight_ref[...]).astype(jnp.bfloat16)
    lora = matmul_rows(normed, down_ref[...]).astype(jnp.bfloat16)
    lora_ref[...] = lora
    value = matmul_rows(normed, value_weight_ref[...]) + matmul_rows(lora, up_ref[...])
    value_ref[...] = (value + bias_ref[...]).astype(jnp.bfloat16)


def ask_kernel(normed_ref, lora_ref, bias_ref, up_ref, weight_ref, query_ref):
    query = matmul_rows(normed_ref[...], weight_ref[...]) + matmul_rows(lora_ref[...], up_ref[...])
    query_ref[...] = (query + bias_ref[...]).astype(jnp.bfloat16)


root_two_over_pi = 0.7978845608028654
cubic = 0.044715


def middle_kernel(
    stripe, x_ref, attended_ref, cotangent_ref,
    out_bias_ref, gain_ref, shift_ref, expand_bias_ref, contract_bias_ref,
    out_weight_from, expand_from, contract_from,
    result_ref, grad_middle_ref, grad_attended_ref,
    out_weight_ref, expand_ref, contract_ref, arrivals,
):
    width, hidden = expand_ref.shape
    parts = [slice(at, at + HIDDEN_BLOCK) for at in range(0, hidden, HIDDEN_BLOCK)]
    copies = [pltpu.make_async_copy(out_weight_from, out_weight_ref, arrivals.at[0])]
    for i, part in enumerate(parts):
        for which, source, to in (
            (1, expand_from.at[:, part], expand_ref.at[:, part]),
            (2, contract_from.at[part, :], contract_ref.at[part, :]),
        ):
            copies.append(pltpu.make_async_copy(source, to, arrivals.at[2 * i + which]))

    def block(first):
        if first:
            for copy in copies:
                copy.start()
            copies[0].wait()
        middle = (
            tokens_of(x_ref, stripe, width).astype(jnp.float32)
            + matmul_rows(attended_ref[...], out_weight_ref[...])
            + out_bias_ref[...]
        )
        shaped, spread_inverse = standardized(middle)
        normed = (shaped * gain_ref[...] + shift_ref[...]).astype(jnp.bfloat16)
        grad_low = tokens_of(cotangent_ref, stripe, width)
        grad_out = grad_low.astype(jnp.float32)
        result = middle + contract_bias_ref[...]
        grad_normed = jnp.zeros_like(middle)
        for i, part in enumerate(parts):
            if first:
                copies[2 * i + 1].wait()
                copies[2 * i + 2].wait()
            pre = matmul_rows(normed, expand_ref[:, part]) + expand_bias_ref[:, part]
            grad_act = matmul_back(grad_low, contract_ref[part, :])
            square = pre * pre
            bent = jnp.tanh(root_two_over_pi * pre * (1.0 + cubic * square))
            upper = 0.5 + 0.5 * bent
            act = (pre * upper).astype(jnp.bfloat16)
            slope = upper + (0.5 * root_two_over_pi) * pre * (1.0 - bent * bent) * (
                1.0 + (3.0 * cubic) * square
            )
            grad_pre = (grad_act * slope).astype(jnp.bfloat16)
            result = result + matmul_rows(act, contract_ref[part, :])
            grad_normed = grad_normed + matmul_back(grad_pre, expand_ref[:, part])
        result_ref[...] = result.astype(jnp.bfloat16)
        grad_middle = grad_out + norm_pull(grad_normed * gain_ref[...], shaped, spread_inverse)
        grad_middle_low = grad_middle.astype(jnp.bfloat16)
        grad_middle_ref[...] = grad_middle_low
        grad_attended = matmul_back(grad_middle_low, out_weight_ref[...])
        grad_attended_ref[...] = grad_attended.astype(jnp.bfloat16)

    pl.when(pl.program_id(0) == 0)(functools.partial(block, True))
    pl.when(pl.program_id(0) != 0)(functools.partial(block, False))


def total(parts):
    out = parts[0][...].astype(jnp.float32)
    for part in parts[1:]:
        out = out + part[...].astype(jnp.float32)
    return out.astype(jnp.bfloat16)


def adapt_kernel(
    cores, normed_ref, lora_ref, grad_lora_ref, grad_query_ref, *refs
):
    down_sum_ref, up_sum_ref = refs[cores:]
    slots = down_sum_ref.shape[0]

    @pl.when(pl.program_id(0) == 0)
    def _():
        down_sum_ref[...] = jnp.zeros_like(down_sum_ref)
        up_sum_ref[...] = jnp.zeros_like(up_sum_ref)

    width = grad_query_ref.shape[1]
    lora = lora_ref[...]
    down_sum_ref[...] += matmul_over(grad_lora_ref[...], normed_ref[...])[:slots]
    up_sum_ref[:, :width] += matmul_over(lora, grad_query_ref[...])[:slots]
    up_sum_ref[:, width:] += matmul_over(lora, total(refs[:cores]))[:slots]


def leave_kernel(
    stripe, cores, x_ref, gain_ref, weight_ref, down_ref, up_ref, grad_middle_ref,
    grad_query_ref, *refs,
):
    key_refs, value_refs = refs[:cores], refs[cores : 2 * cores]
    grad_ref, grad_lora_ref = refs[2 * cores :]
    width = grad_query_ref.shape[1]
    grad_query = grad_query_ref[...]
    grad_value = total(value_refs)
    grad_lora = matmul_back(grad_query, up_ref[:, :width]) + matmul_back(
        grad_value, up_ref[:, width:]
    )
    grad_lora = grad_lora.astype(jnp.bfloat16)
    grad_lora_ref[...] = grad_lora
    shaped, spread_inverse = standardized(tokens_of(x_ref, stripe, width).astype(jnp.float32))
    grad_normed = (
        matmul_back(grad_query, weight_ref[:, :width])
        + matmul_back(total(key_refs), weight_ref[:, width : 2 * width])
        + matmul_back(grad_value, weight_ref[:, 2 * width :])
        + matmul_back(grad_lora, down_ref[...])
    )
    grad = norm_pull(grad_normed * gain_ref[...], shaped, spread_inverse)
    grad_ref[...] = (grad_middle_ref[...].astype(jnp.float32) + grad).astype(jnp.bfloat16)


def tile(x):
    def spec(tokens):
        share = x.shape[0] * min(TOKEN_BLOCK, tokens) // tokens
        return pl.BlockSpec((share, *x.shape[1:]), lambda i: (i,) + (0,) * (len(x.shape) - 1))

    return x, spec


def whole(x):
    def spec(tokens):
        kept = pl.Buffered(1)
        return pl.BlockSpec(x.shape, lambda i: (0,) * len(x.shape), pipeline_mode=kept)

    return x, spec


def columns(x, which, width):
    def spec(tokens):
        kept = pl.Buffered(1)
        return pl.BlockSpec((x.shape[0], width), lambda i: (0, which), pipeline_mode=kept)

    return x, spec


def in_place(x):
    return x, lambda tokens: pl.BlockSpec(memory_space=pl.ANY)


def over_tokens(kernel, name, tokens, operands, outs, sums, flops, scratch=()):
    moved = sum(x.size * x.dtype.itemsize for x in [*(x for x, _ in operands), *outs, *sums])
    return pl.pallas_call(
        kernel,
        grid=(tokens // min(TOKEN_BLOCK, tokens),),
        in_specs=[spec(tokens) for _, spec in operands],
        out_specs=[tile(x)[1](tokens) for x in outs]
        + [pl.BlockSpec(x.shape, lambda i: (0, 0)) for x in sums],
        out_shape=[*outs, *sums],
        scratch_shapes=list(scratch),
        compiler_params=pltpu.CompilerParams(
            dimension_semantics=("arbitrary",), vmem_limit_bytes=VMEM_BYTES
        ),
        cost_estimate=pl.CostEstimate(flops=flops, bytes_accessed=moved, transcendentals=0),
        name=name,
    )(*(x for x, _ in operands))


def attention_calls(tokens, width, cores, reach):
    pair = pl.BlockSpec((tokens, LANES), lambda p, far: (0, p))
    marks = pl.BlockSpec((cores * tokens, LANES), lambda p, far: (0, 0))
    causal = pl.BlockSpec((cores * QUERY_BLOCK, QUERY_BLOCK), lambda p, far: (0, 0))
    logs = pl.BlockSpec((8, tokens), lambda p, far: (p, 0))
    grid = (width // LANES,)
    blocks = tokens // QUERY_BLOCK
    pairs = sum(min(n, reach) + 1 for n in range(blocks)) * cores * QUERY_BLOCK**2 * HEADS
    head_width = width // HEADS
    low = jax.ShapeDtypeStruct((tokens, width), jnp.bfloat16)
    log_rows = jax.ShapeDtypeStruct((8 * grid[0], tokens), jnp.float32)
    params = pltpu.CompilerParams(
        dimension_semantics=("arbitrary",), vmem_limit_bytes=VMEM_BYTES
    )
    low_scratch = functools.partial(pltpu.VMEM, dtype=jnp.bfloat16)
    forward = pl.pallas_call(
        functools.partial(either_way, attend_block, cores, reach),
        grid_spec=pltpu.PrefetchScalarGridSpec(
            num_scalar_prefetch=1,
            grid=grid,
            in_specs=[pair] * (1 + 2 * cores) + [marks, causal],
            out_specs=[pair, logs],
            scratch_shapes=[
                low_scratch((2, cores * tokens, LANES)),
                low_scratch((2, LANES // 2 + 16, cores * tokens)),
            ],
        ),
        out_shape=[low, log_rows],
        compiler_params=params,
        cost_estimate=pl.CostEstimate(
            flops=4 * pairs * head_width,
            bytes_accessed=2 * tokens * width * (2 + 2 * cores),
            transcendentals=pairs,
        ),
        name="attend",
    )
    backward = pl.pallas_call(
        functools.partial(either_way, pull_block, cores, reach),
        grid_spec=pltpu.PrefetchScalarGridSpec(
            num_scalar_prefetch=1,
            grid=grid,
            in_specs=[pair, pair, pair, logs] + [pair] * (2 * cores) + [marks, causal],
            out_specs=[pair] * (1 + 2 * cores),
            scratch_shapes=[
                low_scratch((2, tokens, LANES)),
                low_scratch((2, tokens, LANES)),
                low_scratch((2, cores * tokens, LANES)),
                low_scratch((cores * tokens, LANES)),
                low_scratch((2, tokens, LANES)),
                low_scratch((LANES, cores * tokens)),
                pltpu.VMEM((LANES, tokens), jnp.float32),
                pltpu.VMEM((8, tokens), jnp.float32),
            ],
        ),
        out_shape=[low] * (1 + 2 * cores),
        compiler_params=params,
        cost_estimate=pl.CostEstimate(
            flops=10 * pairs * head_width,
            bytes_accessed=2 * tokens * width * (4 + 4 * cores),
            transcendentals=pairs,
        ),
        name="pull",
    )
    return forward, backward


def body(
    inputs,
    segments,
    groups,
    group_loss_weight,
    attention_norm_gain,
    attention_norm_bias,
    query_key_value_weight,
    query_value_bias,
    attention_out_weight,
    attention_out_bias,
    feedforward_norm_gain,
    feedforward_norm_bias,
    expand_weight,
    expand_bias,
    contract_weight,
    contract_bias,
    adapter_down_maps,
    adapter_up_maps,
    down_velocity,
    up_velocity,
    running_down_mean,
    running_up_mean,
    cotangent,
):
    rows_here, tokens_here, width = inputs.shape
    cores = lax.axis_size("batch")
    ring = lax.axis_size("seq")
    assert rows_here * cores == ring
    stripe = tokens_here // cores
    tokens = ring * stripe
    span = QUERY_BLOCK * cores
    reach = -(-(EXAMPLE_MAX - 1) // span)
    rank = adapter_down_maps.shape[-1]
    core = lax.axis_index("batch")
    attend, pull = attention_calls(tokens, width, cores, reach)

    assert tokens_here == LANES
    marks = jnp.broadcast_to(segments[:, None, :], (rows_here, 8, tokens_here))
    x = rows_home(gather_stripes(inputs, marks.astype(jnp.bfloat16)))
    chooser = groups[..., None] == jnp.arange(group_loss_weight.shape[0], dtype=jnp.int32)
    token_weight = jnp.sum(jnp.where(chooser, group_loss_weight, 0.0), axis=-1, keepdims=True)
    weighted = (cotangent.astype(jnp.float32) * token_weight).astype(jnp.bfloat16)
    stripes = gather_stripes(weighted)
    place = jnp.arange(QUERY_BLOCK, dtype=jnp.int32)
    place = tokens_here * (place // stripe) + place % stripe
    after = []
    for by in range(cores):
        key_place = place + stripe * lax.rem(core - by + cores, cores)
        after.append(key_place[:, None] > (place + stripe * core)[None, :])
    causal = jnp.where(jnp.concatenate(after), masked_score, 0.0).astype(jnp.float32)

    def row_of(vector):
        return vector.astype(jnp.float32).reshape(1, -1)

    first_gain, first_shift = row_of(attention_norm_gain), row_of(attention_norm_bias)
    second_gain, second_shift = row_of(feedforward_norm_gain), row_of(feedforward_norm_bias)
    pad = LANES - 2 * rank
    down_packed = jnp.concatenate([adapter_down_maps[0], adapter_down_maps[1]], axis=1)
    down_packed = jnp.pad(down_packed, ((0, 0), (0, pad))).astype(jnp.bfloat16)
    up_packed = jnp.concatenate(
        [
            jnp.pad(adapter_up_maps[0], ((0, rank + pad), (0, 0))),
            jnp.pad(adapter_up_maps[1], ((rank, pad), (0, 0))),
        ],
        axis=1,
    )
    up_packed = (adapter_scale * up_packed).astype(jnp.bfloat16)
    value_bias = query_value_bias.astype(jnp.float32)
    out_bias, up_bias, down_bias = map(row_of, (attention_out_bias, expand_bias, contract_bias))
    (
        x, stripes, causal, first_gain, first_shift, second_gain, second_shift,
        value_bias, out_bias, up_bias, down_bias, down_packed, up_packed,
    ) = lax.optimization_barrier(
        (
            x, stripes, causal, first_gain, first_shift, second_gain, second_shift,
            value_bias, out_bias, up_bias, down_bias, down_packed, up_packed,
        )
    )
    cotangent_home = rows_home(stripes)
    row_segments = x[:, width // LANES * stripe, :].astype(jnp.int32)
    parts = row_segments.reshape(ring, cores, stripe)
    turns = [lax.rem(core - by + cores, cores) for by in range(cores)]
    parts = [lax.dynamic_index_in_dim(parts, turn, 1, keepdims=False) for turn in turns]
    slot = jnp.arange(LANES, dtype=jnp.int32) % (LANES // 2)
    marks = jnp.concatenate(parts).reshape(cores * tokens, 1) == slot[None, :]
    marks = marks.astype(jnp.bfloat16)
    row_segments = row_segments.reshape(ring * tokens_here)
    blocks = tokens // QUERY_BLOCK
    last = max(0, blocks - 1 - reach)
    far = row_segments[span * (last + 1) - 1] >= row_segments[span * (blocks - 1)]
    far = far.astype(jnp.int32)[None]

    low = jax.ShapeDtypeStruct((tokens, width), jnp.bfloat16)

    keys, values, normed, lora = over_tokens(
        functools.partial(enter_kernel, stripe),
        "enter",
        tokens,
        [tile(x), whole(first_gain), whole(first_shift), whole(value_bias[1:])]
        + [whole(down_packed), columns(up_packed, 1, width)]
        + [columns(query_key_value_weight, kind, width) for kind in (1, 2)],
        [low, low, low, jax.ShapeDtypeStruct((tokens, LANES), jnp.bfloat16)],
        [],
        4 * tokens * width * width,
    )
    all_keys = [keys] + [from_core(keys, by) for by in range(1, cores)]
    all_values = [values] + [from_core(values, by) for by in range(1, cores)]
    (queries,) = over_tokens(
        ask_kernel,
        "ask",
        tokens,
        [tile(normed), tile(lora), whole(value_bias[:1]), columns(up_packed, 0, width)]
        + [columns(query_key_value_weight, 0, width)],
        [low],
        [],
        2 * tokens * width * width,
    )
    attended, log_total = attend(far, queries, *all_keys, *all_values, marks, causal)

    hidden = expand_weight.shape[1]
    layer_result, grad_middle, grad_attended = over_tokens(
        functools.partial(middle_kernel, stripe),
        "middle",
        tokens,
        [tile(x), tile(attended), tile(cotangent_home)]
        + [whole(v) for v in (out_bias, second_gain, second_shift, up_bias, down_bias)]
        + [in_place(w) for w in (attention_out_weight, expand_weight, contract_weight)],
        [low, low, low],
        [],
        4 * tokens * width * (width + 2 * hidden),
        [pltpu.VMEM(w.shape, w.dtype) for w in (attention_out_weight, expand_weight, contract_weight)]
        + [pltpu.SemaphoreType.DMA((1 + 2 * (hidden // HIDDEN_BLOCK),))],
    )
    layer_out = rows_back(layer_result)

    pulled = pull(
        far,
        queries,
        grad_attended,
        attended,
        log_total,
        *all_keys,
        *all_values,
        marks,
        causal,
    )

    layer_out, pulled = lax.optimization_barrier((layer_out, pulled))
    layer_out = spread_stripes(layer_out)

    def owned(parts):
        return [parts[0]] + [from_core(parts[by], -by) for by in range(1, cores)]

    sums = [
        jax.ShapeDtypeStruct((2 * rank, width), jnp.float32),
        jax.ShapeDtypeStruct((2 * rank, 2 * width), jnp.float32),
    ]
    owned_values = owned(pulled[1 + cores :])
    owned_keys = owned(pulled[1 : 1 + cores])
    input_grad, grad_lora = over_tokens(
        functools.partial(leave_kernel, stripe, cores),
        "leave",
        tokens,
        [tile(x), whole(first_gain), whole(query_key_value_weight), whole(down_packed)]
        + [whole(up_packed), tile(grad_middle), tile(pulled[0])]
        + [tile(part) for part in (*owned_keys, *owned_values)],
        [low, jax.ShapeDtypeStruct((tokens, LANES), jnp.bfloat16)],
        [],
        6 * tokens * width * width,
    )
    down_sum, up_sum = over_tokens(
        functools.partial(adapt_kernel, cores),
        "adapt",
        tokens,
        [tile(part) for part in (normed, lora, grad_lora, pulled[0], *owned_values)],
        [],
        sums,
        512 * tokens * width,
    )
    layer_out, down_sum = lax.optimization_barrier((layer_out, down_sum))
    up_parts = [
        adapter_scale * up_sum[j * rank : (j + 1) * rank, j * width : (j + 1) * width]
        for j in range(2)
    ]
    input_grad = spread_stripes(rows_back(input_grad))
    adapter_sums = sum_everywhere(jnp.concatenate([*up_parts, down_sum], axis=0))
    adapter_sums = adapter_sums.reshape(2, 2, rank, width)
    up_map_gradient = adapter_sums[0]
    down_map_gradient = jnp.transpose(adapter_sums[1], (0, 2, 1))

    down_velocity_next = velocity_factor * down_velocity + down_map_gradient
    up_velocity_next = velocity_factor * up_velocity + up_map_gradient
    adapter_down_updated = adapter_down_maps - learning_step_size * (
        down_map_gradient + velocity_factor * down_velocity_next
    )
    adapter_up_updated = adapter_up_maps - learning_step_size * (
        up_map_gradient + velocity_factor * up_velocity_next
    )
    updated_down_mean = (
        mean_decay_factor * running_down_mean + (1.0 - mean_decay_factor) * adapter_down_updated
    )
    updated_up_mean = (
        mean_decay_factor * running_up_mean + (1.0 - mean_decay_factor) * adapter_up_updated
    )
    return (
        layer_out,
        input_grad,
        down_map_gradient,
        up_map_gradient,
        adapter_down_updated,
        adapter_up_updated,
        down_velocity_next,
        up_velocity_next,
        updated_down_mean,
        updated_up_mean,
        adapter_down_updated.astype(jnp.bfloat16),
        adapter_up_updated.astype(jnp.bfloat16),
    )


def solution(mesh):
    tokens = P("batch", "seq", None)
    codes = P("batch", "seq")
    return jax.shard_map(
        body,
        mesh=mesh,
        in_specs=(tokens, codes, codes) + (P(),) * 19 + (tokens,),
        out_specs=(tokens, tokens) + (P(),) * 10,
        check_vma=False,
    )
```

```python
import functools

import jax
import jax.numpy as jnp
from jax import lax
from jax.experimental import pallas as pl
from jax.experimental.pallas import tpu as pltpu
from jax.sharding import PartitionSpec as P

HEADS = 16
EXAMPLE_MAX = 1024
SEGMENT_SLOTS = 8
LANES = 128
QUERY_BLOCK = 256
TOKEN_BLOCK = 256
HIDDEN_BLOCK = 1024
AHEAD = 2
PER = 2
SCORES_AHEAD = 2
DELAY = 0
VMEM_BYTES = 63 * 1024 * 1024

norm_eps = 1e-05
adapter_scale = 8.0
learning_step_size = 3e-05
velocity_factor = 0.5
mean_decay_factor = 0.5
masked_score = -1e30
score_scale = 0.125


def matmul_rows(left_side, right_side):
    return lax.dot_general(
        left_side, right_side, (((1,), (0,)), ((), ())), preferred_element_type=jnp.float32
    )


def matmul_back(left_side, right_side):
    return lax.dot_general(
        left_side, right_side, (((1,), (1,)), ((), ())), preferred_element_type=jnp.float32
    )


def matmul_over(left_side, right_side):
    return lax.dot_general(
        left_side, right_side, (((0,), (0,)), ((), ())), preferred_element_type=jnp.float32
    )


def gather_kernel(cores, with_codes, core_ref, *refs):
    stripes, codes, out_ref = refs[:cores], refs[cores:-1], refs[-1]
    came_from = lax.rem(core_ref[0] - pl.program_id(0) + cores, cores)
    stripe, width = stripes[0].shape[1:]
    for by in range(cores):

        @pl.when(came_from == by)
        def _(by=by):
            for group in range(width // LANES):
                rows = pl.ds(group * stripe, stripe)
                out_ref[:, rows, :] = stripes[by][:, :, group * LANES : (group + 1) * LANES]
            if with_codes:
                out_ref[:, width // LANES * stripe :, :] = codes[by][...]


def gather_stripes(x, codes=None):
    cores = lax.axis_size("batch")
    core = lax.axis_index("batch")
    rows, tokens, width = x.shape
    stripe = tokens // cores
    parts, extra = [x], [] if codes is None else [codes]
    for by in range(1, cores):
        goes = lax.rem(core + by, cores)
        parts.append(from_core(lax.dynamic_slice_in_dim(x, goes * stripe, stripe, 1), by))
        extra += [] if codes is None else [from_core(codes, by)]
    deep = width // LANES * stripe + sum(c.shape[1] for c in extra[:1])
    whole = pl.BlockSpec((rows, stripe, width), lambda c, core: (0, 0, 0))
    return pl.pallas_call(
        functools.partial(gather_kernel, cores, bool(extra)),
        grid_spec=pltpu.PrefetchScalarGridSpec(
            num_scalar_prefetch=1,
            grid=(cores,),
            in_specs=[pl.BlockSpec((rows, stripe, width), lambda c, core: (0, core[0], 0))]
            + [whole] * (cores - 1)
            + [pl.BlockSpec(c.shape, lambda c, core: (0, 0, 0)) for c in extra],
            out_specs=pl.BlockSpec((rows, deep, LANES), lambda c, core: (c, 0, 0)),
        ),
        out_shape=jax.ShapeDtypeStruct((rows * cores, deep, LANES), x.dtype),
        compiler_params=pltpu.CompilerParams(vmem_limit_bytes=32 * 1024 * 1024),
        name="gather_stripes",
    )(core[None], *parts, *extra)


def spread_kernel(cores, core_ref, *refs):
    came_from = lax.rem(core_ref[0] - pl.program_id(0) + cores, cores)
    for by in range(cores):

        @pl.when(came_from == by)
        def _(by=by):
            refs[-1][...] = refs[by][...]


def spread_stripes(y):
    cores = lax.axis_size("batch")
    core = lax.axis_index("batch")
    rows, stripe, width = y.shape[0] // cores, *y.shape[1:]
    parts = [y]
    for by in range(1, cores):
        goes = lax.rem(core + by, cores)
        parts.append(from_core(lax.dynamic_slice_in_dim(y, goes * rows, rows, 0), by))
    block = (rows, stripe, width)
    return pl.pallas_call(
        functools.partial(spread_kernel, cores),
        grid_spec=pltpu.PrefetchScalarGridSpec(
            num_scalar_prefetch=1,
            grid=(cores,),
            in_specs=[pl.BlockSpec(block, lambda c, core: (core[0], 0, 0))]
            + [pl.BlockSpec(block, lambda c, core: (0, 0, 0))] * (cores - 1),
            out_specs=pl.BlockSpec(block, lambda c, core: (0, c, 0)),
        ),
        out_shape=jax.ShapeDtypeStruct((rows, stripe * cores, width), y.dtype),
        compiler_params=pltpu.CompilerParams(vmem_limit_bytes=32 * 1024 * 1024),
        name="spread_stripes",
    )(core[None], *parts)


def rows_home(y):
    return lax.all_to_all(y, "seq", 0, 0, tiled=True)


def rows_back(y):
    ring = lax.axis_size("seq")
    y = y.reshape(ring, y.shape[0] // ring, y.shape[1])
    return lax.all_to_all(y, "seq", 0, 0, tiled=True)


def tokens_of(ref, stripe, width):
    groups = []
    for group in range(width // LANES):
        rows = slice(group * stripe, (group + 1) * stripe)
        groups.append(jnp.concatenate([ref[c, rows, :] for c in range(ref.shape[0])], axis=0))
    return jnp.concatenate(groups, axis=1)


def from_core(x, by):
    cores = lax.axis_size("batch")
    return lax.ppermute(x, "batch", [(i, (i + by) % cores) for i in range(cores)])


def paired_sum(terms):
    while len(terms) > 1:
        terms = [terms[i] + terms[i + 1] for i in range(0, len(terms), 2)]
    return terms[0]


def sum_everywhere(x, before_last):
    ring, cores = lax.axis_size("seq"), lax.axis_size("batch")
    assert ring & (ring - 1) == 0 and cores & (cores - 1) == 0

    def exchanged(x, axis, size, by):
        return lax.ppermute(x, axis, [(i, i ^ by) for i in range(size)])

    step = 1
    while step < cores:
        x = x + exchanged(x, "batch", cores, step)
        step *= 2
    near = min(4, ring)
    share = x.shape[0] // near
    me = lax.rem(lax.axis_index("seq"), near)

    def shares_of(x, which):
        return lax.dynamic_slice_in_dim(x, which * share, share, 0)

    terms = [shares_of(x, me)]
    for by in range(1, near):
        terms.append(exchanged(shares_of(x, me ^ by), "seq", ring, by))
    mine = paired_sum(terms)
    step = near
    while step < ring:
        width = min(4, ring // step)
        mine = paired_sum(
            [mine] + [exchanged(mine, "seq", ring, by * step) for by in range(1, width)]
        )
        step *= width
    mine, before_last = lax.optimization_barrier((mine, before_last))
    held = [mine] + [exchanged(mine, "seq", ring, by) for by in range(1, near)]
    held = jnp.concatenate(held)
    return jnp.concatenate([shares_of(held, me ^ at) for at in range(near)]), before_last


def lane_masks(dtype):
    lane = lax.broadcasted_iota(jnp.int32, (1, LANES), 1)
    first = (lane < LANES // 2).astype(jnp.float32).astype(dtype)
    second = (lane >= LANES // 2).astype(jnp.float32).astype(dtype)
    return first, second


def slot_row():
    lane = lax.broadcasted_iota(jnp.int32, (1, LANES), 1)
    return (lax.rem(lane, LANES // 2) < SEGMENT_SLOTS).astype(jnp.float32).astype(jnp.bfloat16)


def block_of(ref, index):
    return ref[pl.ds(index * QUERY_BLOCK, QUERY_BLOCK), :]


def attend_block(cores, reach, skipped, *refs):
    query_ref = refs[0]
    key_refs = refs[1 : 1 + cores]
    value_refs = refs[1 + cores : 1 + 2 * cores]
    mark_ref, causal_ref, out_ref, log_ref, key_heads, turned_values = refs[1 + 2 * cores :]
    slots = slot_row()
    heads = lane_masks(jnp.bfloat16)
    half = LANES // 2
    blocks = query_ref.shape[0] // QUERY_BLOCK
    tile = cores * QUERY_BLOCK
    scale = jnp.asarray(score_scale, jnp.bfloat16)
    excluded = jnp.asarray(masked_score, jnp.bfloat16)
    for h in range(2):
        turned_values[h, half:, :] = jnp.ones_like(turned_values[h, half:, :])
    for j in range(blocks):
        for k in range(cores):
            key = block_of(key_refs[k], j)
            key_mark = slots - block_of(mark_ref, k * blocks + j)
            turned = block_of(value_refs[k], j).T
            at = pl.ds(j * tile + k * QUERY_BLOCK, QUERY_BLOCK)
            for h, own in enumerate(heads):
                key_heads[h, at, :] = key * own + key_mark * heads[1 - h]
                turned_values[h, :half, at] = turned[h * half : (h + 1) * half]

    def scores_of(n, h, start):
        query_head = block_of(query_ref, n) * scale * heads[h] + block_of(mark_ref, n) * excluded * heads[1 - h]
        scores = []
        for j in range(start, n + 1):
            score = matmul_back(key_heads[h, pl.ds(j * tile, tile), :], query_head)
            scores.append(score + causal_ref[...] if j == n else score)
        return scores

    def soften(scores):
        top = scores[0]
        for score in scores[1:]:
            top = jnp.maximum(top, score)
        top = jnp.max(top, axis=0, keepdims=True)
        return top, [jnp.exp(score - top).astype(jnp.bfloat16) for score in scores]

    def finish(n, h, start, top, weights, outs):
        rows = pl.ds(n * QUERY_BLOCK, QUERY_BLOCK)
        keys = pl.ds(start * tile, (n + 1 - start) * tile)
        out = matmul_rows(turned_values[h, :, keys], jnp.concatenate(weights))
        total = out[half : half + 1]
        log_ref[h : h + 1, rows] = top + jnp.log(total)
        outs.append(out[:half] / total)
        if h:
            out_ref[rows, :] = jnp.concatenate(outs[-2:]).T.astype(out_ref.dtype)

    def every(skipped):
        waiting, left, outs = [], [], []
        units = []
        for n in range(blocks):
            start = max(0, n - reach) + (skipped and n == blocks - 1)
            units += [(n, h, start) for h in range(2)]
        for unit in units + [None] * SCORES_AHEAD:
            if unit is not None:
                waiting.append((unit, scores_of(*unit)))
            if len(waiting) > SCORES_AHEAD or unit is None:
                done, scores = waiting.pop(0)
                left.append((*done, *soften(scores)))
                if len(left) > DELAY:
                    finish(*left.pop(0), outs)
        for one in left:
            finish(*one, outs)

    every(skipped)


def either_way(block, cores, reach, mark_at, *refs):
    refs, flag_ref = refs[:-1], refs[-1]
    mark_ref = refs[mark_at]
    blocks = refs[0].shape[0] // QUERY_BLOCK
    if blocks <= reach:
        block(cores, reach, False, *refs)
        return

    @pl.when(pl.program_id(0) == 0)
    def _():
        asking = mark_ref[pl.ds((blocks - 1) * QUERY_BLOCK, 16), :].astype(jnp.float32)[:1]
        shared = jnp.zeros_like(asking)
        for k in range(cores):
            last = (k * blocks + blocks - reach) * QUERY_BLOCK - 16
            shared = shared + asking * mark_ref[pl.ds(last, 16), :].astype(jnp.float32)[15:]
        flag_ref[0] = (jnp.sum(shared) > 0.0).astype(jnp.int32)

    pl.when(flag_ref[0] == 1)(functools.partial(block, cores, reach, False, *refs))
    pl.when(flag_ref[0] != 1)(functools.partial(block, cores, reach, True, *refs))


def spread(wide):
    high = wide.astype(jnp.bfloat16)
    return high, (wide - high.astype(jnp.float32)).astype(jnp.bfloat16)


def pull_block(cores, reach, skipped, *refs):
    query_ref, grad_ref, out_ref, log_ref = refs[:4]
    key_refs = refs[4 : 4 + cores]
    value_refs = refs[4 + cores : 4 + 2 * cores]
    mark_ref, causal_ref = refs[4 + 2 * cores : 6 + 2 * cores]
    outs = refs[6 + 2 * cores :]
    slots = slot_row()
    excluded = jnp.asarray(masked_score, jnp.bfloat16)
    grad_query_ref = outs[0]
    grad_key_refs = outs[1 : 1 + cores]
    grad_value_refs = outs[1 + cores : 1 + 2 * cores]
    (
        query_marked, query_heads, key_heads, all_values, grad_heads, turned_keys, turned_sums,
        dots,
    ) = outs[1 + 2 * cores :]
    heads = lane_masks(jnp.bfloat16)
    half = LANES // 2
    blocks = query_ref.shape[0] // QUERY_BLOCK
    tile = cores * QUERY_BLOCK
    scale = jnp.asarray(score_scale, jnp.bfloat16)
    lane = lax.broadcasted_iota(jnp.int32, (8, LANES), 1)
    row = lax.broadcasted_iota(jnp.int32, (8, LANES), 0)
    chooser = (lane // half == row).astype(jnp.float32).astype(jnp.bfloat16)
    for n in range(blocks):
        rows = pl.ds(n * QUERY_BLOCK, QUERY_BLOCK)
        query = query_ref[rows, :] * scale
        grad = grad_ref[rows, :]
        high, rest = spread(grad.astype(jnp.float32) * out_ref[rows, :].astype(jnp.float32))
        dots[:, rows] = matmul_back(chooser, high) + matmul_back(chooser, rest)
        for h, own in enumerate(heads):
            mine = query * own
            query_heads[h, rows, :] = mine
            query_marked[h, rows, :] = mine + mark_ref[rows, :] * excluded * heads[1 - h]
            grad_heads[h, rows, :] = grad * own
        for k in range(cores):
            key = block_of(key_refs[k], n)
            key_mark = slots - block_of(mark_ref, k * blocks + n)
            at = pl.ds(n * tile + k * QUERY_BLOCK, QUERY_BLOCK)
            turned_keys[:, at] = key.T
            all_values[at, :] = block_of(value_refs[k], n)
            for h, own in enumerate(heads):
                key_heads[h, at, :] = key * own + key_mark * heads[1 - h]
    turned_sums[...] = jnp.zeros_like(turned_sums)

    def products(j, n, h):
        keys = pl.ds(j * tile, tile)
        rows = pl.ds(n * QUERY_BLOCK, QUERY_BLOCK)
        score = matmul_back(key_heads[h, keys, :], query_marked[h, rows, :])
        change = matmul_back(all_values[keys, :], grad_heads[h, rows, :])
        return score, change

    def weigh(j, n, h, score, change):
        rows = pl.ds(n * QUERY_BLOCK, QUERY_BLOCK)
        if n == j:
            score = score + causal_ref[...]
        weight = jnp.exp(score - log_ref[h : h + 1, rows])
        change = (weight * (change - dots[h : h + 1, rows])).astype(jnp.bfloat16)
        return weight.astype(jnp.bfloat16), change

    def finishing(j, members):
        count = len(members) // 2
        keys = pl.ds(j * tile, tile)
        rows = pl.ds(j * QUERY_BLOCK, count * QUERY_BLOCK)

        def query_side(h):
            part = pl.ds(h * half, half)
            mine = jnp.concatenate([m[1] for m in members[h * count : (h + 1) * count]], axis=1)
            turned_sums[part, rows] += matmul_rows(turned_keys[part, keys], mine)

        def key_side(out_refs, which, right):
            left = jnp.concatenate([m[which] for m in members], axis=1)
            right = jnp.concatenate([right[0, rows, :], right[1, rows, :]])
            both = matmul_rows(left, right).astype(jnp.bfloat16)
            for k in range(cores):
                mine = both[k * QUERY_BLOCK : (k + 1) * QUERY_BLOCK]
                out_refs[k][pl.ds(j * QUERY_BLOCK, QUERY_BLOCK), :] = mine

        return [
            functools.partial(key_side, grad_value_refs, 0, grad_heads),
            functools.partial(query_side, 0),
            functools.partial(key_side, grad_key_refs, 1, query_heads),
            functools.partial(query_side, 1),
        ]

    def every(skipped):
        units = []
        for j in range(blocks):
            last = min(blocks - 1, j + reach)
            if skipped and j + reach == blocks - 1:
                last -= 1
            units += [(j, n, h, n == last and h) for h in range(2) for n in range(j, last + 1)]
        waiting, members, left = [], [], []
        for unit in units + [None] * AHEAD:
            if unit is not None:
                waiting.append((unit, products(*unit[:3])))
            if len(waiting) > AHEAD or unit is None:
                (j, n, h, closing), pair = waiting.pop(0)
                members.append(weigh(j, n, h, *pair))
                for task in left[:PER]:
                    task()
                left = left[PER:]
                if closing:
                    left += finishing(j, members)
                    members = []
        for task in left:
            task()

    every(skipped)
    grad_query_ref[...] = (turned_sums[...] * score_scale).T.astype(jnp.bfloat16)


def standardized(values):
    average = jnp.mean(values, axis=-1, keepdims=True)
    centred = values - average
    spread_inverse = lax.rsqrt(jnp.mean(centred * centred, axis=-1, keepdims=True) + norm_eps)
    return centred * spread_inverse, spread_inverse


def norm_pull(grad, shaped, spread_inverse):
    mean_grad = jnp.mean(grad, axis=-1, keepdims=True)
    mean_product = jnp.mean(grad * shaped, axis=-1, keepdims=True)
    return spread_inverse * (grad - mean_grad - shaped * mean_product)


def enter_kernel(
    stripe, x_ref, gain_ref, shift_ref, bias_ref, key_weight_ref, value_weight_ref,
    key_ref, value_ref, normed_ref,
):
    shaped, _ = standardized(tokens_of(x_ref, stripe, key_ref.shape[1]).astype(jnp.float32))
    normed = (shaped * gain_ref[...] + shift_ref[...]).astype(jnp.bfloat16)
    normed_ref[...] = normed
    key_ref[...] = matmul_rows(normed, key_weight_ref[...]).astype(jnp.bfloat16)
    value = matmul_rows(normed, value_weight_ref[...])
    value_ref[...] = (value + bias_ref[...]).astype(jnp.bfloat16)


def ask_kernel(normed_ref, bias_ref, weight_ref, query_ref):
    query = matmul_rows(normed_ref[...], weight_ref[...])
    query_ref[...] = (query + bias_ref[...]).astype(jnp.bfloat16)


root_two_over_pi = 0.7978845608028654
cubic = 0.044715


def middle_kernel(
    stripe, x_ref, attended_ref, cotangent_ref,
    out_bias_ref, gain_ref, shift_ref, expand_bias_ref, contract_bias_ref,
    out_weight_from, expand_from, contract_from,
    result_ref, grad_middle_ref, grad_attended_ref,
    out_weight_ref, expand_ref, contract_ref, arrivals,
):
    width, hidden = expand_ref.shape
    parts = [slice(at, at + HIDDEN_BLOCK) for at in range(0, hidden, HIDDEN_BLOCK)]
    copies = [pltpu.make_async_copy(out_weight_from, out_weight_ref, arrivals.at[0])]
    for i, part in enumerate(parts):
        for which, source, to in (
            (1, expand_from.at[:, part], expand_ref.at[:, part]),
            (2, contract_from.at[part, :], contract_ref.at[part, :]),
        ):
            copies.append(pltpu.make_async_copy(source, to, arrivals.at[2 * i + which]))

    def block(first):
        if first:
            for copy in copies:
                copy.start()
            copies[0].wait()
        middle = (
            tokens_of(x_ref, stripe, width).astype(jnp.float32)
            + matmul_rows(attended_ref[...], out_weight_ref[...])
            + out_bias_ref[...]
        )
        shaped, spread_inverse = standardized(middle)
        normed = (shaped * gain_ref[...] + shift_ref[...]).astype(jnp.bfloat16)
        grad_low = tokens_of(cotangent_ref, stripe, width)
        grad_out = grad_low.astype(jnp.float32)
        result = middle + contract_bias_ref[...]
        grad_normed = jnp.zeros_like(middle)
        for i, part in enumerate(parts):
            if first:
                copies[2 * i + 1].wait()
                copies[2 * i + 2].wait()
            pre = matmul_rows(normed, expand_ref[:, part]) + expand_bias_ref[:, part]
            grad_act = matmul_back(grad_low, contract_ref[part, :])
            square = pre * pre
            bent = jnp.tanh(root_two_over_pi * pre * (1.0 + cubic * square))
            upper = 0.5 + 0.5 * bent
            act = (pre * upper).astype(jnp.bfloat16)
            slope = upper + (0.5 * root_two_over_pi) * pre * (1.0 - bent * bent) * (
                1.0 + (3.0 * cubic) * square
            )
            grad_pre = (grad_act * slope).astype(jnp.bfloat16)
            result = result + matmul_rows(act, contract_ref[part, :])
            grad_normed = grad_normed + matmul_back(grad_pre, expand_ref[:, part])
        result_ref[...] = result.astype(jnp.bfloat16)
        grad_middle = grad_out + norm_pull(grad_normed * gain_ref[...], shaped, spread_inverse)
        grad_middle_low = grad_middle.astype(jnp.bfloat16)
        grad_middle_ref[...] = grad_middle_low
        grad_attended = matmul_back(grad_middle_low, out_weight_ref[...])
        grad_attended_ref[...] = grad_attended.astype(jnp.bfloat16)

    pl.when(pl.program_id(0) == 0)(functools.partial(block, True))
    pl.when(pl.program_id(0) != 0)(functools.partial(block, False))


def total(parts):
    out = parts[0][...].astype(jnp.float32)
    for part in parts[1:]:
        out = out + part[...].astype(jnp.float32)
    return out.astype(jnp.bfloat16)


def adapt_kernel(cores, down_ref, up_ref, normed_ref, grad_query_ref, *refs):
    down_sum_ref, up_sum_ref = refs[cores:]
    slots = down_sum_ref.shape[0]

    @pl.when(pl.program_id(0) == 0)
    def _():
        down_sum_ref[...] = jnp.zeros_like(down_sum_ref)
        up_sum_ref[...] = jnp.zeros_like(up_sum_ref)

    width = grad_query_ref.shape[1]
    normed = normed_ref[...]
    grad_query = grad_query_ref[...]
    grad_value = total(refs[:cores])
    lora = matmul_rows(normed, down_ref[...]).astype(jnp.bfloat16)
    grad_lora = matmul_back(grad_query, up_ref[:, :width]) + matmul_back(
        grad_value, up_ref[:, width:]
    )
    down_sum_ref[...] += matmul_over(grad_lora.astype(jnp.bfloat16), normed)[:slots]
    up_sum_ref[:, :width] += matmul_over(lora, grad_query)[:slots]
    up_sum_ref[:, width:] += matmul_over(lora, grad_value)[:slots]


def leave_kernel(
    stripe, cores, x_ref, gain_ref, query_weight_ref, key_weight_ref, value_weight_ref,
    grad_middle_ref, grad_query_ref, *refs,
):
    key_refs, value_refs, grad_ref = refs[:cores], refs[cores : 2 * cores], refs[-1]
    width = grad_query_ref.shape[1]
    shaped, spread_inverse = standardized(tokens_of(x_ref, stripe, width).astype(jnp.float32))
    grad_normed = (
        matmul_back(grad_query_ref[...], query_weight_ref[...])
        + matmul_back(total(key_refs), key_weight_ref[...])
        + matmul_back(total(value_refs), value_weight_ref[...])
    )
    grad = norm_pull(grad_normed * gain_ref[...], shaped, spread_inverse)
    grad_ref[...] = (grad_middle_ref[...].astype(jnp.float32) + grad).astype(jnp.bfloat16)


def tile(x):
    def spec(tokens):
        share = x.shape[0] * min(TOKEN_BLOCK, tokens) // tokens
        return pl.BlockSpec((share, *x.shape[1:]), lambda i: (i,) + (0,) * (len(x.shape) - 1))

    return x, spec


def whole(x):
    def spec(tokens):
        kept = pl.Buffered(1)
        return pl.BlockSpec(x.shape, lambda i: (0,) * len(x.shape), pipeline_mode=kept)

    return x, spec


def columns(x, which, width):
    def spec(tokens):
        kept = pl.Buffered(1)
        return pl.BlockSpec((x.shape[0], width), lambda i: (0, which), pipeline_mode=kept)

    return x, spec


def in_place(x):
    return x, lambda tokens: pl.BlockSpec(memory_space=pl.ANY)


def over_tokens(kernel, name, tokens, operands, outs, sums, flops, scratch=()):
    moved = sum(x.size * x.dtype.itemsize for x in [*(x for x, _ in operands), *outs, *sums])
    return pl.pallas_call(
        kernel,
        grid=(tokens // min(TOKEN_BLOCK, tokens),),
        in_specs=[spec(tokens) for _, spec in operands],
        out_specs=[tile(x)[1](tokens) for x in outs]
        + [pl.BlockSpec(x.shape, lambda i: (0, 0)) for x in sums],
        out_shape=[*outs, *sums],
        scratch_shapes=list(scratch),
        compiler_params=pltpu.CompilerParams(
            dimension_semantics=("arbitrary",), vmem_limit_bytes=VMEM_BYTES
        ),
        cost_estimate=pl.CostEstimate(flops=flops, bytes_accessed=moved, transcendentals=0),
        name=name,
    )(*(x for x, _ in operands))


def attention_calls(tokens, width, cores, reach):
    pair = pl.BlockSpec((tokens, LANES), lambda p: (0, p))
    marks = pl.BlockSpec((cores * tokens, LANES), lambda p: (0, 0))
    causal = pl.BlockSpec((cores * QUERY_BLOCK, QUERY_BLOCK), lambda p: (0, 0))
    logs = pl.BlockSpec((8, tokens), lambda p: (p, 0))
    grid = (width // LANES,)
    blocks = tokens // QUERY_BLOCK
    pairs = sum(min(n, reach) + 1 for n in range(blocks)) * cores * QUERY_BLOCK**2 * HEADS
    head_width = width // HEADS
    low = jax.ShapeDtypeStruct((tokens, width), jnp.bfloat16)
    log_rows = jax.ShapeDtypeStruct((8 * grid[0], tokens), jnp.float32)
    params = pltpu.CompilerParams(
        dimension_semantics=("arbitrary",), vmem_limit_bytes=VMEM_BYTES
    )
    low_scratch = functools.partial(pltpu.VMEM, dtype=jnp.bfloat16)
    forward = pl.pallas_call(
        functools.partial(either_way, attend_block, cores, reach, 1 + 2 * cores),
        grid_spec=pl.GridSpec(
            grid=grid,
            in_specs=[pair] * (1 + 2 * cores) + [marks, causal],
            out_specs=[pair, logs],
            scratch_shapes=[
                low_scratch((2, cores * tokens, LANES)),
                low_scratch((2, LANES // 2 + 16, cores * tokens)),
                pltpu.SMEM((1,), jnp.int32),
            ],
        ),
        out_shape=[low, log_rows],
        compiler_params=params,
        cost_estimate=pl.CostEstimate(
            flops=4 * pairs * head_width,
            bytes_accessed=2 * tokens * width * (2 + 2 * cores),
            transcendentals=pairs,
        ),
        name="attend",
    )
    backward = pl.pallas_call(
        functools.partial(either_way, pull_block, cores, reach, 4 + 2 * cores),
        grid_spec=pl.GridSpec(
            grid=grid,
            in_specs=[pair, pair, pair, logs] + [pair] * (2 * cores) + [marks, causal],
            out_specs=[pair] * (1 + 2 * cores),
            scratch_shapes=[
                low_scratch((2, tokens, LANES)),
                low_scratch((2, tokens, LANES)),
                low_scratch((2, cores * tokens, LANES)),
                low_scratch((cores * tokens, LANES)),
                low_scratch((2, tokens, LANES)),
                low_scratch((LANES, cores * tokens)),
                pltpu.VMEM((LANES, tokens), jnp.float32),
                pltpu.VMEM((8, tokens), jnp.float32),
                pltpu.SMEM((1,), jnp.int32),
            ],
        ),
        out_shape=[low] * (1 + 2 * cores),
        compiler_params=params,
        cost_estimate=pl.CostEstimate(
            flops=10 * pairs * head_width,
            bytes_accessed=2 * tokens * width * (4 + 4 * cores),
            transcendentals=pairs,
        ),
        name="pull",
    )
    return forward, backward


def body(
    inputs,
    segments,
    groups,
    group_loss_weight,
    attention_norm_gain,
    attention_norm_bias,
    query_key_value_weight,
    query_value_bias,
    attention_out_weight,
    attention_out_bias,
    feedforward_norm_gain,
    feedforward_norm_bias,
    expand_weight,
    expand_bias,
    contract_weight,
    contract_bias,
    adapter_down_maps,
    adapter_up_maps,
    down_velocity,
    up_velocity,
    running_down_mean,
    running_up_mean,
    cotangent,
):
    rows_here, tokens_here, width = inputs.shape
    cores = lax.axis_size("batch")
    ring = lax.axis_size("seq")
    assert rows_here * cores == ring
    stripe = tokens_here // cores
    tokens = ring * stripe
    span = QUERY_BLOCK * cores
    reach = -(-(EXAMPLE_MAX - 1) // span)
    rank = adapter_down_maps.shape[-1]
    core = lax.axis_index("batch")
    attend, pull = attention_calls(tokens, width, cores, reach)

    assert tokens_here == LANES
    marks = jnp.broadcast_to(segments[:, None, :], (rows_here, 8, tokens_here))
    x = rows_home(gather_stripes(inputs, marks.astype(jnp.bfloat16)))
    chooser = groups[..., None] == jnp.arange(group_loss_weight.shape[0], dtype=jnp.int32)
    token_weight = jnp.sum(jnp.where(chooser, group_loss_weight, 0.0), axis=-1, keepdims=True)
    weighted = (cotangent.astype(jnp.float32) * token_weight).astype(jnp.bfloat16)
    stripes = gather_stripes(weighted)
    place = jnp.arange(QUERY_BLOCK, dtype=jnp.int32)
    place = tokens_here * (place // stripe) + place % stripe
    after = []
    for by in range(cores):
        key_place = place + stripe * lax.rem(core - by + cores, cores)
        after.append(key_place[:, None] > (place + stripe * core)[None, :])
    causal = jnp.where(jnp.concatenate(after), masked_score, 0.0).astype(jnp.float32)

    def row_of(vector):
        return vector.astype(jnp.float32).reshape(1, -1)

    first_gain, first_shift = row_of(attention_norm_gain), row_of(attention_norm_bias)
    second_gain, second_shift = row_of(feedforward_norm_gain), row_of(feedforward_norm_bias)
    pad = LANES - 2 * rank
    down_packed = jnp.concatenate([adapter_down_maps[0], adapter_down_maps[1]], axis=1)
    down_packed = jnp.pad(down_packed, ((0, 0), (0, pad))).astype(jnp.bfloat16)
    up_packed = jnp.concatenate(
        [
            jnp.pad(adapter_up_maps[0], ((0, rank + pad), (0, 0))),
            jnp.pad(adapter_up_maps[1], ((rank, pad), (0, 0))),
        ],
        axis=1,
    )
    up_packed = (adapter_scale * up_packed).astype(jnp.bfloat16)

    def folded(which, j):
        added = matmul_rows(
            adapter_down_maps[j].astype(jnp.bfloat16), adapter_up_maps[j].astype(jnp.bfloat16)
        )
        frozen = query_key_value_weight[:, which * width : (which + 1) * width]
        return (frozen.astype(jnp.float32) + adapter_scale * added).astype(jnp.bfloat16)

    query_weight, value_weight = folded(0, 0), folded(2, 1)
    value_bias = query_value_bias.astype(jnp.float32)
    out_bias, up_bias, down_bias = map(row_of, (attention_out_bias, expand_bias, contract_bias))
    (
        x, stripes, causal, first_gain, first_shift, second_gain, second_shift,
        value_bias, out_bias, up_bias, down_bias, down_packed, up_packed, query_weight,
        value_weight,
    ) = lax.optimization_barrier(
        (
            x, stripes, causal, first_gain, first_shift, second_gain, second_shift,
            value_bias, out_bias, up_bias, down_bias, down_packed, up_packed, query_weight,
            value_weight,
        )
    )
    cotangent_home = rows_home(stripes)
    parts = x[:, width // LANES * stripe, :].reshape(ring, cores, stripe)
    turns = [lax.rem(core - by + cores, cores) for by in range(cores)]
    parts = [lax.dynamic_index_in_dim(parts, turn, 1, keepdims=False) for turn in turns]
    slot = (jnp.arange(LANES, dtype=jnp.int32) % (LANES // 2)).astype(jnp.bfloat16)
    marks = jnp.concatenate(parts).reshape(cores * tokens, 1) == slot[None, :]
    marks = marks.astype(jnp.bfloat16)

    low = jax.ShapeDtypeStruct((tokens, width), jnp.bfloat16)

    keys, values, normed = over_tokens(
        functools.partial(enter_kernel, stripe),
        "enter",
        tokens,
        [tile(x), whole(first_gain), whole(first_shift), whole(value_bias[1:])]
        + [columns(query_key_value_weight, 1, width), whole(value_weight)],
        [low, low, low],
        [],
        4 * tokens * width * width,
    )
    all_keys = [keys] + [from_core(keys, by) for by in range(1, cores)]
    all_values = [values] + [from_core(values, by) for by in range(1, cores)]
    (queries,) = over_tokens(
        ask_kernel,
        "ask",
        tokens,
        [tile(normed), whole(value_bias[:1]), whole(query_weight)],
        [low],
        [],
        2 * tokens * width * width,
    )
    attended, log_total = attend(queries, *all_keys, *all_values, marks, causal)

    hidden = expand_weight.shape[1]
    layer_result, grad_middle, grad_attended = over_tokens(
        functools.partial(middle_kernel, stripe),
        "middle",
        tokens,
        [tile(x), tile(attended), tile(cotangent_home)]
        + [whole(v) for v in (out_bias, second_gain, second_shift, up_bias, down_bias)]
        + [in_place(w) for w in (attention_out_weight, expand_weight, contract_weight)],
        [low, low, low],
        [],
        4 * tokens * width * (width + 2 * hidden),
        [pltpu.VMEM(w.shape, w.dtype) for w in (attention_out_weight, expand_weight, contract_weight)]
        + [pltpu.SemaphoreType.DMA((1 + 2 * (hidden // HIDDEN_BLOCK),))],
    )
    layer_out = rows_back(layer_result)

    pulled = pull(
        queries,
        grad_attended,
        attended,
        log_total,
        *all_keys,
        *all_values,
        marks,
        causal,
    )

    layer_out, pulled = lax.optimization_barrier((layer_out, pulled))

    def owned(parts):
        return [parts[0]] + [from_core(parts[by], -by) for by in range(1, cores)]

    sums = [
        jax.ShapeDtypeStruct((2 * rank, width), jnp.float32),
        jax.ShapeDtypeStruct((2 * rank, 2 * width), jnp.float32),
    ]
    owned_values = owned(pulled[1 + cores :])
    owned_keys = owned(pulled[1 : 1 + cores])
    (input_grad,) = over_tokens(
        functools.partial(leave_kernel, stripe, cores),
        "leave",
        tokens,
        [tile(x), whole(first_gain), whole(query_weight)]
        + [columns(query_key_value_weight, 1, width), whole(value_weight)]
        + [tile(part) for part in (grad_middle, pulled[0], *owned_keys, *owned_values)],
        [low],
        [],
        6 * tokens * width * width,
    )
    input_grad, normed = lax.optimization_barrier((input_grad, normed))
    down_sum, up_sum = over_tokens(
        functools.partial(adapt_kernel, cores),
        "adapt",
        tokens,
        [whole(down_packed), whole(up_packed)]
        + [tile(part) for part in (normed, pulled[0], *owned_values)],
        [],
        sums,
        1024 * tokens * width,
    )
    layer_out, down_sum = lax.optimization_barrier((spread_stripes(layer_out), down_sum))
    up_parts = [
        adapter_scale * up_sum[j * rank : (j + 1) * rank, j * width : (j + 1) * width]
        for j in range(2)
    ]
    adapter_sums = jnp.concatenate([*up_parts, down_sum], axis=0)
    adapter_sums, input_grad = sum_everywhere(adapter_sums, rows_back(input_grad))
    input_grad = spread_stripes(input_grad)
    adapter_sums = adapter_sums.reshape(2, 2, rank, width)
    up_map_gradient = adapter_sums[0]
    down_map_gradient = jnp.transpose(adapter_sums[1], (0, 2, 1))

    down_velocity_next = velocity_factor * down_velocity + down_map_gradient
    up_velocity_next = velocity_factor * up_velocity + up_map_gradient
    adapter_down_updated = adapter_down_maps - learning_step_size * (
        down_map_gradient + velocity_factor * down_velocity_next
    )
    adapter_up_updated = adapter_up_maps - learning_step_size * (
        up_map_gradient + velocity_factor * up_velocity_next
    )
    updated_down_mean = (
        mean_decay_factor * running_down_mean + (1.0 - mean_decay_factor) * adapter_down_updated
    )
    updated_up_mean = (
        mean_decay_factor * running_up_mean + (1.0 - mean_decay_factor) * adapter_up_updated
    )
    return (
        layer_out,
        input_grad,
        down_map_gradient,
        up_map_gradient,
        adapter_down_updated,
        adapter_up_updated,
        down_velocity_next,
        up_velocity_next,
        updated_down_mean,
        updated_up_mean,
        adapter_down_updated.astype(jnp.bfloat16),
        adapter_up_updated.astype(jnp.bfloat16),
    )


def solution(mesh):
    tokens = P("batch", "seq", None)
    codes = P("batch", "seq")
    return jax.shard_map(
        body,
        mesh=mesh,
        in_specs=(tokens, codes, codes) + (P(),) * 19 + (tokens,),
        out_specs=(tokens, tokens) + (P(),) * 10,
        check_vma=False,
    )
```

```python
import functools

import jax
import jax.numpy as jnp
from jax import lax
from jax.experimental import pallas as pl
from jax.experimental.pallas import tpu as pltpu
from jax.sharding import PartitionSpec as P

HEADS = 16
EXAMPLE_MAX = 1024
SEGMENT_SLOTS = 8
LANES = 128
QUERY_BLOCK = 256
TOKEN_BLOCK = 256
HIDDEN_BLOCK = 1024
AHEAD = 2
PER = 2
SCORES_AHEAD = 2
DELAY = 0
VMEM_BYTES = 63 * 1024 * 1024

norm_eps = 1e-05
adapter_scale = 8.0
learning_step_size = 3e-05
velocity_factor = 0.5
mean_decay_factor = 0.5
masked_score = -1e30
score_scale = 0.125


def matmul_rows(left_side, right_side):
    return lax.dot_general(
        left_side, right_side, (((1,), (0,)), ((), ())), preferred_element_type=jnp.float32
    )


def matmul_back(left_side, right_side):
    return lax.dot_general(
        left_side, right_side, (((1,), (1,)), ((), ())), preferred_element_type=jnp.float32
    )


def matmul_over(left_side, right_side):
    return lax.dot_general(
        left_side, right_side, (((0,), (0,)), ((), ())), preferred_element_type=jnp.float32
    )


def gather_kernel(cores, with_codes, core_ref, *refs):
    stripes, codes, out_ref = refs[:cores], refs[cores:-1], refs[-1]
    came_from = lax.rem(core_ref[0] - pl.program_id(0) + cores, cores)
    stripe, width = stripes[0].shape[1:]
    for by in range(cores):

        @pl.when(came_from == by)
        def _(by=by):
            for group in range(width // LANES):
                rows = pl.ds(group * stripe, stripe)
                out_ref[:, rows, :] = stripes[by][:, :, group * LANES : (group + 1) * LANES]
            if with_codes:
                out_ref[:, width // LANES * stripe :, :] = codes[by][...]


def gather_stripes(x, codes=None):
    cores = lax.axis_size("batch")
    core = lax.axis_index("batch")
    rows, tokens, width = x.shape
    stripe = tokens // cores
    parts, extra = [x], [] if codes is None else [codes]
    for by in range(1, cores):
        goes = lax.rem(core + by, cores)
        parts.append(from_core(lax.dynamic_slice_in_dim(x, goes * stripe, stripe, 1), by))
        extra += [] if codes is None else [from_core(codes, by)]
    deep = width // LANES * stripe + sum(c.shape[1] for c in extra[:1])
    whole = pl.BlockSpec((rows, stripe, width), lambda c, core: (0, 0, 0))
    return pl.pallas_call(
        functools.partial(gather_kernel, cores, bool(extra)),
        grid_spec=pltpu.PrefetchScalarGridSpec(
            num_scalar_prefetch=1,
            grid=(cores,),
            in_specs=[pl.BlockSpec((rows, stripe, width), lambda c, core: (0, core[0], 0))]
            + [whole] * (cores - 1)
            + [pl.BlockSpec(c.shape, lambda c, core: (0, 0, 0)) for c in extra],
            out_specs=pl.BlockSpec((rows, deep, LANES), lambda c, core: (c, 0, 0)),
        ),
        out_shape=jax.ShapeDtypeStruct((rows * cores, deep, LANES), x.dtype),
        compiler_params=pltpu.CompilerParams(vmem_limit_bytes=32 * 1024 * 1024),
        name="gather_stripes",
    )(core[None], *parts, *extra)


def spread_kernel(cores, core_ref, *refs):
    came_from = lax.rem(core_ref[0] - pl.program_id(0) + cores, cores)
    for by in range(cores):

        @pl.when(came_from == by)
        def _(by=by):
            refs[-1][...] = refs[by][...]


def spread_stripes(y):
    cores = lax.axis_size("batch")
    core = lax.axis_index("batch")
    rows, stripe, width = y.shape[0] // cores, *y.shape[1:]
    parts = [y]
    for by in range(1, cores):
        goes = lax.rem(core + by, cores)
        parts.append(from_core(lax.dynamic_slice_in_dim(y, goes * rows, rows, 0), by))
    block = (rows, stripe, width)
    return pl.pallas_call(
        functools.partial(spread_kernel, cores),
        grid_spec=pltpu.PrefetchScalarGridSpec(
            num_scalar_prefetch=1,
            grid=(cores,),
            in_specs=[pl.BlockSpec(block, lambda c, core: (core[0], 0, 0))]
            + [pl.BlockSpec(block, lambda c, core: (0, 0, 0))] * (cores - 1),
            out_specs=pl.BlockSpec(block, lambda c, core: (0, c, 0)),
        ),
        out_shape=jax.ShapeDtypeStruct((rows, stripe * cores, width), y.dtype),
        compiler_params=pltpu.CompilerParams(vmem_limit_bytes=32 * 1024 * 1024),
        name="spread_stripes",
    )(core[None], *parts)


def rows_home(y):
    return lax.all_to_all(y, "seq", 0, 0, tiled=True)


def rows_back(y):
    ring = lax.axis_size("seq")
    y = y.reshape(ring, y.shape[0] // ring, y.shape[1])
    return lax.all_to_all(y, "seq", 0, 0, tiled=True)


def tokens_of(ref, stripe, width):
    groups = []
    for group in range(width // LANES):
        rows = slice(group * stripe, (group + 1) * stripe)
        groups.append(jnp.concatenate([ref[c, rows, :] for c in range(ref.shape[0])], axis=0))
    return jnp.concatenate(groups, axis=1)


def from_core(x, by):
    cores = lax.axis_size("batch")
    return lax.ppermute(x, "batch", [(i, (i + by) % cores) for i in range(cores)])


def paired_sum(terms):
    while len(terms) > 1:
        terms = [terms[i] + terms[i + 1] for i in range(0, len(terms), 2)]
    return terms[0]


def sum_everywhere(x, before_last):
    ring, cores = lax.axis_size("seq"), lax.axis_size("batch")
    assert ring & (ring - 1) == 0 and cores & (cores - 1) == 0

    def exchanged(x, axis, size, by):
        return lax.ppermute(x, axis, [(i, i ^ by) for i in range(size)])

    step = 1
    while step < cores:
        x = x + exchanged(x, "batch", cores, step)
        step *= 2
    near = min(4, ring)
    share = x.shape[0] // near
    me = lax.rem(lax.axis_index("seq"), near)

    def shares_of(x, which):
        return lax.dynamic_slice_in_dim(x, which * share, share, 0)

    terms = [shares_of(x, me)]
    for by in range(1, near):
        terms.append(exchanged(shares_of(x, me ^ by), "seq", ring, by))
    mine = paired_sum(terms)
    step = near
    while step < ring:
        width = min(4, ring // step)
        mine = paired_sum(
            [mine] + [exchanged(mine, "seq", ring, by * step) for by in range(1, width)]
        )
        step *= width
    mine, before_last = lax.optimization_barrier((mine, before_last))
    held = [mine] + [exchanged(mine, "seq", ring, by) for by in range(1, near)]
    held = jnp.concatenate(held)
    return jnp.concatenate([shares_of(held, me ^ at) for at in range(near)]), before_last


def lane_masks(dtype):
    lane = lax.broadcasted_iota(jnp.int32, (1, LANES), 1)
    first = (lane < LANES // 2).astype(jnp.float32).astype(dtype)
    second = (lane >= LANES // 2).astype(jnp.float32).astype(dtype)
    return first, second


def slot_row():
    lane = lax.broadcasted_iota(jnp.int32, (1, LANES), 1)
    return (lax.rem(lane, LANES // 2) < SEGMENT_SLOTS).astype(jnp.float32).astype(jnp.bfloat16)


def block_of(ref, index):
    return ref[pl.ds(index * QUERY_BLOCK, QUERY_BLOCK), :]


def attend_block(cores, reach, skipped, *refs):
    query_ref = refs[0]
    key_refs = refs[1 : 1 + cores]
    value_refs = refs[1 + cores : 1 + 2 * cores]
    mark_ref, causal_ref, out_ref, log_ref, key_heads, turned_values = refs[1 + 2 * cores :]
    slots = slot_row()
    heads = lane_masks(jnp.bfloat16)
    half = LANES // 2
    blocks = query_ref.shape[0] // QUERY_BLOCK
    tile = cores * QUERY_BLOCK
    scale = jnp.asarray(score_scale, jnp.bfloat16)
    excluded = jnp.asarray(masked_score, jnp.bfloat16)
    for h in range(2):
        turned_values[h, half:, :] = jnp.ones_like(turned_values[h, half:, :])
    for j in range(blocks):
        for k in range(cores):
            key = block_of(key_refs[k], j)
            key_mark = slots - block_of(mark_ref, k * blocks + j)
            turned = block_of(value_refs[k], j).T
            at = pl.ds(j * tile + k * QUERY_BLOCK, QUERY_BLOCK)
            for h, own in enumerate(heads):
                key_heads[h, at, :] = key * own + key_mark * heads[1 - h]
                turned_values[h, :half, at] = turned[h * half : (h + 1) * half]

    def scores_of(n, h, start):
        query_head = block_of(query_ref, n) * scale * heads[h] + block_of(mark_ref, n) * excluded * heads[1 - h]
        scores = []
        for j in range(start, n + 1):
            score = matmul_back(key_heads[h, pl.ds(j * tile, tile), :], query_head)
            scores.append(score + causal_ref[...] if j == n else score)
        return scores

    def soften(scores):
        top = scores[0]
        for score in scores[1:]:
            top = jnp.maximum(top, score)
        top = jnp.max(top, axis=0, keepdims=True)
        return top, [jnp.exp(score - top).astype(jnp.bfloat16) for score in scores]

    def finish(n, h, start, top, weights, outs):
        rows = pl.ds(n * QUERY_BLOCK, QUERY_BLOCK)
        keys = pl.ds(start * tile, (n + 1 - start) * tile)
        out = matmul_rows(turned_values[h, :, keys], jnp.concatenate(weights))
        total = out[half : half + 1]
        log_ref[h : h + 1, rows] = top + jnp.log(total)
        outs.append(out[:half] / total)
        if h:
            out_ref[rows, :] = jnp.concatenate(outs[-2:]).T.astype(out_ref.dtype)

    def every(skipped):
        waiting, left, outs = [], [], []
        units = []
        for n in range(blocks):
            start = max(0, n - reach) + (skipped and n == blocks - 1)
            units += [(n, h, start) for h in range(2)]
        for unit in units + [None] * SCORES_AHEAD:
            if unit is not None:
                waiting.append((unit, scores_of(*unit)))
            if len(waiting) > SCORES_AHEAD or unit is None:
                done, scores = waiting.pop(0)
                left.append((*done, *soften(scores)))
                if len(left) > DELAY:
                    finish(*left.pop(0), outs)
        for one in left:
            finish(*one, outs)

    every(skipped)


def either_way(block, cores, reach, mark_at, *refs):
    refs, flag_ref = refs[:-1], refs[-1]
    mark_ref = refs[mark_at]
    blocks = refs[0].shape[0] // QUERY_BLOCK
    if blocks <= reach:
        block(cores, reach, False, *refs)
        return

    @pl.when(pl.program_id(0) == 0)
    def _():
        asking = mark_ref[pl.ds((blocks - 1) * QUERY_BLOCK, 16), :].astype(jnp.float32)[:1]
        shared = jnp.zeros_like(asking)
        for k in range(cores):
            last = (k * blocks + blocks - reach) * QUERY_BLOCK - 16
            shared = shared + asking * mark_ref[pl.ds(last, 16), :].astype(jnp.float32)[15:]
        flag_ref[0] = (jnp.sum(shared) > 0.0).astype(jnp.int32)

    pl.when(flag_ref[0] == 1)(functools.partial(block, cores, reach, False, *refs))
    pl.when(flag_ref[0] != 1)(functools.partial(block, cores, reach, True, *refs))


def spread(wide):
    high = wide.astype(jnp.bfloat16)
    return high, (wide - high.astype(jnp.float32)).astype(jnp.bfloat16)


def pull_block(cores, reach, skipped, *refs):
    query_ref, grad_ref, out_ref, log_ref = refs[:4]
    key_refs = refs[4 : 4 + cores]
    value_refs = refs[4 + cores : 4 + 2 * cores]
    mark_ref, causal_ref = refs[4 + 2 * cores : 6 + 2 * cores]
    outs = refs[6 + 2 * cores :]
    slots = slot_row()
    excluded = jnp.asarray(masked_score, jnp.bfloat16)
    grad_query_ref = outs[0]
    grad_key_refs = outs[1 : 1 + cores]
    grad_value_refs = outs[1 + cores : 1 + 2 * cores]
    (
        query_marked, query_heads, key_heads, all_values, grad_heads, turned_keys, turned_sums,
        dots,
    ) = outs[1 + 2 * cores :]
    heads = lane_masks(jnp.bfloat16)
    half = LANES // 2
    blocks = query_ref.shape[0] // QUERY_BLOCK
    tile = cores * QUERY_BLOCK
    scale = jnp.asarray(score_scale, jnp.bfloat16)
    lane = lax.broadcasted_iota(jnp.int32, (8, LANES), 1)
    row = lax.broadcasted_iota(jnp.int32, (8, LANES), 0)
    chooser = (lane // half == row).astype(jnp.float32).astype(jnp.bfloat16)
    for n in range(blocks):
        rows = pl.ds(n * QUERY_BLOCK, QUERY_BLOCK)
        query = query_ref[rows, :] * scale
        grad = grad_ref[rows, :]
        high, rest = spread(grad.astype(jnp.float32) * out_ref[rows, :].astype(jnp.float32))
        dots[:, rows] = matmul_back(chooser, high) + matmul_back(chooser, rest)
        for h, own in enumerate(heads):
            mine = query * own
            query_heads[h, rows, :] = mine
            query_marked[h, rows, :] = mine + mark_ref[rows, :] * excluded * heads[1 - h]
            grad_heads[h, rows, :] = grad * own
        for k in range(cores):
            key = block_of(key_refs[k], n)
            key_mark = slots - block_of(mark_ref, k * blocks + n)
            at = pl.ds(n * tile + k * QUERY_BLOCK, QUERY_BLOCK)
            turned_keys[:, at] = key.T
            all_values[at, :] = block_of(value_refs[k], n)
            for h, own in enumerate(heads):
                key_heads[h, at, :] = key * own + key_mark * heads[1 - h]
    turned_sums[...] = jnp.zeros_like(turned_sums)

    def products(j, n, h):
        keys = pl.ds(j * tile, tile)
        rows = pl.ds(n * QUERY_BLOCK, QUERY_BLOCK)
        score = matmul_back(key_heads[h, keys, :], query_marked[h, rows, :])
        change = matmul_back(all_values[keys, :], grad_heads[h, rows, :])
        return score, change

    def weigh(j, n, h, score, change):
        rows = pl.ds(n * QUERY_BLOCK, QUERY_BLOCK)
        if n == j:
            score = score + causal_ref[...]
        weight = jnp.exp(score - log_ref[h : h + 1, rows])
        change = (weight * (change - dots[h : h + 1, rows])).astype(jnp.bfloat16)
        return weight.astype(jnp.bfloat16), change

    def finishing(j, members):
        count = len(members) // 2
        keys = pl.ds(j * tile, tile)
        rows = pl.ds(j * QUERY_BLOCK, count * QUERY_BLOCK)

        def query_side(h):
            part = pl.ds(h * half, half)
            mine = jnp.concatenate([m[1] for m in members[h * count : (h + 1) * count]], axis=1)
            turned_sums[part, rows] += matmul_rows(turned_keys[part, keys], mine)

        def key_side(out_refs, which, right):
            left = jnp.concatenate([m[which] for m in members], axis=1)
            right = jnp.concatenate([right[0, rows, :], right[1, rows, :]])
            both = matmul_rows(left, right).astype(jnp.bfloat16)
            for k in range(cores):
                mine = both[k * QUERY_BLOCK : (k + 1) * QUERY_BLOCK]
                out_refs[k][pl.ds(j * QUERY_BLOCK, QUERY_BLOCK), :] = mine

        return [
            functools.partial(key_side, grad_value_refs, 0, grad_heads),
            functools.partial(query_side, 0),
            functools.partial(key_side, grad_key_refs, 1, query_heads),
            functools.partial(query_side, 1),
        ]

    def every(skipped):
        units = []
        for j in range(blocks):
            last = min(blocks - 1, j + reach)
            if skipped and j + reach == blocks - 1:
                last -= 1
            units += [(j, n, h, n == last and h) for h in range(2) for n in range(j, last + 1)]
        waiting, members, left = [], [], []
        for unit in units + [None] * AHEAD:
            if unit is not None:
                waiting.append((unit, products(*unit[:3])))
            if len(waiting) > AHEAD or unit is None:
                (j, n, h, closing), pair = waiting.pop(0)
                members.append(weigh(j, n, h, *pair))
                for task in left[:PER]:
                    task()
                left = left[PER:]
                if closing:
                    left += finishing(j, members)
                    members = []
        for task in left:
            task()

    every(skipped)
    grad_query_ref[...] = (turned_sums[...] * score_scale).T.astype(jnp.bfloat16)


def standardized(values):
    average = jnp.mean(values, axis=-1, keepdims=True)
    centred = values - average
    spread_inverse = lax.rsqrt(jnp.mean(centred * centred, axis=-1, keepdims=True) + norm_eps)
    return centred * spread_inverse, spread_inverse


def norm_pull(grad, shaped, spread_inverse):
    mean_grad = jnp.mean(grad, axis=-1, keepdims=True)
    mean_product = jnp.mean(grad * shaped, axis=-1, keepdims=True)
    return spread_inverse * (grad - mean_grad - shaped * mean_product)


def enter_kernel(
    stripe, x_ref, gain_ref, shift_ref, bias_ref, key_weight_ref, value_weight_ref,
    key_ref, value_ref, normed_ref,
):
    shaped, _ = standardized(tokens_of(x_ref, stripe, key_ref.shape[1]).astype(jnp.float32))
    normed = (shaped * gain_ref[...] + shift_ref[...]).astype(jnp.bfloat16)
    normed_ref[...] = normed
    key_ref[...] = matmul_rows(normed, key_weight_ref[...]).astype(jnp.bfloat16)
    value = matmul_rows(normed, value_weight_ref[...])
    value_ref[...] = (value + bias_ref[...]).astype(jnp.bfloat16)


def ask_kernel(normed_ref, bias_ref, weight_ref, query_ref):
    query = matmul_rows(normed_ref[...], weight_ref[...])
    query_ref[...] = (query + bias_ref[...]).astype(jnp.bfloat16)


root_two_over_pi = 0.7978845608028654
cubic = 0.044715


def middle_kernel(
    stripe, x_ref, attended_ref, cotangent_ref,
    out_bias_ref, gain_ref, shift_ref, expand_bias_ref, contract_bias_ref,
    out_weight_from, expand_from, contract_from,
    result_ref, grad_middle_ref, grad_attended_ref,
    out_weight_ref, expand_ref, contract_ref, arrivals,
):
    width, hidden = expand_ref.shape
    parts = [slice(at, at + HIDDEN_BLOCK) for at in range(0, hidden, HIDDEN_BLOCK)]
    copies = [pltpu.make_async_copy(out_weight_from, out_weight_ref, arrivals.at[0])]
    for i, part in enumerate(parts):
        for which, source, to in (
            (1, expand_from.at[:, part], expand_ref.at[:, part]),
            (2, contract_from.at[part, :], contract_ref.at[part, :]),
        ):
            copies.append(pltpu.make_async_copy(source, to, arrivals.at[2 * i + which]))

    def block(first):
        if first:
            for copy in copies:
                copy.start()
            copies[0].wait()
        middle = (
            tokens_of(x_ref, stripe, width).astype(jnp.float32)
            + matmul_rows(attended_ref[...], out_weight_ref[...])
            + out_bias_ref[...]
        )
        shaped, spread_inverse = standardized(middle)
        normed = (shaped * gain_ref[...] + shift_ref[...]).astype(jnp.bfloat16)
        grad_low = tokens_of(cotangent_ref, stripe, width)
        grad_out = grad_low.astype(jnp.float32)
        result = middle + contract_bias_ref[...]
        grad_normed = jnp.zeros_like(middle)
        for i, part in enumerate(parts):
            if first:
                copies[2 * i + 1].wait()
                copies[2 * i + 2].wait()
            pre = matmul_rows(normed, expand_ref[:, part]) + expand_bias_ref[:, part]
            grad_act = matmul_back(grad_low, contract_ref[part, :])
            square = pre * pre
            bent = jnp.tanh(root_two_over_pi * pre * (1.0 + cubic * square))
            upper = 0.5 + 0.5 * bent
            act = (pre * upper).astype(jnp.bfloat16)
            slope = upper + (0.5 * root_two_over_pi) * pre * (1.0 - bent * bent) * (
                1.0 + (3.0 * cubic) * square
            )
            grad_pre = (grad_act * slope).astype(jnp.bfloat16)
            result = result + matmul_rows(act, contract_ref[part, :])
            grad_normed = grad_normed + matmul_back(grad_pre, expand_ref[:, part])
        result_ref[...] = result.astype(jnp.bfloat16)
        grad_middle = grad_out + norm_pull(grad_normed * gain_ref[...], shaped, spread_inverse)
        grad_middle_low = grad_middle.astype(jnp.bfloat16)
        grad_middle_ref[...] = grad_middle_low
        grad_attended = matmul_back(grad_middle_low, out_weight_ref[...])
        grad_attended_ref[...] = grad_attended.astype(jnp.bfloat16)

    pl.when(pl.program_id(0) == 0)(functools.partial(block, True))
    pl.when(pl.program_id(0) != 0)(functools.partial(block, False))


def total(parts):
    out = parts[0][...].astype(jnp.float32)
    for part in parts[1:]:
        out = out + part[...].astype(jnp.float32)
    return out.astype(jnp.bfloat16)


def adapt_kernel(cores, down_ref, up_ref, normed_ref, grad_query_ref, *refs):
    down_sum_ref, up_sum_ref = refs[cores:]
    slots = down_sum_ref.shape[0]

    @pl.when(pl.program_id(0) == 0)
    def _():
        down_sum_ref[...] = jnp.zeros_like(down_sum_ref)
        up_sum_ref[...] = jnp.zeros_like(up_sum_ref)

    width = grad_query_ref.shape[1]
    normed = normed_ref[...]
    grad_query = grad_query_ref[...]
    grad_value = total(refs[:cores])
    lora = matmul_rows(normed, down_ref[...]).astype(jnp.bfloat16)
    grad_lora = matmul_back(grad_query, up_ref[:, :width]) + matmul_back(
        grad_value, up_ref[:, width:]
    )
    down_sum_ref[...] += matmul_over(grad_lora.astype(jnp.bfloat16), normed)[:slots]
    up_sum_ref[:, :width] += matmul_over(lora, grad_query)[:slots]
    up_sum_ref[:, width:] += matmul_over(lora, grad_value)[:slots]


def return_kernel(grad_query_ref, query_weight_ref, grad_normed_ref):
    grad_normed_ref[...] = matmul_back(grad_query_ref[...], query_weight_ref[...])


def leave_kernel(
    stripe, cores, x_ref, gain_ref, key_weight_ref, value_weight_ref,
    grad_middle_ref, from_queries_ref, *refs,
):
    key_refs, value_refs, grad_ref = refs[:cores], refs[cores : 2 * cores], refs[-1]
    width = grad_middle_ref.shape[1]
    shaped, spread_inverse = standardized(tokens_of(x_ref, stripe, width).astype(jnp.float32))
    grad_normed = (
        from_queries_ref[...]
        + matmul_back(total(key_refs), key_weight_ref[...])
        + matmul_back(total(value_refs), value_weight_ref[...])
    )
    grad = norm_pull(grad_normed * gain_ref[...], shaped, spread_inverse)
    grad_ref[...] = (grad_middle_ref[...].astype(jnp.float32) + grad).astype(jnp.bfloat16)


def tile(x):
    def spec(tokens):
        share = x.shape[0] * min(TOKEN_BLOCK, tokens) // tokens
        return pl.BlockSpec((share, *x.shape[1:]), lambda i: (i,) + (0,) * (len(x.shape) - 1))

    return x, spec


def whole(x):
    def spec(tokens):
        kept = pl.Buffered(1)
        return pl.BlockSpec(x.shape, lambda i: (0,) * len(x.shape), pipeline_mode=kept)

    return x, spec


def columns(x, which, width):
    def spec(tokens):
        kept = pl.Buffered(1)
        return pl.BlockSpec((x.shape[0], width), lambda i: (0, which), pipeline_mode=kept)

    return x, spec


def in_place(x):
    return x, lambda tokens: pl.BlockSpec(memory_space=pl.ANY)


def over_tokens(kernel, name, tokens, operands, outs, sums, flops, scratch=()):
    moved = sum(x.size * x.dtype.itemsize for x in [*(x for x, _ in operands), *outs, *sums])
    return pl.pallas_call(
        kernel,
        grid=(tokens // min(TOKEN_BLOCK, tokens),),
        in_specs=[spec(tokens) for _, spec in operands],
        out_specs=[tile(x)[1](tokens) for x in outs]
        + [pl.BlockSpec(x.shape, lambda i: (0, 0)) for x in sums],
        out_shape=[*outs, *sums],
        scratch_shapes=list(scratch),
        compiler_params=pltpu.CompilerParams(
            dimension_semantics=("arbitrary",), vmem_limit_bytes=VMEM_BYTES
        ),
        cost_estimate=pl.CostEstimate(flops=flops, bytes_accessed=moved, transcendentals=0),
        name=name,
    )(*(x for x, _ in operands))


def attention_calls(tokens, width, cores, reach):
    pair = pl.BlockSpec((tokens, LANES), lambda p: (0, p))
    marks = pl.BlockSpec((cores * tokens, LANES), lambda p: (0, 0))
    causal = pl.BlockSpec((cores * QUERY_BLOCK, QUERY_BLOCK), lambda p: (0, 0))
    logs = pl.BlockSpec((8, tokens), lambda p: (p, 0))
    grid = (width // LANES,)
    blocks = tokens // QUERY_BLOCK
    pairs = sum(min(n, reach) + 1 for n in range(blocks)) * cores * QUERY_BLOCK**2 * HEADS
    head_width = width // HEADS
    low = jax.ShapeDtypeStruct((tokens, width), jnp.bfloat16)
    log_rows = jax.ShapeDtypeStruct((8 * grid[0], tokens), jnp.float32)
    params = pltpu.CompilerParams(
        dimension_semantics=("arbitrary",), vmem_limit_bytes=VMEM_BYTES
    )
    low_scratch = functools.partial(pltpu.VMEM, dtype=jnp.bfloat16)
    forward = pl.pallas_call(
        functools.partial(either_way, attend_block, cores, reach, 1 + 2 * cores),
        grid_spec=pl.GridSpec(
            grid=grid,
            in_specs=[pair] * (1 + 2 * cores) + [marks, causal],
            out_specs=[pair, logs],
            scratch_shapes=[
                low_scratch((2, cores * tokens, LANES)),
                low_scratch((2, LANES // 2 + 16, cores * tokens)),
                pltpu.SMEM((1,), jnp.int32),
            ],
        ),
        out_shape=[low, log_rows],
        compiler_params=params,
        cost_estimate=pl.CostEstimate(
            flops=4 * pairs * head_width,
            bytes_accessed=2 * tokens * width * (2 + 2 * cores),
            transcendentals=pairs,
        ),
        name="attend",
    )
    backward = pl.pallas_call(
        functools.partial(either_way, pull_block, cores, reach, 4 + 2 * cores),
        grid_spec=pl.GridSpec(
            grid=grid,
            in_specs=[pair, pair, pair, logs] + [pair] * (2 * cores) + [marks, causal],
            out_specs=[pair] * (1 + 2 * cores),
            scratch_shapes=[
                low_scratch((2, tokens, LANES)),
                low_scratch((2, tokens, LANES)),
                low_scratch((2, cores * tokens, LANES)),
                low_scratch((cores * tokens, LANES)),
                low_scratch((2, tokens, LANES)),
                low_scratch((LANES, cores * tokens)),
                pltpu.VMEM((LANES, tokens), jnp.float32),
                pltpu.VMEM((8, tokens), jnp.float32),
                pltpu.SMEM((1,), jnp.int32),
            ],
        ),
        out_shape=[low] * (1 + 2 * cores),
        compiler_params=params,
        cost_estimate=pl.CostEstimate(
            flops=10 * pairs * head_width,
            bytes_accessed=2 * tokens * width * (4 + 4 * cores),
            transcendentals=pairs,
        ),
        name="pull",
    )
    return forward, backward


def body(
    inputs,
    segments,
    groups,
    group_loss_weight,
    attention_norm_gain,
    attention_norm_bias,
    query_key_value_weight,
    query_value_bias,
    attention_out_weight,
    attention_out_bias,
    feedforward_norm_gain,
    feedforward_norm_bias,
    expand_weight,
    expand_bias,
    contract_weight,
    contract_bias,
    adapter_down_maps,
    adapter_up_maps,
    down_velocity,
    up_velocity,
    running_down_mean,
    running_up_mean,
    cotangent,
):
    rows_here, tokens_here, width = inputs.shape
    cores = lax.axis_size("batch")
    ring = lax.axis_size("seq")
    assert rows_here * cores == ring
    stripe = tokens_here // cores
    tokens = ring * stripe
    span = QUERY_BLOCK * cores
    reach = -(-(EXAMPLE_MAX - 1) // span)
    rank = adapter_down_maps.shape[-1]
    core = lax.axis_index("batch")
    attend, pull = attention_calls(tokens, width, cores, reach)

    assert tokens_here == LANES
    marks = jnp.broadcast_to(segments[:, None, :], (rows_here, 8, tokens_here))
    x = rows_home(gather_stripes(inputs, marks.astype(jnp.bfloat16)))
    chooser = groups[..., None] == jnp.arange(group_loss_weight.shape[0], dtype=jnp.int32)
    token_weight = jnp.sum(jnp.where(chooser, group_loss_weight, 0.0), axis=-1, keepdims=True)
    weighted = (cotangent.astype(jnp.float32) * token_weight).astype(jnp.bfloat16)
    stripes = gather_stripes(weighted)
    place = jnp.arange(QUERY_BLOCK, dtype=jnp.int32)
    place = tokens_here * (place // stripe) + place % stripe
    after = []
    for by in range(cores):
        key_place = place + stripe * lax.rem(core - by + cores, cores)
        after.append(key_place[:, None] > (place + stripe * core)[None, :])
    causal = jnp.where(jnp.concatenate(after), masked_score, 0.0).astype(jnp.float32)

    def row_of(vector):
        return vector.astype(jnp.float32).reshape(1, -1)

    first_gain, first_shift = row_of(attention_norm_gain), row_of(attention_norm_bias)
    second_gain, second_shift = row_of(feedforward_norm_gain), row_of(feedforward_norm_bias)
    pad = LANES - 2 * rank
    down_packed = jnp.concatenate([adapter_down_maps[0], adapter_down_maps[1]], axis=1)
    down_packed = jnp.pad(down_packed, ((0, 0), (0, pad))).astype(jnp.bfloat16)
    up_packed = jnp.concatenate(
        [
            jnp.pad(adapter_up_maps[0], ((0, rank + pad), (0, 0))),
            jnp.pad(adapter_up_maps[1], ((rank, pad), (0, 0))),
        ],
        axis=1,
    )
    up_packed = (adapter_scale * up_packed).astype(jnp.bfloat16)

    def folded(which, j):
        added = matmul_rows(
            adapter_down_maps[j].astype(jnp.bfloat16), adapter_up_maps[j].astype(jnp.bfloat16)
        )
        frozen = query_key_value_weight[:, which * width : (which + 1) * width]
        return (frozen.astype(jnp.float32) + adapter_scale * added).astype(jnp.bfloat16)

    query_weight, value_weight = folded(0, 0), folded(2, 1)
    value_bias = query_value_bias.astype(jnp.float32)
    out_bias, up_bias, down_bias = map(row_of, (attention_out_bias, expand_bias, contract_bias))
    (
        x, stripes, causal, first_gain, first_shift, second_gain, second_shift,
        value_bias, out_bias, up_bias, down_bias, down_packed, up_packed, query_weight,
        value_weight,
    ) = lax.optimization_barrier(
        (
            x, stripes, causal, first_gain, first_shift, second_gain, second_shift,
            value_bias, out_bias, up_bias, down_bias, down_packed, up_packed, query_weight,
            value_weight,
        )
    )
    cotangent_home = rows_home(stripes)
    parts = x[:, width // LANES * stripe, :].reshape(ring, cores, stripe)
    turns = [lax.rem(core - by + cores, cores) for by in range(cores)]
    parts = [lax.dynamic_index_in_dim(parts, turn, 1, keepdims=False) for turn in turns]
    slot = (jnp.arange(LANES, dtype=jnp.int32) % (LANES // 2)).astype(jnp.bfloat16)
    marks = jnp.concatenate(parts).reshape(cores * tokens, 1) == slot[None, :]
    marks = marks.astype(jnp.bfloat16)

    low = jax.ShapeDtypeStruct((tokens, width), jnp.bfloat16)

    keys, values, normed = over_tokens(
        functools.partial(enter_kernel, stripe),
        "enter",
        tokens,
        [tile(x), whole(first_gain), whole(first_shift), whole(value_bias[1:])]
        + [columns(query_key_value_weight, 1, width), whole(value_weight)],
        [low, low, low],
        [],
        4 * tokens * width * width,
    )
    all_keys = [keys] + [from_core(keys, by) for by in range(1, cores)]
    all_values = [values] + [from_core(values, by) for by in range(1, cores)]
    (queries,) = over_tokens(
        ask_kernel,
        "ask",
        tokens,
        [tile(normed), whole(value_bias[:1]), whole(query_weight)],
        [low],
        [],
        2 * tokens * width * width,
    )
    attended, log_total = attend(queries, *all_keys, *all_values, marks, causal)

    hidden = expand_weight.shape[1]
    layer_result, grad_middle, grad_attended = over_tokens(
        functools.partial(middle_kernel, stripe),
        "middle",
        tokens,
        [tile(x), tile(attended), tile(cotangent_home)]
        + [whole(v) for v in (out_bias, second_gain, second_shift, up_bias, down_bias)]
        + [in_place(w) for w in (attention_out_weight, expand_weight, contract_weight)],
        [low, low, low],
        [],
        4 * tokens * width * (width + 2 * hidden),
        [pltpu.VMEM(w.shape, w.dtype) for w in (attention_out_weight, expand_weight, contract_weight)]
        + [pltpu.SemaphoreType.DMA((1 + 2 * (hidden // HIDDEN_BLOCK),))],
    )
    layer_out = rows_back(layer_result)

    pulled = pull(
        queries,
        grad_attended,
        attended,
        log_total,
        *all_keys,
        *all_values,
        marks,
        causal,
    )

    layer_out, pulled = lax.optimization_barrier((layer_out, pulled))

    def owned(parts):
        return [parts[0]] + [from_core(parts[by], -by) for by in range(1, cores)]

    sums = [
        jax.ShapeDtypeStruct((2 * rank, width), jnp.float32),
        jax.ShapeDtypeStruct((2 * rank, 2 * width), jnp.float32),
    ]
    owned_values = owned(pulled[1 + cores :])
    owned_keys = owned(pulled[1 : 1 + cores])
    (from_queries,) = over_tokens(
        return_kernel,
        "return",
        tokens,
        [tile(pulled[0]), whole(query_weight)],
        [jax.ShapeDtypeStruct((tokens, width), jnp.float32)],
        [],
        2 * tokens * width * width,
    )
    (input_grad,) = over_tokens(
        functools.partial(leave_kernel, stripe, cores),
        "leave",
        tokens,
        [tile(x), whole(first_gain)]
        + [columns(query_key_value_weight, 1, width), whole(value_weight)]
        + [tile(part) for part in (grad_middle, from_queries, *owned_keys, *owned_values)],
        [low],
        [],
        4 * tokens * width * width,
    )
    input_grad, normed = lax.optimization_barrier((input_grad, normed))
    down_sum, up_sum = over_tokens(
        functools.partial(adapt_kernel, cores),
        "adapt",
        tokens,
        [whole(down_packed), whole(up_packed)]
        + [tile(part) for part in (normed, pulled[0], *owned_values)],
        [],
        sums,
        1024 * tokens * width,
    )
    layer_out, down_sum = lax.optimization_barrier((spread_stripes(layer_out), down_sum))
    up_parts = [
        adapter_scale * up_sum[j * rank : (j + 1) * rank, j * width : (j + 1) * width]
        for j in range(2)
    ]
    adapter_sums = jnp.concatenate([*up_parts, down_sum], axis=0)
    adapter_sums, input_grad = sum_everywhere(adapter_sums, rows_back(input_grad))
    input_grad = spread_stripes(input_grad)
    adapter_sums = adapter_sums.reshape(2, 2, rank, width)
    up_map_gradient = adapter_sums[0]
    down_map_gradient = jnp.transpose(adapter_sums[1], (0, 2, 1))

    down_velocity_next = velocity_factor * down_velocity + down_map_gradient
    up_velocity_next = velocity_factor * up_velocity + up_map_gradient
    adapter_down_updated = adapter_down_maps - learning_step_size * (
        down_map_gradient + velocity_factor * down_velocity_next
    )
    adapter_up_updated = adapter_up_maps - learning_step_size * (
        up_map_gradient + velocity_factor * up_velocity_next
    )
    updated_down_mean = (
        mean_decay_factor * running_down_mean + (1.0 - mean_decay_factor) * adapter_down_updated
    )
    updated_up_mean = (
        mean_decay_factor * running_up_mean + (1.0 - mean_decay_factor) * adapter_up_updated
    )
    return (
        layer_out,
        input_grad,
        down_map_gradient,
        up_map_gradient,
        adapter_down_updated,
        adapter_up_updated,
        down_velocity_next,
        up_velocity_next,
        updated_down_mean,
        updated_up_mean,
        adapter_down_updated.astype(jnp.bfloat16),
        adapter_up_updated.astype(jnp.bfloat16),
    )


def solution(mesh):
    tokens = P("batch", "seq", None)
    codes = P("batch", "seq")
    return jax.shard_map(
        body,
        mesh=mesh,
        in_specs=(tokens, codes, codes) + (P(),) * 19 + (tokens,),
        out_specs=(tokens, tokens) + (P(),) * 10,
        check_vma=False,
    )
```

```python
import functools

import jax
import jax.numpy as jnp
from jax import lax
from jax.experimental import pallas as pl
from jax.experimental.pallas import tpu as pltpu
from jax.sharding import PartitionSpec as P

HEADS = 16
EXAMPLE_MAX = 1024
SEGMENT_SLOTS = 8
LANES = 128
QUERY_BLOCK = 256
TOKEN_BLOCK = 256
HIDDEN_BLOCK = 1024
AHEAD = 2
PER = 2
SCORES_AHEAD = 2
DELAY = 0
VMEM_BYTES = 63 * 1024 * 1024

norm_eps = 1e-05
adapter_scale = 8.0
learning_step_size = 3e-05
velocity_factor = 0.5
mean_decay_factor = 0.5
masked_score = -1e30
score_scale = 0.125


def matmul_rows(left_side, right_side):
    return lax.dot_general(
        left_side, right_side, (((1,), (0,)), ((), ())), preferred_element_type=jnp.float32
    )


def matmul_back(left_side, right_side):
    return lax.dot_general(
        left_side, right_side, (((1,), (1,)), ((), ())), preferred_element_type=jnp.float32
    )


def matmul_over(left_side, right_side):
    return lax.dot_general(
        left_side, right_side, (((0,), (0,)), ((), ())), preferred_element_type=jnp.float32
    )


def gather_kernel(cores, with_codes, core_ref, *refs):
    stripes, codes, out_ref = refs[:cores], refs[cores:-1], refs[-1]
    came_from = lax.rem(core_ref[0] - pl.program_id(0) + cores, cores)
    stripe, width = stripes[0].shape[1:]
    for by in range(cores):

        @pl.when(came_from == by)
        def _(by=by):
            for group in range(width // LANES):
                rows = pl.ds(group * stripe, stripe)
                out_ref[:, rows, :] = stripes[by][:, :, group * LANES : (group + 1) * LANES]
            if with_codes:
                out_ref[:, width // LANES * stripe :, :] = codes[by][...]


def gather_stripes(x, codes=None):
    cores = lax.axis_size("batch")
    core = lax.axis_index("batch")
    rows, tokens, width = x.shape
    stripe = tokens // cores
    parts, extra = [x], [] if codes is None else [codes]
    for by in range(1, cores):
        goes = lax.rem(core + by, cores)
        parts.append(from_core(lax.dynamic_slice_in_dim(x, goes * stripe, stripe, 1), by))
        extra += [] if codes is None else [from_core(codes, by)]
    deep = width // LANES * stripe + sum(c.shape[1] for c in extra[:1])
    whole = pl.BlockSpec((rows, stripe, width), lambda c, core: (0, 0, 0))
    return pl.pallas_call(
        functools.partial(gather_kernel, cores, bool(extra)),
        grid_spec=pltpu.PrefetchScalarGridSpec(
            num_scalar_prefetch=1,
            grid=(cores,),
            in_specs=[pl.BlockSpec((rows, stripe, width), lambda c, core: (0, core[0], 0))]
            + [whole] * (cores - 1)
            + [pl.BlockSpec(c.shape, lambda c, core: (0, 0, 0)) for c in extra],
            out_specs=pl.BlockSpec((rows, deep, LANES), lambda c, core: (c, 0, 0)),
        ),
        out_shape=jax.ShapeDtypeStruct((rows * cores, deep, LANES), x.dtype),
        compiler_params=pltpu.CompilerParams(vmem_limit_bytes=32 * 1024 * 1024),
        name="gather_stripes",
    )(core[None], *parts, *extra)


def spread_kernel(cores, core_ref, *refs):
    came_from = lax.rem(core_ref[0] - pl.program_id(0) + cores, cores)
    for by in range(cores):

        @pl.when(came_from == by)
        def _(by=by):
            refs[-1][...] = refs[by][...]


def spread_stripes(y):
    cores = lax.axis_size("batch")
    core = lax.axis_index("batch")
    rows, stripe, width = y.shape[0] // cores, *y.shape[1:]
    parts = [y]
    for by in range(1, cores):
        goes = lax.rem(core + by, cores)
        parts.append(from_core(lax.dynamic_slice_in_dim(y, goes * rows, rows, 0), by))
    block = (rows, stripe, width)
    return pl.pallas_call(
        functools.partial(spread_kernel, cores),
        grid_spec=pltpu.PrefetchScalarGridSpec(
            num_scalar_prefetch=1,
            grid=(cores,),
            in_specs=[pl.BlockSpec(block, lambda c, core: (core[0], 0, 0))]
            + [pl.BlockSpec(block, lambda c, core: (0, 0, 0))] * (cores - 1),
            out_specs=pl.BlockSpec(block, lambda c, core: (0, c, 0)),
        ),
        out_shape=jax.ShapeDtypeStruct((rows, stripe * cores, width), y.dtype),
        compiler_params=pltpu.CompilerParams(vmem_limit_bytes=32 * 1024 * 1024),
        name="spread_stripes",
    )(core[None], *parts)


def rows_home(y):
    return lax.all_to_all(y, "seq", 0, 0, tiled=True)


def rows_back(y):
    ring = lax.axis_size("seq")
    y = y.reshape(ring, y.shape[0] // ring, y.shape[1])
    return lax.all_to_all(y, "seq", 0, 0, tiled=True)


def tokens_of(ref, stripe, width):
    groups = []
    for group in range(width // LANES):
        rows = slice(group * stripe, (group + 1) * stripe)
        groups.append(jnp.concatenate([ref[c, rows, :] for c in range(ref.shape[0])], axis=0))
    return jnp.concatenate(groups, axis=1)


def from_core(x, by):
    cores = lax.axis_size("batch")
    return lax.ppermute(x, "batch", [(i, (i + by) % cores) for i in range(cores)])


def paired_sum(terms):
    while len(terms) > 1:
        terms = [terms[i] + terms[i + 1] for i in range(0, len(terms), 2)]
    return terms[0]


def sum_everywhere(x, before_last):
    ring, cores = lax.axis_size("seq"), lax.axis_size("batch")
    assert ring & (ring - 1) == 0 and cores & (cores - 1) == 0

    def exchanged(x, axis, size, by):
        return lax.ppermute(x, axis, [(i, i ^ by) for i in range(size)])

    step = 1
    while step < cores:
        x = x + exchanged(x, "batch", cores, step)
        step *= 2
    near = min(4, ring)
    share = x.shape[0] // near
    me = lax.rem(lax.axis_index("seq"), near)

    def shares_of(x, which):
        return lax.dynamic_slice_in_dim(x, which * share, share, 0)

    terms = [shares_of(x, me)]
    for by in range(1, near):
        terms.append(exchanged(shares_of(x, me ^ by), "seq", ring, by))
    mine = paired_sum(terms)
    step = near
    while step < ring:
        width = min(4, ring // step)
        mine = paired_sum(
            [mine] + [exchanged(mine, "seq", ring, by * step) for by in range(1, width)]
        )
        step *= width
    mine, before_last = lax.optimization_barrier((mine, before_last))
    held = [mine] + [exchanged(mine, "seq", ring, by) for by in range(1, near)]
    held = jnp.concatenate(held)
    return jnp.concatenate([shares_of(held, me ^ at) for at in range(near)]), before_last


def lane_masks(dtype):
    lane = lax.broadcasted_iota(jnp.int32, (1, LANES), 1)
    first = (lane < LANES // 2).astype(jnp.float32).astype(dtype)
    second = (lane >= LANES // 2).astype(jnp.float32).astype(dtype)
    return first, second


def slot_row():
    lane = lax.broadcasted_iota(jnp.int32, (1, LANES), 1)
    return (lax.rem(lane, LANES // 2) < SEGMENT_SLOTS).astype(jnp.float32).astype(jnp.bfloat16)


def block_of(ref, index):
    return ref[pl.ds(index * QUERY_BLOCK, QUERY_BLOCK), :]


def attend_block(cores, reach, skipped, *refs):
    query_ref = refs[0]
    key_refs = refs[1 : 1 + cores]
    value_refs = refs[1 + cores : 1 + 2 * cores]
    mark_ref, causal_ref, out_ref, log_ref, key_heads, turned_values = refs[1 + 2 * cores :]
    slots = slot_row()
    heads = lane_masks(jnp.bfloat16)
    half = LANES // 2
    blocks = query_ref.shape[0] // QUERY_BLOCK
    tile = cores * QUERY_BLOCK
    scale = jnp.asarray(score_scale, jnp.bfloat16)
    excluded = jnp.asarray(masked_score, jnp.bfloat16)
    for h in range(2):
        turned_values[h, half:, :] = jnp.ones_like(turned_values[h, half:, :])
    for j in range(blocks):
        for k in range(cores):
            key = block_of(key_refs[k], j)
            key_mark = slots - block_of(mark_ref, k * blocks + j)
            turned = block_of(value_refs[k], j).T
            at = pl.ds(j * tile + k * QUERY_BLOCK, QUERY_BLOCK)
            for h, own in enumerate(heads):
                key_heads[h, at, :] = key * own + key_mark * heads[1 - h]
                turned_values[h, :half, at] = turned[h * half : (h + 1) * half]

    def scores_of(n, h, start):
        query_head = block_of(query_ref, n) * scale * heads[h] + block_of(mark_ref, n) * excluded * heads[1 - h]
        scores = []
        for j in range(start, n + 1):
            score = matmul_back(key_heads[h, pl.ds(j * tile, tile), :], query_head)
            scores.append(score + causal_ref[...] if j == n else score)
        return scores

    def soften(scores):
        top = scores[0]
        for score in scores[1:]:
            top = jnp.maximum(top, score)
        top = jnp.max(top, axis=0, keepdims=True)
        return top, [jnp.exp(score - top).astype(jnp.bfloat16) for score in scores]

    def finish(n, h, start, top, weights, outs):
        rows = pl.ds(n * QUERY_BLOCK, QUERY_BLOCK)
        keys = pl.ds(start * tile, (n + 1 - start) * tile)
        out = matmul_rows(turned_values[h, :, keys], jnp.concatenate(weights))
        total = out[half : half + 1]
        log_ref[h : h + 1, rows] = top + jnp.log(total)
        outs.append(out[:half] / total)
        if h:
            out_ref[rows, :] = jnp.concatenate(outs[-2:]).T.astype(out_ref.dtype)

    def every(skipped):
        waiting, left, outs = [], [], []
        units = []
        for n in range(blocks):
            start = max(0, n - reach) + (skipped and n == blocks - 1)
            units += [(n, h, start) for h in range(2)]
        for unit in units + [None] * SCORES_AHEAD:
            if unit is not None:
                waiting.append((unit, scores_of(*unit)))
            if len(waiting) > SCORES_AHEAD or unit is None:
                done, scores = waiting.pop(0)
                left.append((*done, *soften(scores)))
                if len(left) > DELAY:
                    finish(*left.pop(0), outs)
        for one in left:
            finish(*one, outs)

    every(skipped)


def either_way(block, cores, reach, mark_at, *refs):
    refs, flag_ref = refs[:-1], refs[-1]
    mark_ref = refs[mark_at]
    blocks = refs[0].shape[0] // QUERY_BLOCK
    if blocks <= reach:
        block(cores, reach, False, *refs)
        return

    @pl.when(pl.program_id(0) == 0)
    def _():
        asking = mark_ref[pl.ds((blocks - 1) * QUERY_BLOCK, 16), :].astype(jnp.float32)[:1]
        shared = jnp.zeros_like(asking)
        for k in range(cores):
            last = (k * blocks + blocks - reach) * QUERY_BLOCK - 16
            shared = shared + asking * mark_ref[pl.ds(last, 16), :].astype(jnp.float32)[15:]
        flag_ref[0] = (jnp.sum(shared) > 0.0).astype(jnp.int32)

    pl.when(flag_ref[0] == 1)(functools.partial(block, cores, reach, False, *refs))
    pl.when(flag_ref[0] != 1)(functools.partial(block, cores, reach, True, *refs))


def spread(wide):
    high = wide.astype(jnp.bfloat16)
    return high, (wide - high.astype(jnp.float32)).astype(jnp.bfloat16)


def pull_block(cores, reach, skipped, *refs):
    query_ref, grad_ref, out_ref, log_ref = refs[:4]
    key_refs = refs[4 : 4 + cores]
    value_refs = refs[4 + cores : 4 + 2 * cores]
    mark_ref, causal_ref = refs[4 + 2 * cores : 6 + 2 * cores]
    outs = refs[6 + 2 * cores :]
    slots = slot_row()
    excluded = jnp.asarray(masked_score, jnp.bfloat16)
    grad_query_ref = outs[0]
    grad_key_refs = outs[1 : 1 + cores]
    grad_value_refs = outs[1 + cores : 1 + 2 * cores]
    (
        query_marked, query_heads, key_heads, all_values, grad_heads, turned_keys, turned_sums,
        dots,
    ) = outs[1 + 2 * cores :]
    heads = lane_masks(jnp.bfloat16)
    half = LANES // 2
    blocks = query_ref.shape[0] // QUERY_BLOCK
    tile = cores * QUERY_BLOCK
    scale = jnp.asarray(score_scale, jnp.bfloat16)
    lane = lax.broadcasted_iota(jnp.int32, (8, LANES), 1)
    row = lax.broadcasted_iota(jnp.int32, (8, LANES), 0)
    chooser = (lane // half == row).astype(jnp.float32).astype(jnp.bfloat16)
    for n in range(blocks):
        rows = pl.ds(n * QUERY_BLOCK, QUERY_BLOCK)
        query = query_ref[rows, :] * scale
        grad = grad_ref[rows, :]
        high, rest = spread(grad.astype(jnp.float32) * out_ref[rows, :].astype(jnp.float32))
        dots[:, rows] = matmul_back(chooser, high) + matmul_back(chooser, rest)
        for h, own in enumerate(heads):
            mine = query * own
            query_heads[h, rows, :] = mine
            query_marked[h, rows, :] = mine + mark_ref[rows, :] * excluded * heads[1 - h]
            grad_heads[h, rows, :] = grad * own
        for k in range(cores):
            key = block_of(key_refs[k], n)
            key_mark = slots - block_of(mark_ref, k * blocks + n)
            at = pl.ds(n * tile + k * QUERY_BLOCK, QUERY_BLOCK)
            turned_keys[:, at] = key.T
            all_values[at, :] = block_of(value_refs[k], n)
            for h, own in enumerate(heads):
                key_heads[h, at, :] = key * own + key_mark * heads[1 - h]
    turned_sums[...] = jnp.zeros_like(turned_sums)

    def products(j, n, h):
        keys = pl.ds(j * tile, tile)
        rows = pl.ds(n * QUERY_BLOCK, QUERY_BLOCK)
        score = matmul_back(key_heads[h, keys, :], query_marked[h, rows, :])
        change = matmul_back(all_values[keys, :], grad_heads[h, rows, :])
        return score, change

    def weigh(j, n, h, score, change):
        rows = pl.ds(n * QUERY_BLOCK, QUERY_BLOCK)
        if n == j:
            score = score + causal_ref[...]
        weight = jnp.exp(score - log_ref[h : h + 1, rows])
        change = (weight * (change - dots[h : h + 1, rows])).astype(jnp.bfloat16)
        return weight.astype(jnp.bfloat16), change

    def finishing(j, members):
        count = len(members) // 2
        keys = pl.ds(j * tile, tile)
        rows = pl.ds(j * QUERY_BLOCK, count * QUERY_BLOCK)

        def query_side(h):
            part = pl.ds(h * half, half)
            mine = jnp.concatenate([m[1] for m in members[h * count : (h + 1) * count]], axis=1)
            turned_sums[part, rows] += matmul_rows(turned_keys[part, keys], mine)

        def key_side(out_refs, which, right):
            left = jnp.concatenate([m[which] for m in members], axis=1)
            right = jnp.concatenate([right[0, rows, :], right[1, rows, :]])
            both = matmul_rows(left, right).astype(jnp.bfloat16)
            for k in range(cores):
                mine = both[k * QUERY_BLOCK : (k + 1) * QUERY_BLOCK]
                out_refs[k][pl.ds(j * QUERY_BLOCK, QUERY_BLOCK), :] = mine

        return [
            functools.partial(key_side, grad_value_refs, 0, grad_heads),
            functools.partial(query_side, 0),
            functools.partial(key_side, grad_key_refs, 1, query_heads),
            functools.partial(query_side, 1),
        ]

    def every(skipped):
        units = []
        for j in range(blocks):
            last = min(blocks - 1, j + reach)
            if skipped and j + reach == blocks - 1:
                last -= 1
            units += [(j, n, h, n == last and h) for h in range(2) for n in range(j, last + 1)]
        waiting, members, left = [], [], []
        for unit in units + [None] * AHEAD:
            if unit is not None:
                waiting.append((unit, products(*unit[:3])))
            if len(waiting) > AHEAD or unit is None:
                (j, n, h, closing), pair = waiting.pop(0)
                members.append(weigh(j, n, h, *pair))
                for task in left[:PER]:
                    task()
                left = left[PER:]
                if closing:
                    left += finishing(j, members)
                    members = []
        for task in left:
            task()

    every(skipped)
    grad_query_ref[...] = (turned_sums[...] * score_scale).T.astype(jnp.bfloat16)


def standardized(values):
    average = jnp.mean(values, axis=-1, keepdims=True)
    centred = values - average
    spread_inverse = lax.rsqrt(jnp.mean(centred * centred, axis=-1, keepdims=True) + norm_eps)
    return centred * spread_inverse, spread_inverse


def norm_pull(grad, shaped, spread_inverse):
    mean_grad = jnp.mean(grad, axis=-1, keepdims=True)
    mean_product = jnp.mean(grad * shaped, axis=-1, keepdims=True)
    return spread_inverse * (grad - mean_grad - shaped * mean_product)


def enter_kernel(
    stripe, x_ref, gain_ref, shift_ref, bias_ref, key_weight_ref, value_weight_ref,
    key_ref, value_ref, normed_ref,
):
    shaped, _ = standardized(tokens_of(x_ref, stripe, key_ref.shape[1]).astype(jnp.float32))
    normed = (shaped * gain_ref[...] + shift_ref[...]).astype(jnp.bfloat16)
    normed_ref[...] = normed
    key_ref[...] = matmul_rows(normed, key_weight_ref[...]).astype(jnp.bfloat16)
    value = matmul_rows(normed, value_weight_ref[...])
    value_ref[...] = (value + bias_ref[...]).astype(jnp.bfloat16)


def ask_kernel(normed_ref, bias_ref, weight_ref, query_ref):
    query = matmul_rows(normed_ref[...], weight_ref[...])
    query_ref[...] = (query + bias_ref[...]).astype(jnp.bfloat16)


root_two_over_pi = 0.7978845608028654
cubic = 0.044715


def middle_kernel(
    stripe, x_ref, attended_ref, cotangent_ref,
    out_bias_ref, gain_ref, shift_ref, expand_bias_ref, contract_bias_ref,
    out_weight_from, expand_from, contract_from,
    result_ref, grad_middle_ref, grad_attended_ref,
    out_weight_ref, expand_ref, contract_ref, arrivals,
):
    width, hidden = expand_ref.shape
    parts = [slice(at, at + HIDDEN_BLOCK) for at in range(0, hidden, HIDDEN_BLOCK)]
    copies = [pltpu.make_async_copy(out_weight_from, out_weight_ref, arrivals.at[0])]
    for i, part in enumerate(parts):
        for which, source, to in (
            (1, expand_from.at[:, part], expand_ref.at[:, part]),
            (2, contract_from.at[part, :], contract_ref.at[part, :]),
        ):
            copies.append(pltpu.make_async_copy(source, to, arrivals.at[2 * i + which]))

    def block(first):
        if first:
            for copy in copies:
                copy.start()
            copies[0].wait()
        middle = (
            tokens_of(x_ref, stripe, width).astype(jnp.float32)
            + matmul_rows(attended_ref[...], out_weight_ref[...])
            + out_bias_ref[...]
        )
        shaped, spread_inverse = standardized(middle)
        normed = (shaped * gain_ref[...] + shift_ref[...]).astype(jnp.bfloat16)
        grad_low = tokens_of(cotangent_ref, stripe, width)
        grad_out = grad_low.astype(jnp.float32)
        result = middle + contract_bias_ref[...]
        grad_normed = jnp.zeros_like(middle)
        for i, part in enumerate(parts):
            if first:
                copies[2 * i + 1].wait()
                copies[2 * i + 2].wait()
            pre = matmul_rows(normed, expand_ref[:, part]) + expand_bias_ref[:, part]
            grad_act = matmul_back(grad_low, contract_ref[part, :])
            square = pre * pre
            bent = jnp.tanh(root_two_over_pi * pre * (1.0 + cubic * square))
            upper = 0.5 + 0.5 * bent
            act = (pre * upper).astype(jnp.bfloat16)
            slope = upper + (0.5 * root_two_over_pi) * pre * (1.0 - bent * bent) * (
                1.0 + (3.0 * cubic) * square
            )
            grad_pre = (grad_act * slope).astype(jnp.bfloat16)
            result = result + matmul_rows(act, contract_ref[part, :])
            grad_normed = grad_normed + matmul_back(grad_pre, expand_ref[:, part])
        result_ref[...] = result.astype(jnp.bfloat16)
        grad_middle = grad_out + norm_pull(grad_normed * gain_ref[...], shaped, spread_inverse)
        grad_middle_low = grad_middle.astype(jnp.bfloat16)
        grad_middle_ref[...] = grad_middle_low
        grad_attended = matmul_back(grad_middle_low, out_weight_ref[...])
        grad_attended_ref[...] = grad_attended.astype(jnp.bfloat16)

    pl.when(pl.program_id(0) == 0)(functools.partial(block, True))
    pl.when(pl.program_id(0) != 0)(functools.partial(block, False))


def total(parts):
    out = parts[0][...].astype(jnp.float32)
    for part in parts[1:]:
        out = out + part[...].astype(jnp.float32)
    return out.astype(jnp.bfloat16)


def adapt_kernel(cores, down_ref, up_ref, normed_ref, grad_query_ref, *refs):
    down_sum_ref, up_sum_ref = refs[cores:]
    slots = down_sum_ref.shape[0]

    @pl.when(pl.program_id(0) == 0)
    def _():
        down_sum_ref[...] = jnp.zeros_like(down_sum_ref)
        up_sum_ref[...] = jnp.zeros_like(up_sum_ref)

    width = grad_query_ref.shape[1]
    normed = normed_ref[...]
    grad_query = grad_query_ref[...]
    grad_value = total(refs[:cores])
    lora = matmul_rows(normed, down_ref[...]).astype(jnp.bfloat16)
    grad_lora = matmul_back(grad_query, up_ref[:, :width]) + matmul_back(
        grad_value, up_ref[:, width:]
    )
    down_sum_ref[...] += matmul_over(grad_lora.astype(jnp.bfloat16), normed)[:slots]
    up_sum_ref[:, :width] += matmul_over(lora, grad_query)[:slots]
    up_sum_ref[:, width:] += matmul_over(lora, grad_value)[:slots]


def return_kernel(grad_query_ref, query_weight_ref, grad_normed_ref):
    grad_normed_ref[...] = matmul_back(grad_query_ref[...], query_weight_ref[...])


def leave_kernel(
    stripe, cores, x_ref, gain_ref, key_weight_ref, value_weight_ref,
    grad_middle_ref, from_queries_ref, *refs,
):
    key_refs, value_refs, grad_ref = refs[:cores], refs[cores : 2 * cores], refs[-1]
    width = grad_middle_ref.shape[1]
    shaped, spread_inverse = standardized(tokens_of(x_ref, stripe, width).astype(jnp.float32))
    grad_normed = (
        from_queries_ref[...]
        + matmul_back(total(key_refs), key_weight_ref[...])
        + matmul_back(total(value_refs), value_weight_ref[...])
    )
    grad = norm_pull(grad_normed * gain_ref[...], shaped, spread_inverse)
    grad_ref[...] = (grad_middle_ref[...].astype(jnp.float32) + grad).astype(jnp.bfloat16)


def tile(x):
    def spec(tokens):
        share = x.shape[0] * min(TOKEN_BLOCK, tokens) // tokens
        return pl.BlockSpec((share, *x.shape[1:]), lambda i: (i,) + (0,) * (len(x.shape) - 1))

    return x, spec


def whole(x):
    def spec(tokens):
        kept = pl.Buffered(1)
        return pl.BlockSpec(x.shape, lambda i: (0,) * len(x.shape), pipeline_mode=kept)

    return x, spec


def columns(x, which, width):
    def spec(tokens):
        kept = pl.Buffered(1)
        return pl.BlockSpec((x.shape[0], width), lambda i: (0, which), pipeline_mode=kept)

    return x, spec


def in_place(x):
    return x, lambda tokens: pl.BlockSpec(memory_space=pl.ANY)


def over_tokens(kernel, name, tokens, operands, outs, sums, flops, scratch=(), room=None):
    moved = sum(x.size * x.dtype.itemsize for x in [*(x for x, _ in operands), *outs, *sums])
    return pl.pallas_call(
        kernel,
        grid=(tokens // min(TOKEN_BLOCK, tokens),),
        in_specs=[spec(tokens) for _, spec in operands],
        out_specs=[tile(x)[1](tokens) for x in outs]
        + [pl.BlockSpec(x.shape, lambda i: (0, 0)) for x in sums],
        out_shape=[*outs, *sums],
        scratch_shapes=list(scratch),
        compiler_params=pltpu.CompilerParams(
            dimension_semantics=("arbitrary",), vmem_limit_bytes=room or VMEM_BYTES
        ),
        cost_estimate=pl.CostEstimate(flops=flops, bytes_accessed=moved, transcendentals=0),
        name=name,
    )(*(x for x, _ in operands))


def attention_calls(tokens, width, cores, reach):
    pair = pl.BlockSpec((tokens, LANES), lambda p: (0, p))
    marks = pl.BlockSpec((cores * tokens, LANES), lambda p: (0, 0))
    causal = pl.BlockSpec((cores * QUERY_BLOCK, QUERY_BLOCK), lambda p: (0, 0))
    logs = pl.BlockSpec((8, tokens), lambda p: (p, 0))
    grid = (width // LANES,)
    blocks = tokens // QUERY_BLOCK
    pairs = sum(min(n, reach) + 1 for n in range(blocks)) * cores * QUERY_BLOCK**2 * HEADS
    head_width = width // HEADS
    low = jax.ShapeDtypeStruct((tokens, width), jnp.bfloat16)
    log_rows = jax.ShapeDtypeStruct((8 * grid[0], tokens), jnp.float32)
    params = pltpu.CompilerParams(
        dimension_semantics=("arbitrary",), vmem_limit_bytes=VMEM_BYTES
    )
    low_scratch = functools.partial(pltpu.VMEM, dtype=jnp.bfloat16)
    forward = pl.pallas_call(
        functools.partial(either_way, attend_block, cores, reach, 1 + 2 * cores),
        grid_spec=pl.GridSpec(
            grid=grid,
            in_specs=[pair] * (1 + 2 * cores) + [marks, causal],
            out_specs=[pair, logs],
            scratch_shapes=[
                low_scratch((2, cores * tokens, LANES)),
                low_scratch((2, LANES // 2 + 16, cores * tokens)),
                pltpu.SMEM((1,), jnp.int32),
            ],
        ),
        out_shape=[low, log_rows],
        compiler_params=params,
        cost_estimate=pl.CostEstimate(
            flops=4 * pairs * head_width,
            bytes_accessed=2 * tokens * width * (2 + 2 * cores),
            transcendentals=pairs,
        ),
        name="attend",
    )
    backward = pl.pallas_call(
        functools.partial(either_way, pull_block, cores, reach, 4 + 2 * cores),
        grid_spec=pl.GridSpec(
            grid=grid,
            in_specs=[pair, pair, pair, logs] + [pair] * (2 * cores) + [marks, causal],
            out_specs=[pair] * (1 + 2 * cores),
            scratch_shapes=[
                low_scratch((2, tokens, LANES)),
                low_scratch((2, tokens, LANES)),
                low_scratch((2, cores * tokens, LANES)),
                low_scratch((cores * tokens, LANES)),
                low_scratch((2, tokens, LANES)),
                low_scratch((LANES, cores * tokens)),
                pltpu.VMEM((LANES, tokens), jnp.float32),
                pltpu.VMEM((8, tokens), jnp.float32),
                pltpu.SMEM((1,), jnp.int32),
            ],
        ),
        out_shape=[low] * (1 + 2 * cores),
        compiler_params=params,
        cost_estimate=pl.CostEstimate(
            flops=10 * pairs * head_width,
            bytes_accessed=2 * tokens * width * (4 + 4 * cores),
            transcendentals=pairs,
        ),
        name="pull",
    )
    return forward, backward


def body(
    inputs,
    segments,
    groups,
    group_loss_weight,
    attention_norm_gain,
    attention_norm_bias,
    query_key_value_weight,
    query_value_bias,
    attention_out_weight,
    attention_out_bias,
    feedforward_norm_gain,
    feedforward_norm_bias,
    expand_weight,
    expand_bias,
    contract_weight,
    contract_bias,
    adapter_down_maps,
    adapter_up_maps,
    down_velocity,
    up_velocity,
    running_down_mean,
    running_up_mean,
    cotangent,
):
    rows_here, tokens_here, width = inputs.shape
    cores = lax.axis_size("batch")
    ring = lax.axis_size("seq")
    assert rows_here * cores == ring
    stripe = tokens_here // cores
    tokens = ring * stripe
    span = QUERY_BLOCK * cores
    reach = -(-(EXAMPLE_MAX - 1) // span)
    rank = adapter_down_maps.shape[-1]
    core = lax.axis_index("batch")
    attend, pull = attention_calls(tokens, width, cores, reach)

    assert tokens_here == LANES
    marks = jnp.broadcast_to(segments[:, None, :], (rows_here, 8, tokens_here))
    x = rows_home(gather_stripes(inputs, marks.astype(jnp.bfloat16)))
    chooser = groups[..., None] == jnp.arange(group_loss_weight.shape[0], dtype=jnp.int32)
    token_weight = jnp.sum(jnp.where(chooser, group_loss_weight, 0.0), axis=-1, keepdims=True)
    weighted = (cotangent.astype(jnp.float32) * token_weight).astype(jnp.bfloat16)
    stripes = gather_stripes(weighted)
    place = jnp.arange(QUERY_BLOCK, dtype=jnp.int32)
    place = tokens_here * (place // stripe) + place % stripe
    after = []
    for by in range(cores):
        key_place = place + stripe * lax.rem(core - by + cores, cores)
        after.append(key_place[:, None] > (place + stripe * core)[None, :])
    causal = jnp.where(jnp.concatenate(after), masked_score, 0.0).astype(jnp.float32)

    def row_of(vector):
        return vector.astype(jnp.float32).reshape(1, -1)

    first_gain, first_shift = row_of(attention_norm_gain), row_of(attention_norm_bias)
    second_gain, second_shift = row_of(feedforward_norm_gain), row_of(feedforward_norm_bias)
    pad = LANES - 2 * rank
    down_packed = jnp.concatenate([adapter_down_maps[0], adapter_down_maps[1]], axis=1)
    down_packed = jnp.pad(down_packed, ((0, 0), (0, pad))).astype(jnp.bfloat16)
    up_packed = jnp.concatenate(
        [
            jnp.pad(adapter_up_maps[0], ((0, rank + pad), (0, 0))),
            jnp.pad(adapter_up_maps[1], ((rank, pad), (0, 0))),
        ],
        axis=1,
    )
    up_packed = (adapter_scale * up_packed).astype(jnp.bfloat16)

    def folded(which, j):
        added = matmul_rows(
            adapter_down_maps[j].astype(jnp.bfloat16), adapter_up_maps[j].astype(jnp.bfloat16)
        )
        frozen = query_key_value_weight[:, which * width : (which + 1) * width]
        return (frozen.astype(jnp.float32) + adapter_scale * added).astype(jnp.bfloat16)

    query_weight, value_weight = folded(0, 0), folded(2, 1)
    value_bias = query_value_bias.astype(jnp.float32)
    out_bias, up_bias, down_bias = map(row_of, (attention_out_bias, expand_bias, contract_bias))
    (
        x, stripes, causal, first_gain, first_shift, second_gain, second_shift,
        value_bias, out_bias, up_bias, down_bias, down_packed, up_packed, query_weight,
        value_weight,
    ) = lax.optimization_barrier(
        (
            x, stripes, causal, first_gain, first_shift, second_gain, second_shift,
            value_bias, out_bias, up_bias, down_bias, down_packed, up_packed, query_weight,
            value_weight,
        )
    )
    cotangent_home = rows_home(stripes)
    parts = x[:, width // LANES * stripe, :].reshape(ring, cores, stripe)
    turns = [lax.rem(core - by + cores, cores) for by in range(cores)]
    parts = [lax.dynamic_index_in_dim(parts, turn, 1, keepdims=False) for turn in turns]
    slot = (jnp.arange(LANES, dtype=jnp.int32) % (LANES // 2)).astype(jnp.bfloat16)
    marks = jnp.concatenate(parts).reshape(cores * tokens, 1) == slot[None, :]
    marks = marks.astype(jnp.bfloat16)

    low = jax.ShapeDtypeStruct((tokens, width), jnp.bfloat16)

    keys, values, normed = over_tokens(
        functools.partial(enter_kernel, stripe),
        "enter",
        tokens,
        [tile(x), whole(first_gain), whole(first_shift), whole(value_bias[1:])]
        + [columns(query_key_value_weight, 1, width), whole(value_weight)],
        [low, low, low],
        [],
        4 * tokens * width * width,
    )
    all_keys = [keys] + [from_core(keys, by) for by in range(1, cores)]
    all_values = [values] + [from_core(values, by) for by in range(1, cores)]
    (queries,) = over_tokens(
        ask_kernel,
        "ask",
        tokens,
        [tile(normed), whole(value_bias[:1]), whole(query_weight)],
        [low],
        [],
        2 * tokens * width * width,
    )
    attended, log_total = attend(queries, *all_keys, *all_values, marks, causal)

    hidden = expand_weight.shape[1]
    layer_result, grad_middle, grad_attended = over_tokens(
        functools.partial(middle_kernel, stripe),
        "middle",
        tokens,
        [tile(x), tile(attended), tile(cotangent_home)]
        + [whole(v) for v in (out_bias, second_gain, second_shift, up_bias, down_bias)]
        + [in_place(w) for w in (attention_out_weight, expand_weight, contract_weight)],
        [low, low, low],
        [],
        4 * tokens * width * (width + 2 * hidden),
        [pltpu.VMEM(w.shape, w.dtype) for w in (attention_out_weight, expand_weight, contract_weight)]
        + [pltpu.SemaphoreType.DMA((1 + 2 * (hidden // HIDDEN_BLOCK),))],
    )
    layer_out = rows_back(layer_result)

    pulled = pull(
        queries,
        grad_attended,
        attended,
        log_total,
        *all_keys,
        *all_values,
        marks,
        causal,
    )

    layer_out, pulled = lax.optimization_barrier((layer_out, pulled))

    def owned(parts):
        return [parts[0]] + [from_core(parts[by], -by) for by in range(1, cores)]

    sums = [
        jax.ShapeDtypeStruct((2 * rank, width), jnp.float32),
        jax.ShapeDtypeStruct((2 * rank, 2 * width), jnp.float32),
    ]
    owned_values = owned(pulled[1 + cores :])
    owned_keys = owned(pulled[1 : 1 + cores])
    (from_queries,) = over_tokens(
        return_kernel,
        "return",
        tokens,
        [tile(pulled[0]), whole(query_weight)],
        [jax.ShapeDtypeStruct((tokens, width), jnp.float32)],
        [],
        2 * tokens * width * width,
    )
    (input_grad,) = over_tokens(
        functools.partial(leave_kernel, stripe, cores),
        "leave",
        tokens,
        [tile(x), whole(first_gain)]
        + [columns(query_key_value_weight, 1, width), whole(value_weight)]
        + [tile(part) for part in (grad_middle, from_queries, *owned_keys, *owned_values)],
        [low],
        [],
        4 * tokens * width * width,
    )
    input_grad, normed = lax.optimization_barrier((input_grad, normed))
    down_sum, up_sum = over_tokens(
        functools.partial(adapt_kernel, cores),
        "adapt",
        tokens,
        [whole(down_packed), whole(up_packed)]
        + [tile(part) for part in (normed, pulled[0], *owned_values)],
        [],
        sums,
        1024 * tokens * width,
        room=32 * 1024 * 1024,
    )
    layer_out, down_sum = lax.optimization_barrier((spread_stripes(layer_out), down_sum))
    up_parts = [
        adapter_scale * up_sum[j * rank : (j + 1) * rank, j * width : (j + 1) * width]
        for j in range(2)
    ]
    adapter_sums = jnp.concatenate([*up_parts, down_sum], axis=0)
    adapter_sums, input_grad = sum_everywhere(adapter_sums, rows_back(input_grad))
    input_grad = spread_stripes(input_grad)
    adapter_sums = adapter_sums.reshape(2, 2, rank, width)
    up_map_gradient = adapter_sums[0]
    down_map_gradient = jnp.transpose(adapter_sums[1], (0, 2, 1))

    down_velocity_next = velocity_factor * down_velocity + down_map_gradient
    up_velocity_next = velocity_factor * up_velocity + up_map_gradient
    adapter_down_updated = adapter_down_maps - learning_step_size * (
        down_map_gradient + velocity_factor * down_velocity_next
    )
    adapter_up_updated = adapter_up_maps - learning_step_size * (
        up_map_gradient + velocity_factor * up_velocity_next
    )
    updated_down_mean = (
        mean_decay_factor * running_down_mean + (1.0 - mean_decay_factor) * adapter_down_updated
    )
    updated_up_mean = (
        mean_decay_factor * running_up_mean + (1.0 - mean_decay_factor) * adapter_up_updated
    )
    return (
        layer_out,
        input_grad,
        down_map_gradient,
        up_map_gradient,
        adapter_down_updated,
        adapter_up_updated,
        down_velocity_next,
        up_velocity_next,
        updated_down_mean,
        updated_up_mean,
        adapter_down_updated.astype(jnp.bfloat16),
        adapter_up_updated.astype(jnp.bfloat16),
    )


def solution(mesh):
    tokens = P("batch", "seq", None)
    codes = P("batch", "seq")
    return jax.shard_map(
        body,
        mesh=mesh,
        in_specs=(tokens, codes, codes) + (P(),) * 19 + (tokens,),
        out_specs=(tokens, tokens) + (P(),) * 10,
        check_vma=False,
    )
```

```python
import functools

import jax
import jax.numpy as jnp
from jax import lax
from jax.experimental import pallas as pl
from jax.experimental.pallas import tpu as pltpu
from jax.sharding import PartitionSpec as P

HEADS = 16
EXAMPLE_MAX = 1024
SEGMENT_SLOTS = 8
LANES = 128
QUERY_BLOCK = 256
TOKEN_BLOCK = 256
HIDDEN_BLOCK = 1024
AHEAD = 2
PER = 3
SCORES_AHEAD = 2
DELAY = 0
VMEM_BYTES = 63 * 1024 * 1024

norm_eps = 1e-05
adapter_scale = 8.0
learning_step_size = 3e-05
velocity_factor = 0.5
mean_decay_factor = 0.5
masked_score = -1e30
score_scale = 0.125


def matmul_rows(left_side, right_side):
    return lax.dot_general(
        left_side, right_side, (((1,), (0,)), ((), ())), preferred_element_type=jnp.float32
    )


def matmul_back(left_side, right_side):
    return lax.dot_general(
        left_side, right_side, (((1,), (1,)), ((), ())), preferred_element_type=jnp.float32
    )


def matmul_over(left_side, right_side):
    return lax.dot_general(
        left_side, right_side, (((0,), (0,)), ((), ())), preferred_element_type=jnp.float32
    )


def gather_kernel(cores, with_codes, core_ref, *refs):
    stripes, codes, out_ref = refs[:cores], refs[cores:-1], refs[-1]
    came_from = lax.rem(core_ref[0] - pl.program_id(0) + cores, cores)
    stripe, width = stripes[0].shape[1:]
    for by in range(cores):

        @pl.when(came_from == by)
        def _(by=by):
            for group in range(width // LANES):
                rows = pl.ds(group * stripe, stripe)
                out_ref[:, rows, :] = stripes[by][:, :, group * LANES : (group + 1) * LANES]
            if with_codes:
                out_ref[:, width // LANES * stripe :, :] = codes[by][...]


def gather_stripes(x, codes=None):
    cores = lax.axis_size("batch")
    core = lax.axis_index("batch")
    rows, tokens, width = x.shape
    stripe = tokens // cores
    parts, extra = [x], [] if codes is None else [codes]
    for by in range(1, cores):
        goes = lax.rem(core + by, cores)
        parts.append(from_core(lax.dynamic_slice_in_dim(x, goes * stripe, stripe, 1), by))
        extra += [] if codes is None else [from_core(codes, by)]
    deep = width // LANES * stripe + sum(c.shape[1] for c in extra[:1])
    whole = pl.BlockSpec((rows, stripe, width), lambda c, core: (0, 0, 0))
    return pl.pallas_call(
        functools.partial(gather_kernel, cores, bool(extra)),
        grid_spec=pltpu.PrefetchScalarGridSpec(
            num_scalar_prefetch=1,
            grid=(cores,),
            in_specs=[pl.BlockSpec((rows, stripe, width), lambda c, core: (0, core[0], 0))]
            + [whole] * (cores - 1)
            + [pl.BlockSpec(c.shape, lambda c, core: (0, 0, 0)) for c in extra],
            out_specs=pl.BlockSpec((rows, deep, LANES), lambda c, core: (c, 0, 0)),
        ),
        out_shape=jax.ShapeDtypeStruct((rows * cores, deep, LANES), x.dtype),
        compiler_params=pltpu.CompilerParams(vmem_limit_bytes=32 * 1024 * 1024),
        name="gather_stripes",
    )(core[None], *parts, *extra)


def spread_kernel(cores, core_ref, *refs):
    came_from = lax.rem(core_ref[0] - pl.program_id(0) + cores, cores)
    for by in range(cores):

        @pl.when(came_from == by)
        def _(by=by):
            refs[-1][...] = refs[by][...]


def spread_stripes(y):
    cores = lax.axis_size("batch")
    core = lax.axis_index("batch")
    rows, stripe, width = y.shape[0] // cores, *y.shape[1:]
    parts = [y]
    for by in range(1, cores):
        goes = lax.rem(core + by, cores)
        parts.append(from_core(lax.dynamic_slice_in_dim(y, goes * rows, rows, 0), by))
    block = (rows, stripe, width)
    return pl.pallas_call(
        functools.partial(spread_kernel, cores),
        grid_spec=pltpu.PrefetchScalarGridSpec(
            num_scalar_prefetch=1,
            grid=(cores,),
            in_specs=[pl.BlockSpec(block, lambda c, core: (core[0], 0, 0))]
            + [pl.BlockSpec(block, lambda c, core: (0, 0, 0))] * (cores - 1),
            out_specs=pl.BlockSpec(block, lambda c, core: (0, c, 0)),
        ),
        out_shape=jax.ShapeDtypeStruct((rows, stripe * cores, width), y.dtype),
        compiler_params=pltpu.CompilerParams(vmem_limit_bytes=32 * 1024 * 1024),
        name="spread_stripes",
    )(core[None], *parts)


def rows_home(y):
    return lax.all_to_all(y, "seq", 0, 0, tiled=True)


def rows_back(y):
    ring = lax.axis_size("seq")
    y = y.reshape(ring, y.shape[0] // ring, y.shape[1])
    return lax.all_to_all(y, "seq", 0, 0, tiled=True)


def tokens_of(ref, stripe, width):
    groups = []
    for group in range(width // LANES):
        rows = slice(group * stripe, (group + 1) * stripe)
        groups.append(jnp.concatenate([ref[c, rows, :] for c in range(ref.shape[0])], axis=0))
    return jnp.concatenate(groups, axis=1)


def from_core(x, by):
    cores = lax.axis_size("batch")
    return lax.ppermute(x, "batch", [(i, (i + by) % cores) for i in range(cores)])


def paired_sum(terms):
    while len(terms) > 1:
        terms = [terms[i] + terms[i + 1] for i in range(0, len(terms), 2)]
    return terms[0]


def sum_everywhere(x, before_last):
    ring, cores = lax.axis_size("seq"), lax.axis_size("batch")
    assert ring & (ring - 1) == 0 and cores & (cores - 1) == 0

    def exchanged(x, axis, size, by):
        return lax.ppermute(x, axis, [(i, i ^ by) for i in range(size)])

    step = 1
    while step < cores:
        x = x + exchanged(x, "batch", cores, step)
        step *= 2
    near = min(4, ring)
    share = x.shape[0] // near
    me = lax.rem(lax.axis_index("seq"), near)

    def shares_of(x, which):
        return lax.dynamic_slice_in_dim(x, which * share, share, 0)

    terms = [shares_of(x, me)]
    for by in range(1, near):
        terms.append(exchanged(shares_of(x, me ^ by), "seq", ring, by))
    mine = paired_sum(terms)
    step = near
    while step < ring:
        width = min(4, ring // step)
        mine = paired_sum(
            [mine] + [exchanged(mine, "seq", ring, by * step) for by in range(1, width)]
        )
        step *= width
    mine, before_last = lax.optimization_barrier((mine, before_last))
    held = [mine] + [exchanged(mine, "seq", ring, by) for by in range(1, near)]
    held = jnp.concatenate(held)
    return jnp.concatenate([shares_of(held, me ^ at) for at in range(near)]), before_last


def lane_masks(dtype):
    lane = lax.broadcasted_iota(jnp.int32, (1, LANES), 1)
    first = (lane < LANES // 2).astype(jnp.float32).astype(dtype)
    second = (lane >= LANES // 2).astype(jnp.float32).astype(dtype)
    return first, second


def slot_row():
    lane = lax.broadcasted_iota(jnp.int32, (1, LANES), 1)
    return (lax.rem(lane, LANES // 2) < SEGMENT_SLOTS).astype(jnp.float32).astype(jnp.bfloat16)


def block_of(ref, index):
    return ref[pl.ds(index * QUERY_BLOCK, QUERY_BLOCK), :]


def attend_block(cores, reach, skipped, *refs):
    query_ref = refs[0]
    key_refs = refs[1 : 1 + cores]
    value_refs = refs[1 + cores : 1 + 2 * cores]
    mark_ref, causal_ref, out_ref, log_ref, key_heads, turned_values = refs[1 + 2 * cores :]
    slots = slot_row()
    heads = lane_masks(jnp.bfloat16)
    half = LANES // 2
    blocks = query_ref.shape[0] // QUERY_BLOCK
    tile = cores * QUERY_BLOCK
    scale = jnp.asarray(score_scale, jnp.bfloat16)
    excluded = jnp.asarray(masked_score, jnp.bfloat16)
    for h in range(2):
        turned_values[h, half:, :] = jnp.ones_like(turned_values[h, half:, :])
    for j in range(blocks):
        for k in range(cores):
            key = block_of(key_refs[k], j)
            key_mark = slots - block_of(mark_ref, k * blocks + j)
            turned = block_of(value_refs[k], j).T
            at = pl.ds(j * tile + k * QUERY_BLOCK, QUERY_BLOCK)
            for h, own in enumerate(heads):
                key_heads[h, at, :] = key * own + key_mark * heads[1 - h]
                turned_values[h, :half, at] = turned[h * half : (h + 1) * half]

    def scores_of(n, h, start):
        query_head = block_of(query_ref, n) * scale * heads[h] + block_of(mark_ref, n) * excluded * heads[1 - h]
        scores = []
        for j in range(start, n + 1):
            score = matmul_back(key_heads[h, pl.ds(j * tile, tile), :], query_head)
            scores.append(score + causal_ref[...] if j == n else score)
        return scores

    def soften(scores):
        top = scores[0]
        for score in scores[1:]:
            top = jnp.maximum(top, score)
        top = jnp.max(top, axis=0, keepdims=True)
        return top, [jnp.exp(score - top).astype(jnp.bfloat16) for score in scores]

    def finish(n, h, start, top, weights, outs):
        rows = pl.ds(n * QUERY_BLOCK, QUERY_BLOCK)
        keys = pl.ds(start * tile, (n + 1 - start) * tile)
        out = matmul_rows(turned_values[h, :, keys], jnp.concatenate(weights))
        total = out[half : half + 1]
        log_ref[h : h + 1, rows] = top + jnp.log(total)
        outs.append(out[:half] / total)
        if h:
            out_ref[rows, :] = jnp.concatenate(outs[-2:]).T.astype(out_ref.dtype)

    def every(skipped):
        waiting, left, outs = [], [], []
        units = []
        for n in range(blocks):
            start = max(0, n - reach) + (skipped and n == blocks - 1)
            units += [(n, h, start) for h in range(2)]
        for unit in units + [None] * SCORES_AHEAD:
            if unit is not None:
                waiting.append((unit, scores_of(*unit)))
            if len(waiting) > SCORES_AHEAD or unit is None:
                done, scores = waiting.pop(0)
                left.append((*done, *soften(scores)))
                if len(left) > DELAY:
                    finish(*left.pop(0), outs)
        for one in left:
            finish(*one, outs)

    every(skipped)


def either_way(block, cores, reach, mark_at, *refs):
    refs, flag_ref = refs[:-1], refs[-1]
    mark_ref = refs[mark_at]
    blocks = refs[0].shape[0] // QUERY_BLOCK
    if blocks <= reach:
        block(cores, reach, False, *refs)
        return

    @pl.when(pl.program_id(0) == 0)
    def _():
        asking = mark_ref[pl.ds((blocks - 1) * QUERY_BLOCK, 16), :].astype(jnp.float32)[:1]
        shared = jnp.zeros_like(asking)
        for k in range(cores):
            last = (k * blocks + blocks - reach) * QUERY_BLOCK - 16
            shared = shared + asking * mark_ref[pl.ds(last, 16), :].astype(jnp.float32)[15:]
        flag_ref[0] = (jnp.sum(shared) > 0.0).astype(jnp.int32)

    pl.when(flag_ref[0] == 1)(functools.partial(block, cores, reach, False, *refs))
    pl.when(flag_ref[0] != 1)(functools.partial(block, cores, reach, True, *refs))


def spread(wide):
    high = wide.astype(jnp.bfloat16)
    return high, (wide - high.astype(jnp.float32)).astype(jnp.bfloat16)


def pull_block(cores, reach, skipped, *refs):
    query_ref, grad_ref, out_ref, log_ref = refs[:4]
    key_refs = refs[4 : 4 + cores]
    value_refs = refs[4 + cores : 4 + 2 * cores]
    mark_ref, causal_ref = refs[4 + 2 * cores : 6 + 2 * cores]
    outs = refs[6 + 2 * cores :]
    slots = slot_row()
    excluded = jnp.asarray(masked_score, jnp.bfloat16)
    grad_query_ref = outs[0]
    grad_key_refs = outs[1 : 1 + cores]
    grad_value_refs = outs[1 + cores : 1 + 2 * cores]
    (
        query_marked, query_heads, key_heads, all_values, grad_heads, turned_keys, turned_sums,
        dots,
    ) = outs[1 + 2 * cores :]
    heads = lane_masks(jnp.bfloat16)
    half = LANES // 2
    blocks = query_ref.shape[0] // QUERY_BLOCK
    tile = cores * QUERY_BLOCK
    scale = jnp.asarray(score_scale, jnp.bfloat16)
    lane = lax.broadcasted_iota(jnp.int32, (8, LANES), 1)
    row = lax.broadcasted_iota(jnp.int32, (8, LANES), 0)
    chooser = (lane // half == row).astype(jnp.float32).astype(jnp.bfloat16)
    for n in range(blocks):
        rows = pl.ds(n * QUERY_BLOCK, QUERY_BLOCK)
        query = query_ref[rows, :] * scale
        grad = grad_ref[rows, :]
        high, rest = spread(grad.astype(jnp.float32) * out_ref[rows, :].astype(jnp.float32))
        dots[:, rows] = matmul_back(chooser, high) + matmul_back(chooser, rest)
        for h, own in enumerate(heads):
            mine = query * own
            query_heads[h, rows, :] = mine
            query_marked[h, rows, :] = mine + mark_ref[rows, :] * excluded * heads[1 - h]
            grad_heads[h, rows, :] = grad * own
        for k in range(cores):
            key = block_of(key_refs[k], n)
            key_mark = slots - block_of(mark_ref, k * blocks + n)
            at = pl.ds(n * tile + k * QUERY_BLOCK, QUERY_BLOCK)
            turned_keys[:, at] = key.T
            all_values[at, :] = block_of(value_refs[k], n)
            for h, own in enumerate(heads):
                key_heads[h, at, :] = key * own + key_mark * heads[1 - h]
    turned_sums[...] = jnp.zeros_like(turned_sums)

    def products(j, n, h):
        keys = pl.ds(j * tile, tile)
        rows = pl.ds(n * QUERY_BLOCK, QUERY_BLOCK)
        score = matmul_back(key_heads[h, keys, :], query_marked[h, rows, :])
        change = matmul_back(all_values[keys, :], grad_heads[h, rows, :])
        return score, change

    def weigh(j, n, h, score, change):
        rows = pl.ds(n * QUERY_BLOCK, QUERY_BLOCK)
        if n == j:
            score = score + causal_ref[...]
        weight = jnp.exp(score - log_ref[h : h + 1, rows])
        change = (weight * (change - dots[h : h + 1, rows])).astype(jnp.bfloat16)
        return weight.astype(jnp.bfloat16), change

    def finishing(j, members):
        count = len(members) // 2
        keys = pl.ds(j * tile, tile)
        rows = pl.ds(j * QUERY_BLOCK, count * QUERY_BLOCK)

        def query_side(h):
            part = pl.ds(h * half, half)
            mine = jnp.concatenate([m[1] for m in members[h * count : (h + 1) * count]], axis=1)
            turned_sums[part, rows] += matmul_rows(turned_keys[part, keys], mine)

        def key_side(out_refs, which, right):
            left = jnp.concatenate([m[which] for m in members], axis=1)
            right = jnp.concatenate([right[0, rows, :], right[1, rows, :]])
            both = matmul_rows(left, right).astype(jnp.bfloat16)
            for k in range(cores):
                mine = both[k * QUERY_BLOCK : (k + 1) * QUERY_BLOCK]
                out_refs[k][pl.ds(j * QUERY_BLOCK, QUERY_BLOCK), :] = mine

        return [
            functools.partial(key_side, grad_value_refs, 0, grad_heads),
            functools.partial(query_side, 0),
            functools.partial(key_side, grad_key_refs, 1, query_heads),
            functools.partial(query_side, 1),
        ]

    def every(skipped):
        units = []
        for j in range(blocks):
            last = min(blocks - 1, j + reach)
            if skipped and j + reach == blocks - 1:
                last -= 1
            units += [(j, n, h, n == last and h) for h in range(2) for n in range(j, last + 1)]
        waiting, members, left = [], [], []
        for unit in units + [None] * AHEAD:
            if unit is not None:
                waiting.append((unit, products(*unit[:3])))
            if len(waiting) > AHEAD or unit is None:
                (j, n, h, closing), pair = waiting.pop(0)
                members.append(weigh(j, n, h, *pair))
                for task in left[:PER]:
                    task()
                left = left[PER:]
                if closing:
                    left += finishing(j, members)
                    members = []
        for task in left:
            task()

    every(skipped)
    grad_query_ref[...] = (turned_sums[...] * score_scale).T.astype(jnp.bfloat16)


def standardized(values):
    average = jnp.mean(values, axis=-1, keepdims=True)
    centred = values - average
    spread_inverse = lax.rsqrt(jnp.mean(centred * centred, axis=-1, keepdims=True) + norm_eps)
    return centred * spread_inverse, spread_inverse


def norm_pull(grad, shaped, spread_inverse):
    mean_grad = jnp.mean(grad, axis=-1, keepdims=True)
    mean_product = jnp.mean(grad * shaped, axis=-1, keepdims=True)
    return spread_inverse * (grad - mean_grad - shaped * mean_product)


def enter_kernel(
    stripe, x_ref, gain_ref, shift_ref, bias_ref, key_weight_ref, value_weight_ref,
    key_ref, value_ref, normed_ref,
):
    shaped, _ = standardized(tokens_of(x_ref, stripe, key_ref.shape[1]).astype(jnp.float32))
    normed = (shaped * gain_ref[...] + shift_ref[...]).astype(jnp.bfloat16)
    normed_ref[...] = normed
    key_ref[...] = matmul_rows(normed, key_weight_ref[...]).astype(jnp.bfloat16)
    value = matmul_rows(normed, value_weight_ref[...])
    value_ref[...] = (value + bias_ref[...]).astype(jnp.bfloat16)


def ask_kernel(normed_ref, bias_ref, weight_ref, query_ref):
    query = matmul_rows(normed_ref[...], weight_ref[...])
    query_ref[...] = (query + bias_ref[...]).astype(jnp.bfloat16)


root_two_over_pi = 0.7978845608028654
cubic = 0.044715


def middle_kernel(
    stripe, x_ref, attended_ref, cotangent_ref,
    out_bias_ref, gain_ref, shift_ref, expand_bias_ref, contract_bias_ref,
    out_weight_from, expand_from, contract_from,
    result_ref, grad_middle_ref, grad_attended_ref,
    out_weight_ref, expand_ref, contract_ref, arrivals,
):
    width, hidden = expand_ref.shape
    parts = [slice(at, at + HIDDEN_BLOCK) for at in range(0, hidden, HIDDEN_BLOCK)]
    copies = [pltpu.make_async_copy(out_weight_from, out_weight_ref, arrivals.at[0])]
    for i, part in enumerate(parts):
        for which, source, to in (
            (1, expand_from.at[:, part], expand_ref.at[:, part]),
            (2, contract_from.at[part, :], contract_ref.at[part, :]),
        ):
            copies.append(pltpu.make_async_copy(source, to, arrivals.at[2 * i + which]))

    def block(first):
        if first:
            for copy in copies:
                copy.start()
            copies[0].wait()
        middle = (
            tokens_of(x_ref, stripe, width).astype(jnp.float32)
            + matmul_rows(attended_ref[...], out_weight_ref[...])
            + out_bias_ref[...]
        )
        shaped, spread_inverse = standardized(middle)
        normed = (shaped * gain_ref[...] + shift_ref[...]).astype(jnp.bfloat16)
        grad_low = tokens_of(cotangent_ref, stripe, width)
        grad_out = grad_low.astype(jnp.float32)
        result = middle + contract_bias_ref[...]
        grad_normed = jnp.zeros_like(middle)
        for i, part in enumerate(parts):
            if first:
                copies[2 * i + 1].wait()
                copies[2 * i + 2].wait()
            pre = matmul_rows(normed, expand_ref[:, part]) + expand_bias_ref[:, part]
            grad_act = matmul_back(grad_low, contract_ref[part, :])
            square = pre * pre
            bent = jnp.tanh(root_two_over_pi * pre * (1.0 + cubic * square))
            upper = 0.5 + 0.5 * bent
            act = (pre * upper).astype(jnp.bfloat16)
            slope = upper + (0.5 * root_two_over_pi) * pre * (1.0 - bent * bent) * (
                1.0 + (3.0 * cubic) * square
            )
            grad_pre = (grad_act * slope).astype(jnp.bfloat16)
            result = result + matmul_rows(act, contract_ref[part, :])
            grad_normed = grad_normed + matmul_back(grad_pre, expand_ref[:, part])
        result_ref[...] = result.astype(jnp.bfloat16)
        grad_middle = grad_out + norm_pull(grad_normed * gain_ref[...], shaped, spread_inverse)
        grad_middle_low = grad_middle.astype(jnp.bfloat16)
        grad_middle_ref[...] = grad_middle_low
        grad_attended = matmul_back(grad_middle_low, out_weight_ref[...])
        grad_attended_ref[...] = grad_attended.astype(jnp.bfloat16)

    pl.when(pl.program_id(0) == 0)(functools.partial(block, True))
    pl.when(pl.program_id(0) != 0)(functools.partial(block, False))


def total(parts):
    out = parts[0][...].astype(jnp.float32)
    for part in parts[1:]:
        out = out + part[...].astype(jnp.float32)
    return out.astype(jnp.bfloat16)


def adapt_kernel(cores, down_ref, up_ref, normed_ref, grad_query_ref, *refs):
    down_sum_ref, up_sum_ref = refs[cores:]
    slots = down_sum_ref.shape[0]

    @pl.when(pl.program_id(0) == 0)
    def _():
        down_sum_ref[...] = jnp.zeros_like(down_sum_ref)
        up_sum_ref[...] = jnp.zeros_like(up_sum_ref)

    width = grad_query_ref.shape[1]
    normed = normed_ref[...]
    grad_query = grad_query_ref[...]
    grad_value = total(refs[:cores])
    lora = matmul_rows(normed, down_ref[...]).astype(jnp.bfloat16)
    grad_lora = matmul_back(grad_query, up_ref[:, :width]) + matmul_back(
        grad_value, up_ref[:, width:]
    )
    down_sum_ref[...] += matmul_over(grad_lora.astype(jnp.bfloat16), normed)[:slots]
    up_sum_ref[:, :width] += matmul_over(lora, grad_query)[:slots]
    up_sum_ref[:, width:] += matmul_over(lora, grad_value)[:slots]


def return_kernel(grad_query_ref, query_weight_ref, grad_normed_ref):
    grad_normed_ref[...] = matmul_back(grad_query_ref[...], query_weight_ref[...])


def leave_kernel(
    stripe, cores, x_ref, gain_ref, key_weight_ref, value_weight_ref,
    grad_middle_ref, from_queries_ref, *refs,
):
    key_refs, value_refs, grad_ref = refs[:cores], refs[cores : 2 * cores], refs[-1]
    width = grad_middle_ref.shape[1]
    shaped, spread_inverse = standardized(tokens_of(x_ref, stripe, width).astype(jnp.float32))
    grad_normed = (
        from_queries_ref[...]
        + matmul_back(total(key_refs), key_weight_ref[...])
        + matmul_back(total(value_refs), value_weight_ref[...])
    )
    grad = norm_pull(grad_normed * gain_ref[...], shaped, spread_inverse)
    grad_ref[...] = (grad_middle_ref[...].astype(jnp.float32) + grad).astype(jnp.bfloat16)


def tile(x):
    def spec(tokens):
        share = x.shape[0] * min(TOKEN_BLOCK, tokens) // tokens
        return pl.BlockSpec((share, *x.shape[1:]), lambda i: (i,) + (0,) * (len(x.shape) - 1))

    return x, spec


def whole(x):
    def spec(tokens):
        kept = pl.Buffered(1)
        return pl.BlockSpec(x.shape, lambda i: (0,) * len(x.shape), pipeline_mode=kept)

    return x, spec


def columns(x, which, width):
    def spec(tokens):
        kept = pl.Buffered(1)
        return pl.BlockSpec((x.shape[0], width), lambda i: (0, which), pipeline_mode=kept)

    return x, spec


def in_place(x):
    return x, lambda tokens: pl.BlockSpec(memory_space=pl.ANY)


def over_tokens(kernel, name, tokens, operands, outs, sums, flops, scratch=(), room=None):
    moved = sum(x.size * x.dtype.itemsize for x in [*(x for x, _ in operands), *outs, *sums])
    return pl.pallas_call(
        kernel,
        grid=(tokens // min(TOKEN_BLOCK, tokens),),
        in_specs=[spec(tokens) for _, spec in operands],
        out_specs=[tile(x)[1](tokens) for x in outs]
        + [pl.BlockSpec(x.shape, lambda i: (0, 0)) for x in sums],
        out_shape=[*outs, *sums],
        scratch_shapes=list(scratch),
        compiler_params=pltpu.CompilerParams(
            dimension_semantics=("arbitrary",), vmem_limit_bytes=room or VMEM_BYTES
        ),
        cost_estimate=pl.CostEstimate(flops=flops, bytes_accessed=moved, transcendentals=0),
        name=name,
    )(*(x for x, _ in operands))


def attention_calls(tokens, width, cores, reach):
    pair = pl.BlockSpec((tokens, LANES), lambda p: (0, p))
    marks = pl.BlockSpec((cores * tokens, LANES), lambda p: (0, 0))
    causal = pl.BlockSpec((cores * QUERY_BLOCK, QUERY_BLOCK), lambda p: (0, 0))
    logs = pl.BlockSpec((8, tokens), lambda p: (p, 0))
    grid = (width // LANES,)
    blocks = tokens // QUERY_BLOCK
    pairs = sum(min(n, reach) + 1 for n in range(blocks)) * cores * QUERY_BLOCK**2 * HEADS
    head_width = width // HEADS
    low = jax.ShapeDtypeStruct((tokens, width), jnp.bfloat16)
    log_rows = jax.ShapeDtypeStruct((8 * grid[0], tokens), jnp.float32)
    params = pltpu.CompilerParams(
        dimension_semantics=("arbitrary",), vmem_limit_bytes=VMEM_BYTES
    )
    low_scratch = functools.partial(pltpu.VMEM, dtype=jnp.bfloat16)
    forward = pl.pallas_call(
        functools.partial(either_way, attend_block, cores, reach, 1 + 2 * cores),
        grid_spec=pl.GridSpec(
            grid=grid,
            in_specs=[pair] * (1 + 2 * cores) + [marks, causal],
            out_specs=[pair, logs],
            scratch_shapes=[
                low_scratch((2, cores * tokens, LANES)),
                low_scratch((2, LANES // 2 + 16, cores * tokens)),
                pltpu.SMEM((1,), jnp.int32),
            ],
        ),
        out_shape=[low, log_rows],
        compiler_params=params,
        cost_estimate=pl.CostEstimate(
            flops=4 * pairs * head_width,
            bytes_accessed=2 * tokens * width * (2 + 2 * cores),
            transcendentals=pairs,
        ),
        name="attend",
    )
    backward = pl.pallas_call(
        functools.partial(either_way, pull_block, cores, reach, 4 + 2 * cores),
        grid_spec=pl.GridSpec(
            grid=grid,
            in_specs=[pair, pair, pair, logs] + [pair] * (2 * cores) + [marks, causal],
            out_specs=[pair] * (1 + 2 * cores),
            scratch_shapes=[
                low_scratch((2, tokens, LANES)),
                low_scratch((2, tokens, LANES)),
                low_scratch((2, cores * tokens, LANES)),
                low_scratch((cores * tokens, LANES)),
                low_scratch((2, tokens, LANES)),
                low_scratch((LANES, cores * tokens)),
                pltpu.VMEM((LANES, tokens), jnp.float32),
                pltpu.VMEM((8, tokens), jnp.float32),
                pltpu.SMEM((1,), jnp.int32),
            ],
        ),
        out_shape=[low] * (1 + 2 * cores),
        compiler_params=params,
        cost_estimate=pl.CostEstimate(
            flops=10 * pairs * head_width,
            bytes_accessed=2 * tokens * width * (4 + 4 * cores),
            transcendentals=pairs,
        ),
        name="pull",
    )
    return forward, backward


def body(
    inputs,
    segments,
    groups,
    group_loss_weight,
    attention_norm_gain,
    attention_norm_bias,
    query_key_value_weight,
    query_value_bias,
    attention_out_weight,
    attention_out_bias,
    feedforward_norm_gain,
    feedforward_norm_bias,
    expand_weight,
    expand_bias,
    contract_weight,
    contract_bias,
    adapter_down_maps,
    adapter_up_maps,
    down_velocity,
    up_velocity,
    running_down_mean,
    running_up_mean,
    cotangent,
):
    rows_here, tokens_here, width = inputs.shape
    cores = lax.axis_size("batch")
    ring = lax.axis_size("seq")
    assert rows_here * cores == ring
    stripe = tokens_here // cores
    tokens = ring * stripe
    span = QUERY_BLOCK * cores
    reach = -(-(EXAMPLE_MAX - 1) // span)
    rank = adapter_down_maps.shape[-1]
    core = lax.axis_index("batch")
    attend, pull = attention_calls(tokens, width, cores, reach)

    assert tokens_here == LANES
    marks = jnp.broadcast_to(segments[:, None, :], (rows_here, 8, tokens_here))
    x = rows_home(gather_stripes(inputs, marks.astype(jnp.bfloat16)))
    chooser = groups[..., None] == jnp.arange(group_loss_weight.shape[0], dtype=jnp.int32)
    token_weight = jnp.sum(jnp.where(chooser, group_loss_weight, 0.0), axis=-1, keepdims=True)
    weighted = (cotangent.astype(jnp.float32) * token_weight).astype(jnp.bfloat16)
    stripes = gather_stripes(weighted)
    place = jnp.arange(QUERY_BLOCK, dtype=jnp.int32)
    place = tokens_here * (place // stripe) + place % stripe
    after = []
    for by in range(cores):
        key_place = place + stripe * lax.rem(core - by + cores, cores)
        after.append(key_place[:, None] > (place + stripe * core)[None, :])
    causal = jnp.where(jnp.concatenate(after), masked_score, 0.0).astype(jnp.float32)

    def row_of(vector):
        return vector.astype(jnp.float32).reshape(1, -1)

    first_gain, first_shift = row_of(attention_norm_gain), row_of(attention_norm_bias)
    second_gain, second_shift = row_of(feedforward_norm_gain), row_of(feedforward_norm_bias)
    pad = LANES - 2 * rank
    down_packed = jnp.concatenate([adapter_down_maps[0], adapter_down_maps[1]], axis=1)
    down_packed = jnp.pad(down_packed, ((0, 0), (0, pad))).astype(jnp.bfloat16)
    up_packed = jnp.concatenate(
        [
            jnp.pad(adapter_up_maps[0], ((0, rank + pad), (0, 0))),
            jnp.pad(adapter_up_maps[1], ((rank, pad), (0, 0))),
        ],
        axis=1,
    )
    up_packed = (adapter_scale * up_packed).astype(jnp.bfloat16)

    def folded(which, j):
        added = matmul_rows(
            adapter_down_maps[j].astype(jnp.bfloat16), adapter_up_maps[j].astype(jnp.bfloat16)
        )
        frozen = query_key_value_weight[:, which * width : (which + 1) * width]
        return (frozen.astype(jnp.float32) + adapter_scale * added).astype(jnp.bfloat16)

    query_weight, value_weight = folded(0, 0), folded(2, 1)
    value_bias = query_value_bias.astype(jnp.float32)
    out_bias, up_bias, down_bias = map(row_of, (attention_out_bias, expand_bias, contract_bias))
    (
        x, stripes, causal, first_gain, first_shift, second_gain, second_shift,
        value_bias, out_bias, up_bias, down_bias, down_packed, up_packed, query_weight,
        value_weight,
    ) = lax.optimization_barrier(
        (
            x, stripes, causal, first_gain, first_shift, second_gain, second_shift,
            value_bias, out_bias, up_bias, down_bias, down_packed, up_packed, query_weight,
            value_weight,
        )
    )
    cotangent_home = rows_home(stripes)
    parts = x[:, width // LANES * stripe, :].reshape(ring, cores, stripe)
    turns = [lax.rem(core - by + cores, cores) for by in range(cores)]
    parts = [lax.dynamic_index_in_dim(parts, turn, 1, keepdims=False) for turn in turns]
    slot = (jnp.arange(LANES, dtype=jnp.int32) % (LANES // 2)).astype(jnp.bfloat16)
    marks = jnp.concatenate(parts).reshape(cores * tokens, 1) == slot[None, :]
    marks = marks.astype(jnp.bfloat16)

    low = jax.ShapeDtypeStruct((tokens, width), jnp.bfloat16)

    keys, values, normed = over_tokens(
        functools.partial(enter_kernel, stripe),
        "enter",
        tokens,
        [tile(x), whole(first_gain), whole(first_shift), whole(value_bias[1:])]
        + [columns(query_key_value_weight, 1, width), whole(value_weight)],
        [low, low, low],
        [],
        4 * tokens * width * width,
    )
    all_keys = [keys] + [from_core(keys, by) for by in range(1, cores)]
    all_values = [values] + [from_core(values, by) for by in range(1, cores)]
    (queries,) = over_tokens(
        ask_kernel,
        "ask",
        tokens,
        [tile(normed), whole(value_bias[:1]), whole(query_weight)],
        [low],
        [],
        2 * tokens * width * width,
    )
    attended, log_total = attend(queries, *all_keys, *all_values, marks, causal)

    hidden = expand_weight.shape[1]
    layer_result, grad_middle, grad_attended = over_tokens(
        functools.partial(middle_kernel, stripe),
        "middle",
        tokens,
        [tile(x), tile(attended), tile(cotangent_home)]
        + [whole(v) for v in (out_bias, second_gain, second_shift, up_bias, down_bias)]
        + [in_place(w) for w in (attention_out_weight, expand_weight, contract_weight)],
        [low, low, low],
        [],
        4 * tokens * width * (width + 2 * hidden),
        [pltpu.VMEM(w.shape, w.dtype) for w in (attention_out_weight, expand_weight, contract_weight)]
        + [pltpu.SemaphoreType.DMA((1 + 2 * (hidden // HIDDEN_BLOCK),))],
    )
    layer_out = rows_back(layer_result)

    pulled = pull(
        queries,
        grad_attended,
        attended,
        log_total,
        *all_keys,
        *all_values,
        marks,
        causal,
    )

    layer_out, pulled = lax.optimization_barrier((layer_out, pulled))

    def owned(parts):
        return [parts[0]] + [from_core(parts[by], -by) for by in range(1, cores)]

    sums = [
        jax.ShapeDtypeStruct((2 * rank, width), jnp.float32),
        jax.ShapeDtypeStruct((2 * rank, 2 * width), jnp.float32),
    ]
    owned_values = owned(pulled[1 + cores :])
    owned_keys = owned(pulled[1 : 1 + cores])
    (from_queries,) = over_tokens(
        return_kernel,
        "return",
        tokens,
        [tile(pulled[0]), whole(query_weight)],
        [jax.ShapeDtypeStruct((tokens, width), jnp.float32)],
        [],
        2 * tokens * width * width,
    )
    (input_grad,) = over_tokens(
        functools.partial(leave_kernel, stripe, cores),
        "leave",
        tokens,
        [tile(x), whole(first_gain)]
        + [columns(query_key_value_weight, 1, width), whole(value_weight)]
        + [tile(part) for part in (grad_middle, from_queries, *owned_keys, *owned_values)],
        [low],
        [],
        4 * tokens * width * width,
    )
    input_grad, normed = lax.optimization_barrier((input_grad, normed))
    down_sum, up_sum = over_tokens(
        functools.partial(adapt_kernel, cores),
        "adapt",
        tokens,
        [whole(down_packed), whole(up_packed)]
        + [tile(part) for part in (normed, pulled[0], *owned_values)],
        [],
        sums,
        1024 * tokens * width,
        room=32 * 1024 * 1024,
    )
    layer_out, down_sum = lax.optimization_barrier((spread_stripes(layer_out), down_sum))
    up_parts = [
        adapter_scale * up_sum[j * rank : (j + 1) * rank, j * width : (j + 1) * width]
        for j in range(2)
    ]
    adapter_sums = jnp.concatenate([*up_parts, down_sum], axis=0)
    adapter_sums, input_grad = sum_everywhere(adapter_sums, rows_back(input_grad))
    input_grad = spread_stripes(input_grad)
    adapter_sums = adapter_sums.reshape(2, 2, rank, width)
    up_map_gradient = adapter_sums[0]
    down_map_gradient = jnp.transpose(adapter_sums[1], (0, 2, 1))

    down_velocity_next = velocity_factor * down_velocity + down_map_gradient
    up_velocity_next = velocity_factor * up_velocity + up_map_gradient
    adapter_down_updated = adapter_down_maps - learning_step_size * (
        down_map_gradient + velocity_factor * down_velocity_next
    )
    adapter_up_updated = adapter_up_maps - learning_step_size * (
        up_map_gradient + velocity_factor * up_velocity_next
    )
    updated_down_mean = (
        mean_decay_factor * running_down_mean + (1.0 - mean_decay_factor) * adapter_down_updated
    )
    updated_up_mean = (
        mean_decay_factor * running_up_mean + (1.0 - mean_decay_factor) * adapter_up_updated
    )
    return (
        layer_out,
        input_grad,
        down_map_gradient,
        up_map_gradient,
        adapter_down_updated,
        adapter_up_updated,
        down_velocity_next,
        up_velocity_next,
        updated_down_mean,
        updated_up_mean,
        adapter_down_updated.astype(jnp.bfloat16),
        adapter_up_updated.astype(jnp.bfloat16),
    )


def solution(mesh):
    tokens = P("batch", "seq", None)
    codes = P("batch", "seq")
    return jax.shard_map(
        body,
        mesh=mesh,
        in_specs=(tokens, codes, codes) + (P(),) * 19 + (tokens,),
        out_specs=(tokens, tokens) + (P(),) * 10,
        check_vma=False,
    )
```
